128 devices in a mesh: vox: 8 (over y, core), fas: 16 (over z, x).
Axes of the slice: x: 4, y: 4, z: 4, core: 2. Of those that a mesh axis runs over, the one named last changes fastest.
Arguments:
- signal: float32 [128, 6144], P('vox', 'fas'), may hold values from -6 to 6
- initial_weights: float32 [524288], P('fas'), may hold values from 0.1 to 2
- coefficients: bfloat16 [32768, 4096], P(('vox', 'fas')), may hold values from 0 to 0.0234375
- block_rows: int32 [32768], P(('vox', 'fas')), may hold values from 0 to 127, as said below
- block_cols: int32 [32768], P(('vox', 'fas')), may hold values from 0 to 8191, as said below
- block_atoms: int32 [32768, 64], P(('vox', 'fas')), may hold values from 0 to 359
- block_count: int32 [128], P(('vox', 'fas')), may hold values from 64 to 256, as said below
- dictionary: bfloat16 [360, 96], replicated, may hold values from -6 to 6
Outputs:
- weights: float32 [524288], P('fas')
- residual: float32 [128, 6144], P('vox', 'fas')
The draws below stay inside these ranges and needn't reach their ends.
Inputs may be any that keep to these rules, and one draw needn't show every extreme that they name: Block slots are stored device by device: the device with vox index i and fas index f holds slots (i * 16 + f) * 256 to (i * 16 + f + 1) * 256 - 1, and every block_rows value there lies in i * 16 to (i + 1) * 16 - 1. For the slots of the device with fas index f, every block_cols value lies in f * 512 to (f + 1) * 512 - 1. `block_count`: entry i * 16 + f is the number of live slots of the device with vox index i and fas index f, its first slots; some device has all 256 live.
All inputs are finite; a program needn't handle non-finite values.
Results may differ from the reference program's by a relative error of at most 0.0003.
Values sent between devices are 32-bit elements; how exact they have to be, the bound alone decides.
A program may use at most 128 MiB of HBM per device.

```python
import math
import jax
import jax.numpy as jnp
from jax import lax

BV = 64
BF = 64
DIRS = 96
ATOMS = 360
VB_DEV = 16
FB_DEV = 512
KDEV = 256
ITERS = 5
VBLOCKS = 128
FASC = 524288
BLOCKS = 32768
N_VOX = 8
N_FAS = 16


def draw_block_rows(key, part):
    slot_index = jnp.arange(KDEV * N_VOX * N_FAS, dtype=jnp.int32) // KDEV
    vox_index = slot_index // N_FAS
    offsets = jax.random.randint(key, (KDEV * N_VOX * N_FAS,), 0, VB_DEV, dtype=jnp.int32)
    return (vox_index * VB_DEV + offsets).astype(jnp.int32)


def draw_block_cols(key, part):
    slot_index = jnp.arange(KDEV * N_VOX * N_FAS, dtype=jnp.int32) // KDEV
    fas_index = slot_index % N_FAS
    offsets = jax.random.randint(key, (KDEV * N_VOX * N_FAS,), 0, FB_DEV, dtype=jnp.int32)
    return (fas_index * FB_DEV + offsets).astype(jnp.int32)


def draw_block_count(key, part):
    counts = jax.random.randint(key, (N_VOX * N_FAS,), KDEV // 4, KDEV + 1, dtype=jnp.int32)
    fullest = jax.random.randint(jax.random.fold_in(key, 7), (), 0, N_VOX * N_FAS, dtype=jnp.int32)
    places = jnp.arange(N_VOX * N_FAS, dtype=jnp.int32)
    return jnp.where(places == fullest, KDEV, counts).astype(jnp.int32)


def place_ends(entries, stream_key, smallest, largest):
    spot = [jax.random.randint(jax.random.fold_in(stream_key, axis), (), 0, length) for axis, length in enumerate(entries.shape)]
    longest = entries.shape.index(max(entries.shape))
    next_to = spot[:longest] + [(spot[longest] + 1) % entries.shape[longest]] + spot[longest + 1:]
    return entries.at[tuple(spot)].set(smallest).at[tuple(next_to)].set(largest)


def shard_levels(rng, extent, shards, least, top_value):
    level, own = 1.0, jax.random.fold_in(rng, 6)
    for position, blocks in shards:
        heights = jnp.exp(jax.random.uniform(jax.random.fold_in(own, position), (blocks,), jnp.float32, least / len(shards), top_value / len(shards)))
        level = level * jnp.repeat(heights, extent[position] // blocks).reshape([-1 if axis == position else 1 for axis in range(len(extent))])
    return level


def bell_draw(stream_key, dims, width, reach, shards=(), kind=jnp.bfloat16):
    values = jax.random.normal(stream_key, dims, jnp.float32) * width
    if len(shards) > 0:
        values = shard_levels(stream_key, dims, shards, -0.22, 0.18) * values
    return jnp.clip(values, min=-reach, max=reach).astype(kind)


def setup_inputs(seed: int = 0) -> dict:
    key_of = jax.random.split(jax.random.key(seed), 9)
    signal = bell_draw(key_of[0], (VBLOCKS, BV * DIRS), 1.0, 6.0, ((0, 8), (1, 16)), jnp.float32)
    initial_weights = jnp.clip(jnp.exp(math.log(2.0) - 2.9957323 * jax.random.uniform(key_of[1], (FASC,), jnp.float32) ** shard_levels(key_of[1], (FASC,), ((0, 16),), -0.2, 0.2)), 0.1, 2.0)
    coefficients = jnp.clip(0.0234375 * jax.random.uniform(key_of[2], (BLOCKS, BV * BF), jnp.float32) ** shard_levels(key_of[2], (BLOCKS, BV * BF), ((0, 128),), -0.2, 0.2), 0.0, 0.0234375).astype(jnp.bfloat16)
    block_rows = draw_block_rows(jax.random.fold_in(key_of[8], 71), 0)
    block_cols = draw_block_cols(jax.random.fold_in(key_of[8], 71), 0)
    block_atoms = place_ends(jax.random.randint(key_of[5], (BLOCKS, BF), 0, ATOMS), jax.random.fold_in(key_of[5], 1), 0, ATOMS - 1).astype(jnp.int32)
    block_count = draw_block_count(jax.random.fold_in(key_of[8], 71), 0)
    dictionary = bell_draw(key_of[7], (ATOMS, DIRS), 1.0, 6.0)
    return {"signal": signal, "initial_weights": initial_weights, "coefficients": coefficients, "block_rows": block_rows, "block_cols": block_cols, "block_atoms": block_atoms, "block_count": block_count, "dictionary": dictionary}


def reference(signal, initial_weights, coefficients, block_rows, block_cols, block_atoms, block_count, dictionary):
    device_total = N_VOX * N_FAS
    coef_all = coefficients.reshape(device_total, KDEV, BV, BF)
    rows_all = block_rows.reshape(device_total, KDEV)
    cols_all = block_cols.reshape(device_total, KDEV)
    atoms_all = block_atoms.reshape(device_total, KDEV, BF)
    live_all = (jnp.arange(KDEV, dtype=jnp.int32)[None, :] < block_count[:, None]).astype(jnp.float32)
    vox_blocks = signal.shape[0]
    fas_blocks = initial_weights.shape[0] // BF

    def forward(values):
        table = values.reshape(fas_blocks, BF)

        def accumulate(running, pieces):
            coef_blk, rows_blk, cols_blk, atoms_blk, live_blk = pieces
            atom_rows = dictionary[atoms_blk].astype(jnp.float32)
            scaled = coef_blk.astype(jnp.float32) * table[cols_blk][:, None, :]
            image_blk = jnp.einsum("kvj,kjd->kvd", scaled, atom_rows, precision=lax.Precision.HIGHEST)
            return running.at[rows_blk].add(image_blk * live_blk[:, None, None]), None

        start = jnp.zeros((vox_blocks, BV, DIRS), jnp.float32)
        running, _ = lax.scan(accumulate, start, (coef_all, rows_all, cols_all, atoms_all, live_all))
        return running.reshape(vox_blocks, BV * DIRS)

    def backward(resid):
        rows_view = resid.reshape(vox_blocks, BV, DIRS)

        def accumulate(running, pieces):
            coef_blk, rows_blk, cols_blk, atoms_blk, live_blk = pieces
            atom_rows = dictionary[atoms_blk].astype(jnp.float32)
            gathered = rows_view[rows_blk].astype(jnp.float32)
            inner = jnp.einsum("kvj,kvd->kjd", coef_blk.astype(jnp.float32), gathered, precision=lax.Precision.HIGHEST)
            contrib = jnp.sum(atom_rows * inner, axis=-1) * live_blk[:, None]
            return running.at[cols_blk].add(contrib), None

        start = jnp.zeros((fas_blocks, BF), jnp.float32)
        running, _ = lax.scan(accumulate, start, (coef_all, rows_all, cols_all, atoms_all, live_all))
        return running.reshape(-1)

    weights = initial_weights
    residual = forward(weights) - signal
    for sweep in range(ITERS):
        gradient = backward(residual)
        projected = jnp.where((weights > 0) | (gradient < 0), gradient, 0.0)
        image_pred = forward(projected)
        step_size = jnp.sum(projected * projected) / (jnp.sum(image_pred * image_pred) + 1e-6)
        weights = jnp.maximum(weights - step_size * projected, 0.0)
        residual = forward(weights) - signal
    return weights, residual
```

```python
import jax
import jax.numpy as jnp
from jax import lax
from jax.experimental import pallas as pl
from jax.experimental.pallas import tpu as pltpu
from jax.sharding import PartitionSpec as P

BV = 64
BF = 64
DIRS = 96
ATOMS = 360
ITERS = 5
SLOTS = 256
ROWS = 16
COLS = 512
NV = 8
NF = 16
QUAD = 4
GROUPS = (SLOTS + (QUAD - 1) * ROWS) // QUAD
GPAD = 80
SPAD = 384
ATOMPAD = 384
HALF = DIRS // 2

f32 = jnp.float32
bf16 = jnp.bfloat16


def low_lanes(shape):
    return lax.broadcasted_iota(jnp.int32, shape, len(shape) - 1) < 64


def split_pair(x):
    h = x.astype(bf16).astype(f32)
    low = x - h
    mask = low_lanes(x.shape)
    first = jnp.where(mask, h, pltpu.roll(low, 64, 1))
    second = jnp.where(mask, pltpu.roll(h, 64, 1), low)
    return first.astype(bf16), second.astype(bf16)


def fold(x):
    return x + pltpu.roll(x, 64, 1)


def kernel(
    perm,
    grow,
    last,
    valid,
    keep,
    has,
    coef,
    atoms,
    dict_t,
    cols_lane,
    cols_sub,
    w_in,
    sig_in,
    w_out,
    res_out,
    cg,
    at,
    sel,
    sel_t,
    u_p,
    u_w,
    buf,
    part,
    rs_in,
    r_all,
    r_two,
    contrib,
    b_two,
    g_part,
    g_in,
    g_all,
    p_two,
    sc_f,
    sc_v,
    sg_in,
    turn,
    sig_own,
    fin_out,
    fin_in,
    s_sig,
    r_sig,
    s_rs,
    r_rs,
    s_ag,
    r_ag,
    s_gr,
    r_gr,
    s_ga,
    r_ga,
    s_sf,
    r_sf,
    s_sv,
    r_sv,
    s_fin,
    r_fin,
):
    me_v = lax.axis_index("vox")
    me_f = lax.axis_index("fas")

    def copies(axis, src_at, dst, send_sem, recv_sem):
        n, me = (NF, me_f) if axis == "fas" else (NV, me_v)
        out, arrive = [], []
        for off in range(1, n):
            peer = lax.rem(me + off, n)
            out.append(
                pltpu.make_async_remote_copy(
                    src_ref=src_at(peer),
                    dst_ref=dst.at[me],
                    send_sem=send_sem.at[peer],
                    recv_sem=recv_sem.at[me],
                    device_id={axis: peer},
                    device_id_type=pl.DeviceIdType.MESH,
                )
            )
            arrive.append(
                pltpu.make_async_remote_copy(
                    src_ref=src_at(peer),
                    dst_ref=dst.at[peer],
                    send_sem=send_sem.at[peer],
                    recv_sem=recv_sem.at[peer],
                    device_id={axis: peer},
                    device_id_type=pl.DeviceIdType.MESH,
                )
            )

        def start():
            for c in out:
                c.start()

        def wait():
            for c in arrive:
                c.wait_recv()
            for c in out:
                c.wait_send()

        return start, wait

    barrier = pltpu.get_barrier_semaphore()
    for axis, n, me in (("fas", NF, me_f), ("vox", NV, me_v)):
        for off in range(1, n):
            pl.semaphore_signal(
                barrier,
                inc=1,
                device_id={axis: lax.rem(me + off, n)},
                device_id_type=pl.DeviceIdType.MESH,
            )

    def build(g, carry):
        mask = low_lanes((BV, 128))
        for half in range(2):
            k0 = g * QUAD + 2 * half
            x = coef[perm[k0]].astype(f32) * valid[k0]
            y = coef[perm[k0 + 1]].astype(f32) * valid[k0 + 1]
            cg[g, :, half * 128 : (half + 1) * 128] = jnp.where(mask, x, y).astype(bf16)
        row = atoms[pl.ds(g, 1), :]
        hot = (lax.broadcasted_iota(jnp.int32, (ATOMPAD, 256), 0) == row).astype(f32).astype(bf16)
        at[g] = jnp.dot(dict_t[...], hot, preferred_element_type=f32).astype(bf16)
        return carry

    lax.fori_loop(0, GROUPS, build, 0)
    sel[...] = (
        (lax.broadcasted_iota(jnp.int32, (COLS, SPAD), 0) == cols_lane[...]).astype(f32).astype(bf16)
    )
    sel_t[...] = (
        (lax.broadcasted_iota(jnp.int32, (SPAD, COLS), 1) == cols_sub[...]).astype(f32).astype(bf16)
    )
    contrib[...] = jnp.zeros_like(contrib)
    b_two[...] = jnp.zeros_like(b_two)

    pl.semaphore_wait(barrier, NF - 1 + NV - 1)

    start_sig, wait_sig = copies("fas", lambda p: sig_in.at[p // 2], sg_in, s_sig, r_sig)
    start_sig()

    def gather(values, u_ref):
        first, second = split_pair(values)
        p_two[0:256, :] = first
        p_two[256:512, :] = second
        got = fold(jnp.dot(sel_t[...], p_two[...], preferred_element_type=f32))
        mask = low_lanes((GPAD, 128))
        u_ref[:, 0:128] = jnp.where(mask, got[0:GPAD], got[GPAD : 2 * GPAD])
        u_ref[:, 128:256] = jnp.where(mask, got[2 * GPAD : 3 * GPAD], got[3 * GPAD : 4 * GPAD])

    def forward(u_ref):
        def step(g, acc):
            scaled = cg[g].astype(f32) * u_ref[pl.ds(g, 1), :]
            high = scaled.astype(bf16)
            low = (scaled - high.astype(f32)).astype(bf16)
            both = jnp.concatenate([high, low], axis=0)
            made = lax.dot_general(
                at[g], both, (((1,), (1,)), ((), ())), preferred_element_type=f32
            )
            acc = acc * keep[g] + made
            buf[g] = acc
            return acc

        lax.fori_loop(0, GROUPS, step, jnp.zeros((DIRS, 128), f32), unroll=4)
        mask = low_lanes((DIRS, 128))
        for pair in range(ROWS // 2):
            even = fold(buf[last[2 * pair]] * has[2 * pair])
            odd = fold(buf[last[2 * pair + 1]] * has[2 * pair + 1])
            both = jnp.where(mask, even, odd)
            part[2 * pair] = both[:HALF]
            part[2 * pair + 1] = both[HALF:]

    start_rs, wait_rs = copies("fas", lambda p: part.at[p], rs_in, s_rs, r_rs)
    start_ag, wait_ag = copies("fas", lambda p: r_all.at[me_f], r_all, s_ag, r_ag)
    start_gr, wait_gr = copies("vox", lambda p: g_part.at[p], g_in, s_gr, r_gr)
    start_ga, wait_ga = copies("vox", lambda p: g_all.at[me_v], g_all, s_ga, r_ga)
    start_sf, wait_sf = copies("fas", lambda p: sc_f.at[me_f], sc_f, s_sf, r_sf)
    start_sv, wait_sv = copies("vox", lambda p: sc_v.at[me_v], sc_v, s_sv, r_sv)
    start_fin, wait_fin = copies("fas", lambda p: fin_out.at[p], fin_in, s_fin, r_fin)

    def reduce_fas():
        start_rs()
        wait_rs()
        total = part[me_f]
        for off in range(1, NF):
            total = total + rs_in[lax.rem(me_f + off, NF)]
        return total

    w_out[...] = w_in[...]
    gather(w_in[...], u_w)
    forward(u_w)
    start_rs()
    wait_sig()
    sg_in[me_f] = sig_in[me_f // 2]
    for f in range(NF):
        for r in range(2):
            turn[r * 64 + f * 4 : r * 64 + f * 4 + 4, :] = sg_in[f, r * 4 : r * 4 + 4, :]
    turn[...] = jnp.transpose(turn[...])
    half_at = pl.multiple_of(lax.rem(me_f, 2) * HALF, 8)
    sig_own[...] = turn[pl.ds(half_at, HALF), :]
    wait_rs()
    total = part[me_f]
    for off in range(1, NF):
        total = total + rs_in[lax.rem(me_f + off, NF)]
    r_all[me_f] = total - sig_own[...]

    def sweep(_, carry):
        start_ag()
        wait_ag()
        for pair in range(ROWS // 2):
            x = jnp.concatenate([r_all[2 * pair], r_all[2 * pair + 1]], axis=0)
            even, odd = split_pair(x)
            r_two[2 * pair] = even
            r_two[2 * pair + 1] = odd

        def step(g, c):
            block = cg[g]
            twice = jnp.concatenate([block, block], axis=0)
            inner = jnp.dot(r_two[grow[g]], twice, preferred_element_type=f32)
            contrib[pl.ds(g, 1), :] = jnp.sum(inner * at[g].astype(f32), axis=0, keepdims=True)
            return c

        lax.fori_loop(0, GROUPS, step, 0, unroll=4)
        for half in range(2):
            first, second = split_pair(contrib[:, half * 128 : (half + 1) * 128])
            b_two[2 * half * GPAD : (2 * half + 1) * GPAD, :] = first
            b_two[(2 * half + 1) * GPAD : (2 * half + 2) * GPAD, :] = second
        got = fold(jnp.dot(sel[...], b_two[...], preferred_element_type=f32))
        mask = low_lanes((256, 128))
        g_part[...] = jnp.where(mask, got[0:256], got[256:512]).reshape(NV, 32, 128)
        start_gr()
        wait_gr()
        total = g_part[me_v]
        for off in range(1, NV):
            total = total + g_in[lax.rem(me_v + off, NV)]
        g_all[me_v] = total
        start_ga()
        wait_ga()
        weights = w_out[...]
        gradient = g_all[...].reshape(256, 128)
        projected = jnp.where((weights > 0) | (gradient < 0), gradient, 0.0)
        gather(projected, u_p)
        forward(u_p)
        image = reduce_fas()
        sc_f[me_f, 0:8] = jnp.sum((projected * projected).reshape(32, 8, 128), axis=0)
        sc_f[me_f, 8:16] = jnp.sum((image * image).reshape(6, 8, 128), axis=0)
        start_sf()
        wait_sf()
        sums = sc_f[0]
        for f in range(1, NF):
            sums = sums + sc_f[f]
        sc_v[me_v] = sums[8:16]
        start_sv()
        wait_sv()
        squares = sc_v[0]
        for v in range(1, NV):
            squares = squares + sc_v[v]
        grad_sq = jnp.sum(sums[0:8], axis=(0, 1), keepdims=True)
        image_sq = jnp.sum(squares, axis=(0, 1), keepdims=True)
        size = grad_sq / (image_sq + 1e-06)
        w_out[...] = jnp.maximum(weights - size * projected, 0.0)
        u_w[...] = jnp.maximum(u_w[...] - size * u_p[...], 0.0)
        forward(u_w)
        r_all[me_f] = reduce_fas() - sig_own[...]
        return carry

    lax.fori_loop(0, ITERS, sweep, 0)

    turn[0:HALF, :] = r_all[me_f]
    turn[HALF:, :] = jnp.zeros((128 - HALF, 128), f32)
    turn[...] = jnp.transpose(turn[...])
    for f in range(NF):
        for r in range(2):
            fin_out[f, r * 4 : r * 4 + 4, :] = turn[r * 64 + f * 4 : r * 64 + f * 4 + 4, :]
    start_fin()
    wait_fin()
    fin_in[me_f] = fin_out[me_f]
    res_out[...] = fin_in[...]


def local(
    signal,
    initial_weights,
    coefficients,
    block_rows,
    block_cols,
    block_atoms,
    block_count,
    dictionary,
):
    i32 = jnp.int32
    rows = block_rows - lax.axis_index("vox") * ROWS
    cols = block_cols - lax.axis_index("fas") * COLS
    slots = jnp.arange(SLOTS, dtype=i32)
    lives = slots < block_count[0]
    hot = (rows[:, None] == jnp.arange(ROWS, dtype=i32)[None, :]) & lives[:, None]
    before = (slots[None, :] < slots[:, None]) & lives[None, :] & (rows[None, :] == rows[:, None])
    rank = jnp.sum(before.astype(i32), axis=1)
    count = jnp.sum(hot.astype(i32), axis=0)
    groups = (count + QUAD - 1) // QUAD
    span = jnp.arange(ROWS, dtype=i32)
    ends = jnp.sum(jnp.where(span[None, :] <= span[:, None], groups[None, :], 0), axis=1)
    firsts = ends - groups
    place = jnp.where(
        lives, jnp.sum(jnp.where(hot, firsts[None, :], 0), axis=1) * QUAD + rank, -1
    )
    spots = jnp.arange(GPAD * QUAD, dtype=i32)
    match = place[None, :] == spots[:, None]
    perm = jnp.sum(jnp.where(match, slots[None, :], 0), axis=1)
    filled = jnp.any(match, axis=1)
    col_at = jnp.sum(jnp.where(match, cols[None, :] + 1, 0), axis=1) - 1
    col_q = jnp.concatenate(
        [col_at.reshape(GPAD, QUAD).T.reshape(-1), jnp.full((SPAD - GPAD * QUAD,), -1, i32)]
    )
    turns = jnp.arange(GPAD, dtype=i32)
    grow = jnp.minimum(jnp.sum((ends[None, :] <= turns[:, None]).astype(i32), axis=1), ROWS - 1)
    is_first = jnp.any((firsts[None, :] == turns[:, None]) & (groups[None, :] > 0), axis=1)
    keep = 1.0 - is_first.astype(f32)
    last = jnp.maximum(ends - 1, 0)
    has = (groups > 0).astype(f32)
    atoms = block_atoms[perm].reshape(GPAD, QUAD * BF)
    coef = coefficients.reshape(SLOTS, BV, BF)
    coef = jnp.concatenate([coef, coef], axis=2)
    dict_t = jnp.pad(dictionary.T, ((0, 0), (0, ATOMPAD - ATOMS)))
    w_in = initial_weights.reshape(2, 256, BF)
    w_in = jnp.concatenate([w_in[0], w_in[1]], axis=1)
    sig_in = jnp.pad(signal.reshape(8, 8, DIRS), ((0, 0), (0, 0), (0, 128 - DIRS)))

    smem = pl.BlockSpec(memory_space=pltpu.SMEM)
    vmem = pl.BlockSpec(memory_space=pltpu.VMEM)
    dma = pltpu.SemaphoreType.DMA
    w_new, res = pl.pallas_call(
        kernel,
        out_shape=(
            jax.ShapeDtypeStruct((256, 128), f32),
            jax.ShapeDtypeStruct((NF, 8, 128), f32),
        ),
        in_specs=[smem] * 6 + [vmem] * 7,
        out_specs=(vmem, vmem),
        scratch_shapes=[
            pltpu.VMEM((GROUPS, BV, 256), bf16),
            pltpu.VMEM((GROUPS, DIRS, 256), bf16),
            pltpu.VMEM((COLS, SPAD), bf16),
            pltpu.VMEM((SPAD, COLS), bf16),
            pltpu.VMEM((GPAD, 256), f32),
            pltpu.VMEM((GPAD, 256), f32),
            pltpu.VMEM((GROUPS, DIRS, 128), f32),
            pltpu.VMEM((NF, HALF, 128), f32),
            pltpu.VMEM((NF, HALF, 128), f32),
            pltpu.VMEM((NF, HALF, 128), f32),
            pltpu.VMEM((ROWS, DIRS, 128), bf16),
            pltpu.VMEM((GPAD, 256), f32),
            pltpu.VMEM((SPAD, 128), bf16),
            pltpu.VMEM((NV, 32, 128), f32),
            pltpu.VMEM((NV, 32, 128), f32),
            pltpu.VMEM((NV, 32, 128), f32),
            pltpu.VMEM((COLS, 128), bf16),
            pltpu.VMEM((NF, 16, 128), f32),
            pltpu.VMEM((NV, 8, 128), f32),
            pltpu.VMEM((NF, 8, 128), f32),
            pltpu.VMEM((128, 128), f32),
            pltpu.VMEM((HALF, 128), f32),
            pltpu.VMEM((NF, 8, 128), f32),
            pltpu.VMEM((NF, 8, 128), f32),
        ]
        + [dma((NF,)), dma((NF,))] * 3
        + [dma((NV,)), dma((NV,))] * 2
        + [dma((NF,)), dma((NF,)), dma((NV,)), dma((NV,)), dma((NF,)), dma((NF,))],
        compiler_params=pltpu.CompilerParams(
            collective_id=0, has_side_effects=True, vmem_limit_bytes=48 * 1024 * 1024
        ),
    )(
        perm,
        grow,
        last,
        filled.astype(f32),
        keep,
        has,
        coef,
        atoms,
        dict_t,
        col_q[None, :],
        col_q[:, None],
        w_in,
        sig_in,
    )
    weights = jnp.concatenate([w_new[:, :BF], w_new[:, BF:]], axis=0).reshape(-1)
    res = res[:, :, :HALF].reshape(8, 2, 8, HALF).transpose(0, 2, 1, 3)
    return (weights, res.reshape(ROWS, 4 * DIRS))


def solution(mesh):
    placed = (
        P("vox", "fas"),
        P("fas"),
        P(("vox", "fas"), None),
        P(("vox", "fas")),
        P(("vox", "fas")),
        P(("vox", "fas"), None),
        P(("vox", "fas")),
        P(),
    )
    return jax.shard_map(
        local, mesh=mesh, in_specs=placed, out_specs=(P("fas"), P("vox", "fas")), check_vma=False
    )
```

```python
import jax
import jax.numpy as jnp
from jax import lax
from jax.experimental import pallas as pl
from jax.experimental.pallas import tpu as pltpu
from jax.sharding import PartitionSpec as P

BV = 64
BF = 64
DIRS = 96
ATOMS = 360
ITERS = 5
SLOTS = 256
ROWS = 16
COLS = 512
NV = 8
NF = 16
SIDE = 4
CHIPS = 64
QUAD = 4
GROUPS = (SLOTS + (QUAD - 1) * ROWS) // QUAD
GPAD = 80
SPAD = 384
ATOMPAD = 384
HALF = DIRS // 2


def hops(off):
    return sum(min(d, SIDE - d) for d in off)


CHIP_FAR_FIRST = sorted(
    [(y, z, x) for y in range(SIDE) for z in range(SIDE) for x in range(SIDE) if y + z + x],
    key=lambda off: (-hops(off), off),
)
FAR_FIRST = [off[1:] for off in CHIP_FAR_FIRST if off[0] == 0]

f32 = jnp.float32
bf16 = jnp.bfloat16


def low_lanes(shape):
    return lax.broadcasted_iota(jnp.int32, shape, len(shape) - 1) < 64


def split_pair(x):
    h = x.astype(bf16).astype(f32)
    low = x - h
    mask = low_lanes(x.shape)
    first = jnp.where(mask, h, pltpu.roll(low, 64, 1))
    second = jnp.where(mask, pltpu.roll(h, 64, 1), low)
    return first.astype(bf16), second.astype(bf16)


def fold(x):
    return x + pltpu.roll(x, 64, 1)


def kernel(
    grow,
    last,
    keep,
    has,
    coef_hbm,
    digits,
    dict_t,
    place_lane,
    cols_lane,
    cols_sub,
    w_in,
    sig_in,
    w_out,
    res_out,
    coef,
    wide,
    pick,
    names,
    cg,
    at,
    sel,
    sel_t,
    u_p,
    u_w,
    buf,
    part,
    rs_in,
    r_all,
    r_two,
    contrib,
    b_two,
    g_part,
    g_pair,
    g_in,
    g_all,
    p_two,
    sc_in,
    sc_pair,
    sg_in,
    turn,
    sig_own,
    fin_out,
    fin_in,
    s_sig,
    r_sig,
    s_rs,
    r_rs,
    s_ag,
    r_ag,
    s_gr,
    r_gr,
    s_sc,
    r_sc,
    s_fin,
    r_fin,
    s_two,
    r_twin,
    s_coef,
):
    me_v = lax.axis_index("vox")
    me_f = lax.axis_index("fas")
    me_c = lax.rem(me_v, 2)
    me_y = me_v // 2
    twin = me_v + 1 - 2 * me_c
    fetch = pltpu.make_async_copy(coef_hbm, coef, s_coef)
    fetch.start()

    def remote(src, dst, send_sem, recv_sem, device):
        return pltpu.make_async_remote_copy(
            src_ref=src,
            dst_ref=dst,
            send_sem=send_sem,
            recv_sem=recv_sem,
            device_id=device,
            device_id_type=pl.DeviceIdType.MESH,
        )

    def pair(out, arrive):
        def start():
            for c in out:
                c.start()

        def wait():
            for c in arrive:
                c.wait_recv()
            for c in out:
                c.wait_send()

        return start, wait

    def copies(src_at, dst, send_sem, recv_sem):
        out, arrive = [], []
        for off in FAR_FIRST:
            peer = other_fas(off)
            where = {"fas": peer}
            out.append(
                remote(src_at(peer), dst.at[me_f], send_sem.at[peer], recv_sem.at[me_f], where)
            )
            arrive.append(
                remote(src_at(peer), dst.at[peer], send_sem.at[peer], recv_sem.at[peer], where)
            )
        return pair(out, arrive)

    def other_fas(off):
        return lax.rem(me_f // SIDE + off[0], SIDE) * SIDE + lax.rem(me_f + off[1], SIDE)

    def with_twin(src, dst, landing, index):
        sems, where = (s_two.at[index], r_twin.at[index]), {"vox": twin}
        return pair([remote(src, dst, *sems, where)], [remote(src, landing, *sems, where)])

    barrier = pltpu.get_barrier_semaphore()
    pl.semaphore_signal(
        barrier, inc=1, device_id={"vox": twin}, device_id_type=pl.DeviceIdType.MESH
    )
    for off in CHIP_FAR_FIRST:
        pl.semaphore_signal(
            barrier,
            inc=1,
            device_id={"vox": lax.rem(me_y + off[0], SIDE) * 2 + me_c, "fas": other_fas(off[1:])},
            device_id_type=pl.DeviceIdType.MESH,
        )

    turn_row = lax.broadcasted_iota(jnp.int32, (GPAD, SLOTS), 0) * QUAD
    for q in range(QUAD):
        hot = (place_lane[...] == turn_row + q).astype(f32).astype(bf16)
        pick[q * GPAD : (q + 1) * GPAD, :] = hot
    pick[QUAD * GPAD :, :] = jnp.zeros((SPAD - QUAD * GPAD, SLOTS), bf16)
    found = jnp.dot(pick[0 : QUAD * GPAD, :], digits[...], preferred_element_type=f32)
    found = jnp.where(low_lanes(found.shape), found, found * 256.0)
    found = fold(found)
    mask = low_lanes((GPAD, 128))
    names[:, 0:128] = jnp.where(mask, found[0:GPAD], found[GPAD : 2 * GPAD])
    names[:, 128:256] = jnp.where(mask, found[2 * GPAD : 3 * GPAD], found[3 * GPAD :])

    def name_atoms(g, carry):
        row = names[pl.ds(g, 1), :].astype(jnp.int32)
        hot = (lax.broadcasted_iota(jnp.int32, (ATOMPAD, 256), 0) == row).astype(f32).astype(bf16)
        at[g] = jnp.dot(dict_t[...], hot, preferred_element_type=f32).astype(bf16)
        return carry

    lax.fori_loop(0, GROUPS, name_atoms, 0, unroll=4)
    where_col = (lax.broadcasted_iota(jnp.int32, (COLS, SLOTS), 0) == cols_lane[...]).astype(f32)
    sel[...] = lax.dot_general(
        where_col.astype(bf16), pick[...], (((1,), (1,)), ((), ())), preferred_element_type=f32
    ).astype(bf16)
    where_col = (lax.broadcasted_iota(jnp.int32, (SLOTS, COLS), 1) == cols_sub[...]).astype(f32)
    sel_t[...] = jnp.dot(
        pick[...], where_col.astype(bf16), preferred_element_type=f32
    ).astype(bf16)
    contrib[...] = jnp.zeros_like(contrib)
    b_two[...] = jnp.zeros_like(b_two)

    pl.semaphore_wait(barrier, CHIPS)
    start_sig, wait_sig = copies(lambda p: sig_in.at[p // 2], sg_in, s_sig, r_sig)
    start_sig()

    fetch.wait()

    def spread(t, carry):
        at_lane = pl.multiple_of(t * 128, 128)
        moved = jnp.dot(pick[0 : QUAD * GPAD, :], coef[:, pl.ds(at_lane, 128)], preferred_element_type=f32)
        mask = low_lanes((GPAD, 128))
        for half in range(2):
            x = moved[2 * half * GPAD : (2 * half + 1) * GPAD]
            y = moved[(2 * half + 1) * GPAD : (2 * half + 2) * GPAD]
            lanes = slice(half * 128, half * 128 + 128)
            even = jnp.where(mask, x, pltpu.roll(y, 64, 1))
            odd = jnp.where(mask, pltpu.roll(x, 64, 1), y)
            first = pl.multiple_of(t * (2 * GPAD), 8)
            wide[half, pl.ds(first, GPAD), :] = even
            wide[half, pl.ds(first + GPAD, GPAD), :] = odd
        return carry

    lax.fori_loop(0, BV // 2, spread, 0, unroll=4)

    def bring(g, carry):
        for half in range(2):
            block = wide[half, pl.ds(g, BV, stride=GPAD), :]
            cg[g, :, half * 128 : half * 128 + 128] = block.astype(bf16)
        return carry

    lax.fori_loop(0, GROUPS, bring, 0, unroll=4)


    def gather(values, u_ref):
        first, second = split_pair(values)
        p_two[0:256, :] = first
        p_two[256:512, :] = second
        got = fold(jnp.dot(sel_t[...], p_two[...], preferred_element_type=f32))
        mask = low_lanes((GPAD, 128))
        u_ref[:, 0:128] = jnp.where(mask, got[0:GPAD], got[GPAD : 2 * GPAD])
        u_ref[:, 128:256] = jnp.where(mask, got[2 * GPAD : 3 * GPAD], got[3 * GPAD : 4 * GPAD])

    def forward(u_ref):
        def step(g, acc):
            scaled = cg[g].astype(f32) * u_ref[pl.ds(g, 1), :]
            high = scaled.astype(bf16)
            low = (scaled - high.astype(f32)).astype(bf16)
            both = jnp.concatenate([high, low], axis=0)
            made = lax.dot_general(
                at[g], both, (((1,), (1,)), ((), ())), preferred_element_type=f32
            )
            acc = acc * keep[g] + made
            buf[g] = acc
            return acc

        lax.fori_loop(0, GROUPS, step, jnp.zeros((DIRS, 128), f32), unroll=19)
        mask = low_lanes((DIRS, 128))
        for pair in range(ROWS // 2):
            even = fold(buf[last[2 * pair]] * has[2 * pair])
            odd = fold(buf[last[2 * pair + 1]] * has[2 * pair + 1])
            both = jnp.where(mask, even, odd)
            part[2 * pair] = both[:HALF]
            part[2 * pair + 1] = both[HALF:]

    start_rs, wait_rs = copies(lambda p: part.at[p], rs_in, s_rs, r_rs)
    start_ag, wait_ag = copies(lambda p: r_all.at[me_f], r_all, s_ag, r_ag)
    start_fin, wait_fin = copies(lambda p: fin_out.at[p], fin_in, s_fin, r_fin)

    start_swap, wait_swap = with_twin(g_part.at[1 - me_c], g_pair, g_pair, 0)
    start_back, wait_back = with_twin(g_all.at[me_c], g_all.at[me_c], g_all.at[1 - me_c], 1)
    out, arrive = [], []
    for off in (2, 1, 3):
        y = lax.rem(me_y + off, SIDE)
        where = {"vox": y * 2 + me_c}
        out.append(remote(g_in.at[me_y], g_in.at[me_y], s_gr.at[y], r_gr.at[me_y], where))
        arrive.append(remote(g_in.at[y], g_in.at[y], s_gr.at[y], r_gr.at[y], where))
    start_gr, wait_gr = pair(out, arrive)

    mine = me_y * NF + me_f
    out, arrive = [], []
    for off in CHIP_FAR_FIRST:
        y, f = lax.rem(me_y + off[0], SIDE), other_fas(off[1:])
        where = {"vox": y * 2 + me_c, "fas": f}
        chip = y * NF + f
        src = sc_in.at[mine, 0:1]
        out.append(remote(src, src, s_sc.at[chip], r_sc.at[mine], where))
        src = sc_in.at[chip, 0:1]
        arrive.append(remote(src, src, s_sc.at[chip], r_sc.at[chip], where))
    start_sc, wait_sc = pair(out, arrive)
    start_two, wait_two = with_twin(sc_pair.at[me_c], sc_pair.at[me_c], sc_pair.at[1 - me_c], 2)

    def added():
        total = part[me_f]
        for off in range(1, NF):
            total = total + rs_in[lax.rem(me_f + off, NF)]
        return total

    def reduce_fas():
        start_rs()
        wait_rs()
        return added()

    w_out[...] = w_in[...]
    gather(w_in[...], u_w)
    forward(u_w)
    start_rs()
    wait_sig()
    sg_in[me_f] = sig_in[me_f // 2]
    for f in range(NF):
        for r in range(2):
            turn[r * 64 + f * 4 : r * 64 + f * 4 + 4, :] = sg_in[f, r * 4 : r * 4 + 4, :]
    turn[...] = jnp.transpose(turn[...])
    half_at = pl.multiple_of(lax.rem(me_f, 2) * HALF, 8)
    sig_own[...] = turn[pl.ds(half_at, HALF), :]
    wait_rs()
    r_all[me_f] = added() - sig_own[...]

    def sweep(_, carry):
        start_ag()
        wait_ag()
        for pair in range(ROWS // 2):
            x = jnp.concatenate([r_all[2 * pair], r_all[2 * pair + 1]], axis=0)
            even, odd = split_pair(x)
            r_two[2 * pair] = even
            r_two[2 * pair + 1] = odd

        def step(g, c):
            block = cg[g]
            twice = jnp.concatenate([block, block], axis=0)
            inner = jnp.dot(r_two[grow[g]], twice, preferred_element_type=f32)
            contrib[pl.ds(g, 1), :] = jnp.sum(inner * at[g].astype(f32), axis=0, keepdims=True)
            return c

        lax.fori_loop(0, GROUPS, step, 0, unroll=19)
        for half in range(2):
            first, second = split_pair(contrib[:, half * 128 : (half + 1) * 128])
            b_two[2 * half * GPAD : (2 * half + 1) * GPAD, :] = first
            b_two[(2 * half + 1) * GPAD : (2 * half + 2) * GPAD, :] = second
        got = fold(jnp.dot(sel[...], b_two[...], preferred_element_type=f32))
        mask = low_lanes((256, 128))
        g_part[...] = jnp.where(mask, got[0:256], got[256:512]).reshape(2, 128, 128)
        start_swap()
        wait_swap()
        g_in[me_y] = g_part[me_c] + g_pair[...]
        start_gr()
        wait_gr()
        g_all[me_c] = (g_in[0] + g_in[1]) + (g_in[2] + g_in[3])
        start_back()
        wait_back()
        weights = w_out[...]
        gradient = g_all[...].reshape(256, 128)
        projected = jnp.where((weights > 0) | (gradient < 0), gradient, 0.0)
        gather(projected, u_p)
        forward(u_p)
        image = reduce_fas()
        squares = jnp.sum((image * image).reshape(6, 8, 128), axis=0)
        steep = jnp.sum((projected * projected).reshape(32, 8, 128), axis=0)
        squares = jnp.sum(fold(squares), axis=0, keepdims=True)
        steep = jnp.sum(fold(steep), axis=0, keepdims=True)
        sc_in[mine, 0:1, :] = jnp.where(low_lanes((1, 128)), squares, steep)
        start_sc()
        wait_sc()
        sums = jnp.sum(sc_in[:, 0, :], axis=0, keepdims=True)
        sc_pair[me_c] = jnp.broadcast_to(sums, (8, 128))
        start_two()
        wait_two()
        both = sc_pair[0, 0:1, :] + sc_pair[1, 0:1, :]
        mask = low_lanes((1, 128))
        image_sq = jnp.sum(jnp.where(mask, both, 0.0), axis=(0, 1), keepdims=True)
        grad_sq = jnp.sum(jnp.where(mask, 0.0, both), axis=(0, 1), keepdims=True) * (1.0 / NV)
        size = grad_sq / (image_sq + 1e-06)
        w_out[...] = jnp.maximum(weights - size * projected, 0.0)
        u_w[...] = jnp.maximum(u_w[...] - size * u_p[...], 0.0)
        forward(u_w)
        r_all[me_f] = reduce_fas() - sig_own[...]
        return carry

    lax.fori_loop(0, ITERS, sweep, 0)

    turn[0:HALF, :] = r_all[me_f]
    turn[HALF:, :] = jnp.zeros((128 - HALF, 128), f32)
    turn[...] = jnp.transpose(turn[...])
    for f in range(NF):
        for r in range(2):
            fin_out[f, r * 4 : r * 4 + 4, :] = turn[r * 64 + f * 4 : r * 64 + f * 4 + 4, :]
    start_fin()
    wait_fin()
    fin_in[me_f] = fin_out[me_f]
    res_out[...] = fin_in[...]


def local(
    signal,
    initial_weights,
    coefficients,
    block_rows,
    block_cols,
    block_atoms,
    block_count,
    dictionary,
):
    i32 = jnp.int32
    rows = block_rows - lax.axis_index("vox") * ROWS
    cols = block_cols - lax.axis_index("fas") * COLS
    slots = jnp.arange(SLOTS, dtype=i32)
    lives = slots < block_count[0]
    hot = (rows[:, None] == jnp.arange(ROWS, dtype=i32)[None, :]) & lives[:, None]
    before = (slots[None, :] < slots[:, None]) & lives[None, :] & (rows[None, :] == rows[:, None])
    rank = jnp.sum(before.astype(i32), axis=1)
    count = jnp.sum(hot.astype(i32), axis=0)
    groups = (count + QUAD - 1) // QUAD
    span = jnp.arange(ROWS, dtype=i32)
    ends = jnp.sum(jnp.where(span[None, :] <= span[:, None], groups[None, :], 0), axis=1)
    firsts = ends - groups
    place = jnp.where(
        lives, jnp.sum(jnp.where(hot, firsts[None, :], 0), axis=1) * QUAD + rank, -1
    )
    turns = jnp.arange(GPAD, dtype=i32)
    grow = jnp.minimum(jnp.sum((ends[None, :] <= turns[:, None]).astype(i32), axis=1), ROWS - 1)
    is_first = jnp.any((firsts[None, :] == turns[:, None]) & (groups[None, :] > 0), axis=1)
    keep = 1.0 - is_first.astype(f32)
    last = jnp.maximum(ends - 1, 0)
    has = (groups > 0).astype(f32)
    upper = (block_atoms >= 256).astype(i32)
    digits = jnp.concatenate([block_atoms - 256 * upper, upper], axis=1).astype(bf16)
    dict_t = jnp.pad(dictionary.T, ((0, 0), (0, ATOMPAD - ATOMS)))
    w_in = initial_weights.reshape(2, 256, BF)
    w_in = jnp.concatenate([w_in[0], w_in[1]], axis=1)
    sig_in = jnp.pad(signal.reshape(8, 8, DIRS), ((0, 0), (0, 0), (0, 128 - DIRS)))

    smem = pl.BlockSpec(memory_space=pltpu.SMEM)
    vmem = pl.BlockSpec(memory_space=pltpu.VMEM)
    dma = pltpu.SemaphoreType.DMA
    w_new, res = pl.pallas_call(
        kernel,
        out_shape=(
            jax.ShapeDtypeStruct((256, 128), f32),
            jax.ShapeDtypeStruct((NF, 8, 128), f32),
        ),
        in_specs=[smem] * 4 + [pl.BlockSpec(memory_space=pl.ANY)] + [vmem] * 7,
        out_specs=(vmem, vmem),
        scratch_shapes=[
            pltpu.VMEM((SLOTS, BV * BF), bf16),
            pltpu.VMEM((2, BV * GPAD, 128), f32),
            pltpu.VMEM((SPAD, SLOTS), bf16),
            pltpu.VMEM((GPAD, 256), f32),
            pltpu.VMEM((GROUPS, BV, 256), bf16),
            pltpu.VMEM((GROUPS, DIRS, 256), bf16),
            pltpu.VMEM((COLS, SPAD), bf16),
            pltpu.VMEM((SPAD, COLS), bf16),
            pltpu.VMEM((GPAD, 256), f32),
            pltpu.VMEM((GPAD, 256), f32),
            pltpu.VMEM((GROUPS, DIRS, 128), f32),
            pltpu.VMEM((NF, HALF, 128), f32),
            pltpu.VMEM((NF, HALF, 128), f32),
            pltpu.VMEM((NF, HALF, 128), f32),
            pltpu.VMEM((ROWS, DIRS, 128), bf16),
            pltpu.VMEM((GPAD, 256), f32),
            pltpu.VMEM((SPAD, 128), bf16),
            pltpu.VMEM((2, 128, 128), f32),
            pltpu.VMEM((128, 128), f32),
            pltpu.VMEM((SIDE, 128, 128), f32),
            pltpu.VMEM((2, 128, 128), f32),
            pltpu.VMEM((COLS, 128), bf16),
            pltpu.VMEM((CHIPS, 8, 128), f32),
            pltpu.VMEM((2, 8, 128), f32),
            pltpu.VMEM((NF, 8, 128), f32),
            pltpu.VMEM((128, 128), f32),
            pltpu.VMEM((HALF, 128), f32),
            pltpu.VMEM((NF, 8, 128), f32),
            pltpu.VMEM((NF, 8, 128), f32),
        ]
        + [dma((n,)) for n in (NF, NF, NF, SIDE, CHIPS, NF, 3) for _ in range(2)]
        + [dma(())],
        compiler_params=pltpu.CompilerParams(
            collective_id=0, has_side_effects=True, vmem_limit_bytes=52 * 1024 * 1024
        ),
    )(
        grow,
        last,
        keep,
        has,
        coefficients,
        digits,
        dict_t,
        place[None, :],
        cols[None, :],
        cols[:, None],
        w_in,
        sig_in,
    )
    weights = jnp.concatenate([w_new[:, :BF], w_new[:, BF:]], axis=0).reshape(-1)
    res = res[:, :, :HALF].reshape(8, 2, 8, HALF).transpose(0, 2, 1, 3)
    return (weights, res.reshape(ROWS, 4 * DIRS))


def solution(mesh):
    placed = (
        P("vox", "fas"),
        P("fas"),
        P(("vox", "fas"), None),
        P(("vox", "fas")),
        P(("vox", "fas")),
        P(("vox", "fas"), None),
        P(("vox", "fas")),
        P(),
    )
    return jax.shard_map(
        local, mesh=mesh, in_specs=placed, out_specs=(P("fas"), P("vox", "fas")), check_vma=False
    )
```

```python
import jax
import jax.numpy as jnp
from jax import lax
from jax.experimental import pallas as pl
from jax.experimental.pallas import tpu as pltpu
from jax.sharding import PartitionSpec as P

BV = 64
BF = 64
DIRS = 96
ATOMS = 360
ITERS = 5
SLOTS = 256
ROWS = 16
COLS = 512
NV = 8
NF = 16
SIDE = 4
CHIPS = 64
QUAD = 4
GROUPS = (SLOTS + (QUAD - 1) * ROWS) // QUAD
GPAD = 80
SPAD = 384
ATOMPAD = 384
HALF = DIRS // 2
PIECE = HALF // 2


def hops(off):
    return sum(min(d, SIDE - d) for d in off)


CHIP_FAR_FIRST = sorted(
    [(y, z, x) for y in range(SIDE) for z in range(SIDE) for x in range(SIDE) if y + z + x],
    key=lambda off: (-hops(off), off),
)
FAR_FIRST = [off[1:] for off in CHIP_FAR_FIRST if off[0] == 0]

f32 = jnp.float32
bf16 = jnp.bfloat16


def low_lanes(shape):
    return lax.broadcasted_iota(jnp.int32, shape, len(shape) - 1) < 64


def split_pair(x):
    h = x.astype(bf16).astype(f32)
    low = x - h
    mask = low_lanes(x.shape)
    first = jnp.where(mask, h, pltpu.roll(low, 64, 1))
    second = jnp.where(mask, pltpu.roll(h, 64, 1), low)
    return first.astype(bf16), second.astype(bf16)


def fold(x):
    return x + pltpu.roll(x, 64, 1)


def kernel(
    grow,
    last,
    keep,
    has,
    coef_hbm,
    digits,
    dict_t,
    place_lane,
    cols_lane,
    cols_sub,
    w_in,
    sig_in,
    w_out,
    res_out,
    coef,
    wide,
    pick,
    names,
    cg,
    at,
    sel,
    sel_t,
    u_p,
    u_w,
    table,
    buf,
    part,
    rs_in,
    r_all,
    r_two,
    contrib,
    b_two,
    g_part,
    g_pair,
    g_in,
    g_all,
    p_two,
    sc_in,
    sc_pair,
    sg_in,
    turn,
    sig_own,
    fin_out,
    fin_in,
    s_sig,
    r_sig,
    s_rs,
    r_rs,
    s_ag,
    r_ag,
    s_gr,
    r_gr,
    s_sc,
    r_sc,
    s_fin,
    r_fin,
    s_two,
    r_twin,
    s_coef,
):
    me_v = lax.axis_index("vox")
    me_f = lax.axis_index("fas")
    me_c = lax.rem(me_v, 2)
    me_y = me_v // 2
    twin = me_v + 1 - 2 * me_c
    fetch = pltpu.make_async_copy(coef_hbm, coef, s_coef)
    fetch.start()

    def remote(src, dst, send_sem, recv_sem, device):
        return pltpu.make_async_remote_copy(
            src_ref=src,
            dst_ref=dst,
            send_sem=send_sem,
            recv_sem=recv_sem,
            device_id=device,
            device_id_type=pl.DeviceIdType.MESH,
        )

    def pair(out, arrive):
        def start():
            for c in out:
                c.start()

        def wait():
            for c in arrive:
                c.wait_recv()
            for c in out:
                c.wait_send()

        return start, wait

    def copies(src_at, dst, send_sem, recv_sem):
        out, arrive = [], []
        for off in FAR_FIRST:
            peer = other_fas(off)
            where = {"fas": peer}
            out.append(
                remote(src_at(peer), dst.at[me_f], send_sem.at[peer], recv_sem.at[me_f], where)
            )
            arrive.append(
                remote(src_at(peer), dst.at[peer], send_sem.at[peer], recv_sem.at[peer], where)
            )
        return pair(out, arrive)

    def half_copies(src_at, dst, send_sem, recv_sem):
        return [
            copies(lambda p: src_at(h, p), dst.at[h], send_sem.at[h], recv_sem.at[h])
            for h in range(2)
        ]

    def other_fas(off):
        return lax.rem(me_f // SIDE + off[0], SIDE) * SIDE + lax.rem(me_f + off[1], SIDE)

    def with_twin(src, dst, landing, index):
        sems, where = (s_two.at[index], r_twin.at[index]), {"vox": twin}
        return pair([remote(src, dst, *sems, where)], [remote(src, landing, *sems, where)])

    barrier = pltpu.get_barrier_semaphore()
    pl.semaphore_signal(
        barrier, inc=1, device_id={"vox": twin}, device_id_type=pl.DeviceIdType.MESH
    )
    for off in CHIP_FAR_FIRST:
        pl.semaphore_signal(
            barrier,
            inc=1,
            device_id={"vox": lax.rem(me_y + off[0], SIDE) * 2 + me_c, "fas": other_fas(off[1:])},
            device_id_type=pl.DeviceIdType.MESH,
        )

    turn_row = lax.broadcasted_iota(jnp.int32, (GPAD, SLOTS), 0) * QUAD
    for q in range(QUAD):
        hot = (place_lane[...] == turn_row + q).astype(f32).astype(bf16)
        pick[q * GPAD : (q + 1) * GPAD, :] = hot
    pick[QUAD * GPAD :, :] = jnp.zeros((SPAD - QUAD * GPAD, SLOTS), bf16)
    found = jnp.dot(pick[0 : QUAD * GPAD, :], digits[...], preferred_element_type=f32)
    found = jnp.where(low_lanes(found.shape), found, found * 256.0)
    found = fold(found)
    mask = low_lanes((GPAD, 128))
    names[:, 0:128] = jnp.where(mask, found[0:GPAD], found[GPAD : 2 * GPAD])
    names[:, 128:256] = jnp.where(mask, found[2 * GPAD : 3 * GPAD], found[3 * GPAD :])

    def name_atoms(g, carry):
        row = names[pl.ds(g, 1), :].astype(jnp.int32)
        hot = (lax.broadcasted_iota(jnp.int32, (ATOMPAD, 256), 0) == row).astype(f32).astype(bf16)
        made = jnp.dot(dict_t[...], hot, preferred_element_type=f32).astype(bf16)
        at[0, g] = made[:HALF]
        at[1, g] = made[HALF:]
        return carry

    lax.fori_loop(0, GROUPS, name_atoms, 0, unroll=4)
    where_col = (lax.broadcasted_iota(jnp.int32, (COLS, SLOTS), 0) == cols_lane[...]).astype(f32)
    sel[...] = lax.dot_general(
        where_col.astype(bf16), pick[...], (((1,), (1,)), ((), ())), preferred_element_type=f32
    ).astype(bf16)
    where_col = (lax.broadcasted_iota(jnp.int32, (SLOTS, COLS), 1) == cols_sub[...]).astype(f32)
    sel_t[...] = jnp.dot(
        pick[...], where_col.astype(bf16), preferred_element_type=f32
    ).astype(bf16)
    contrib[...] = jnp.zeros_like(contrib)
    b_two[...] = jnp.zeros_like(b_two)

    pl.semaphore_wait(barrier, CHIPS)
    start_sig, wait_sig = copies(lambda p: sig_in.at[p // 2], sg_in, s_sig, r_sig)
    start_sig()

    fetch.wait()

    def spread(t, carry):
        at_lane = pl.multiple_of(t * 128, 128)
        moved = jnp.dot(pick[0 : QUAD * GPAD, :], coef[:, pl.ds(at_lane, 128)], preferred_element_type=f32)
        mask = low_lanes((GPAD, 128))
        for half in range(2):
            x = moved[2 * half * GPAD : (2 * half + 1) * GPAD]
            y = moved[(2 * half + 1) * GPAD : (2 * half + 2) * GPAD]
            lanes = slice(half * 128, half * 128 + 128)
            even = jnp.where(mask, x, pltpu.roll(y, 64, 1))
            odd = jnp.where(mask, pltpu.roll(x, 64, 1), y)
            first = pl.multiple_of(t * (2 * GPAD), 8)
            wide[half, pl.ds(first, GPAD), :] = even
            wide[half, pl.ds(first + GPAD, GPAD), :] = odd
        return carry

    lax.fori_loop(0, BV // 2, spread, 0, unroll=4)

    def bring(g, carry):
        for half in range(2):
            block = wide[half, pl.ds(g, BV, stride=GPAD), :]
            cg[g, :, half * 128 : half * 128 + 128] = block.astype(bf16)
        return carry

    lax.fori_loop(0, GROUPS, bring, 0, unroll=4)


    def gather(values, u_ref):
        first, second = split_pair(values)
        p_two[0:256, :] = first
        p_two[256:512, :] = second
        got = fold(jnp.dot(sel_t[...], p_two[...], preferred_element_type=f32))
        mask = low_lanes((GPAD, 128))
        u_ref[:, 0:128] = jnp.where(mask, got[0:GPAD], got[GPAD : 2 * GPAD])
        u_ref[:, 128:256] = jnp.where(mask, got[2 * GPAD : 3 * GPAD], got[3 * GPAD : 4 * GPAD])

    def forward(u_ref, exact):
        lanes = 128 if exact else 64

        def finish(g, acc, h, block):
            made = lax.dot_general(
                at[h, g], block, (((1,), (1,)), ((), ())), preferred_element_type=f32
            )
            acc = acc * keep[g] + made
            buf[h, g, :, 0:lanes] = acc
            return acc

        def first(g, acc):
            scaled = cg[g].astype(f32) * u_ref[pl.ds(g, 1), :]
            block = scaled.astype(bf16)
            if exact:
                low = (scaled - block.astype(f32)).astype(bf16)
                block = jnp.concatenate([block, low], axis=0)
            table[g, 0:lanes, :] = block
            return finish(g, acc, 0, block)

        def second(g, acc):
            return finish(g, acc, 1, table[g, 0:lanes, :])

        mask = low_lanes((HALF, 128))
        for h, step in ((0, first), (1, second)):
            lax.fori_loop(0, GROUPS, step, jnp.zeros((HALF, lanes), f32), unroll=19)
            for two in range(ROWS // 2):
                even = buf[h, last[2 * two]] * has[2 * two]
                odd = buf[h, last[2 * two + 1]] * has[2 * two + 1]
                if exact:
                    both = jnp.where(mask, fold(even), fold(odd))
                else:
                    both = jnp.where(mask, even, pltpu.roll(odd, 64, 1))
                part[h, 2 * two] = both[:PIECE]
                part[h, 2 * two + 1] = both[PIECE:]
            rs[h][0]()

    def summed(h):
        rs[h][1]()
        total = part[h, me_f]
        for off in range(1, NF):
            total = total + rs_in[h, lax.rem(me_f + off, NF)]
        return total

    def gather_residual(start):
        for h in range(2):
            r_all[h, me_f] = summed(h) - sig_own[h]
            pl.when(start)(ag[h][0])

    rs = half_copies(lambda h, p: part.at[h, p], rs_in, s_rs, r_rs)
    ag = half_copies(lambda h, p: r_all.at[h, me_f], r_all, s_ag, r_ag)
    start_fin, wait_fin = copies(lambda p: fin_out.at[p], fin_in, s_fin, r_fin)

    swap, along_y, back = [], [], []
    for h in range(2):
        landing = g_pair.at[h]
        swap.append(with_twin(g_part.at[1 - me_c, h], landing, landing, h))
        own, other = g_all.at[me_c, h], g_all.at[1 - me_c, h]
        back.append(with_twin(own, own, other, 2 + h))
        out, arrive = [], []
        for off in (2, 1, 3):
            y = lax.rem(me_y + off, SIDE)
            where = {"vox": y * 2 + me_c}
            own, other = g_in.at[h, me_y], g_in.at[h, y]
            out.append(remote(own, own, s_gr.at[h, y], r_gr.at[h, me_y], where))
            arrive.append(remote(own, other, s_gr.at[h, y], r_gr.at[h, y], where))
        along_y.append(pair(out, arrive))

    mine = me_y * NF + me_f
    out, arrive = [], []
    for off in CHIP_FAR_FIRST:
        y, f = lax.rem(me_y + off[0], SIDE), other_fas(off[1:])
        where = {"vox": y * 2 + me_c, "fas": f}
        chip = y * NF + f
        src = sc_in.at[mine, 0:1]
        out.append(remote(src, src, s_sc.at[chip], r_sc.at[mine], where))
        src = sc_in.at[chip, 0:1]
        arrive.append(remote(src, src, s_sc.at[chip], r_sc.at[chip], where))
    start_sc, wait_sc = pair(out, arrive)
    start_two, wait_two = with_twin(sc_pair.at[me_c], sc_pair.at[me_c], sc_pair.at[1 - me_c], 4)

    w_out[...] = w_in[...]
    gather(w_in[...], u_w)
    forward(u_w, True)
    wait_sig()
    sg_in[me_f] = sig_in[me_f // 2]
    for f in range(NF):
        for r in range(2):
            turn[r * 64 + f * 4 : r * 64 + f * 4 + 4, :] = sg_in[f, r * 4 : r * 4 + 4, :]
    turn[...] = jnp.transpose(turn[...])
    for h in range(2):
        first_row = pl.multiple_of(h * HALF + lax.rem(me_f, 2) * PIECE, 8)
        sig_own[h] = turn[pl.ds(first_row, PIECE), :]
    gather_residual(me_f >= 0)

    def backward(h):
        for two in range(ROWS // 2):
            x = jnp.concatenate([r_all[h, 2 * two], r_all[h, 2 * two + 1]], axis=0)
            even, odd = split_pair(x)
            r_two[h, 2 * two] = even
            r_two[h, 2 * two + 1] = odd

        def step(g, c):
            block = cg[g]
            twice = jnp.concatenate([block, block], axis=0)
            inner = jnp.dot(r_two[h, grow[g]], twice, preferred_element_type=f32)
            row = jnp.sum(inner * at[h, g].astype(f32), axis=0, keepdims=True)
            contrib[pl.ds(g, 1), :] = row if h == 0 else contrib[pl.ds(g, 1), :] + row
            return c

        lax.fori_loop(0, GROUPS, step, 0, unroll=19)

    def sweep(turns, carry):
        for h in range(2):
            ag[h][1]()
            backward(h)
        for half in range(2):
            first, second = split_pair(contrib[:, half * 128 : (half + 1) * 128])
            b_two[2 * half * GPAD : (2 * half + 1) * GPAD, :] = first
            b_two[(2 * half + 1) * GPAD : (2 * half + 2) * GPAD, :] = second
        got = fold(jnp.dot(sel[...], b_two[...], preferred_element_type=f32))
        mask = low_lanes((256, 128))
        g_part[...] = jnp.where(mask, got[0:256], got[256:512]).reshape(2, 2, 64, 128)
        for h in range(2):
            swap[h][0]()
        for h in range(2):
            swap[h][1]()
            g_in[h, me_y] = g_part[me_c, h] + g_pair[h]
            along_y[h][0]()
        for h in range(2):
            along_y[h][1]()
            g_all[me_c, h] = (g_in[h, 0] + g_in[h, 1]) + (g_in[h, 2] + g_in[h, 3])
            back[h][0]()
        for h in range(2):
            back[h][1]()
        weights = w_out[...]
        gradient = g_all[...].reshape(256, 128)
        projected = jnp.where((weights > 0) | (gradient < 0), gradient, 0.0)
        gather(projected, u_p)
        forward(u_p, False)
        steep = jnp.sum((projected * projected).reshape(32, 8, 128), axis=0)
        steep = jnp.sum(fold(steep), axis=0, keepdims=True)
        squares = jnp.zeros((8, 128), f32)
        for h in range(2):
            image = summed(h)
            squares = squares + jnp.sum((image * image).reshape(PIECE // 8, 8, 128), axis=0)
        squares = jnp.sum(fold(squares), axis=0, keepdims=True)
        sc_in[mine, 0:1, :] = jnp.where(low_lanes((1, 128)), squares, steep)
        start_sc()
        wait_sc()
        sums = jnp.sum(sc_in[:, 0, :], axis=0, keepdims=True)
        sc_pair[me_c] = jnp.broadcast_to(sums, (8, 128))
        start_two()
        wait_two()
        both = sc_pair[0, 0:1, :] + sc_pair[1, 0:1, :]
        mask = low_lanes((1, 128))
        image_sq = jnp.sum(jnp.where(mask, both, 0.0), axis=(0, 1), keepdims=True)
        grad_sq = jnp.sum(jnp.where(mask, 0.0, both), axis=(0, 1), keepdims=True) * (1.0 / NV)
        size = grad_sq / (image_sq + 1e-06)
        w_out[...] = jnp.maximum(weights - size * projected, 0.0)
        u_w[...] = jnp.maximum(u_w[...] - size * u_p[...], 0.0)
        forward(u_w, True)
        gather_residual(turns < ITERS - 1)
        return carry

    lax.fori_loop(0, ITERS, sweep, 0)

    turn[0:PIECE, :] = r_all[0, me_f]
    turn[PIECE:HALF, :] = r_all[1, me_f]
    turn[HALF:, :] = jnp.zeros((128 - HALF, 128), f32)
    turn[...] = jnp.transpose(turn[...])
    for f in range(NF):
        for r in range(2):
            fin_out[f, r * 4 : r * 4 + 4, :] = turn[r * 64 + f * 4 : r * 64 + f * 4 + 4, :]
    start_fin()
    wait_fin()
    fin_in[me_f] = fin_out[me_f]
    res_out[...] = fin_in[...]


def local(
    signal,
    initial_weights,
    coefficients,
    block_rows,
    block_cols,
    block_atoms,
    block_count,
    dictionary,
):
    i32 = jnp.int32
    rows = block_rows - lax.axis_index("vox") * ROWS
    cols = block_cols - lax.axis_index("fas") * COLS
    slots = jnp.arange(SLOTS, dtype=i32)
    lives = slots < block_count[0]
    hot = (rows[:, None] == jnp.arange(ROWS, dtype=i32)[None, :]) & lives[:, None]
    before = (slots[None, :] < slots[:, None]) & lives[None, :] & (rows[None, :] == rows[:, None])
    rank = jnp.sum(before.astype(i32), axis=1)
    count = jnp.sum(hot.astype(i32), axis=0)
    groups = (count + QUAD - 1) // QUAD
    span = jnp.arange(ROWS, dtype=i32)
    ends = jnp.sum(jnp.where(span[None, :] <= span[:, None], groups[None, :], 0), axis=1)
    firsts = ends - groups
    place = jnp.where(
        lives, jnp.sum(jnp.where(hot, firsts[None, :], 0), axis=1) * QUAD + rank, -1
    )
    turns = jnp.arange(GPAD, dtype=i32)
    grow = jnp.minimum(jnp.sum((ends[None, :] <= turns[:, None]).astype(i32), axis=1), ROWS - 1)
    is_first = jnp.any((firsts[None, :] == turns[:, None]) & (groups[None, :] > 0), axis=1)
    keep = 1.0 - is_first.astype(f32)
    last = jnp.maximum(ends - 1, 0)
    has = (groups > 0).astype(f32)
    upper = (block_atoms >= 256).astype(i32)
    digits = jnp.concatenate([block_atoms - 256 * upper, upper], axis=1).astype(bf16)
    dict_t = jnp.pad(dictionary.T, ((0, 0), (0, ATOMPAD - ATOMS)))
    w_in = initial_weights.reshape(2, 256, BF)
    w_in = jnp.concatenate([w_in[0], w_in[1]], axis=1)
    sig_in = jnp.pad(signal.reshape(8, 8, DIRS), ((0, 0), (0, 0), (0, 128 - DIRS)))

    smem = pl.BlockSpec(memory_space=pltpu.SMEM)
    vmem = pl.BlockSpec(memory_space=pltpu.VMEM)
    dma = pltpu.SemaphoreType.DMA
    w_new, res = pl.pallas_call(
        kernel,
        out_shape=(
            jax.ShapeDtypeStruct((256, 128), f32),
            jax.ShapeDtypeStruct((NF, 8, 128), f32),
        ),
        in_specs=[smem] * 4 + [pl.BlockSpec(memory_space=pl.ANY)] + [vmem] * 7,
        out_specs=(vmem, vmem),
        scratch_shapes=[
            pltpu.VMEM((SLOTS, BV * BF), bf16),
            pltpu.VMEM((2, BV * GPAD, 128), f32),
            pltpu.VMEM((SPAD, SLOTS), bf16),
            pltpu.VMEM((GPAD, 256), f32),
            pltpu.VMEM((GROUPS, BV, 256), bf16),
            pltpu.VMEM((2, GROUPS, HALF, 256), bf16),
            pltpu.VMEM((COLS, SPAD), bf16),
            pltpu.VMEM((SPAD, COLS), bf16),
            pltpu.VMEM((GPAD, 256), f32),
            pltpu.VMEM((GPAD, 256), f32),
            pltpu.VMEM((GROUPS, 128, 256), bf16),
            pltpu.VMEM((2, GROUPS, HALF, 128), f32),
            pltpu.VMEM((2, NF, PIECE, 128), f32),
            pltpu.VMEM((2, NF, PIECE, 128), f32),
            pltpu.VMEM((2, NF, PIECE, 128), f32),
            pltpu.VMEM((2, ROWS, HALF, 128), bf16),
            pltpu.VMEM((GPAD, 256), f32),
            pltpu.VMEM((SPAD, 128), bf16),
            pltpu.VMEM((2, 2, 64, 128), f32),
            pltpu.VMEM((2, 64, 128), f32),
            pltpu.VMEM((2, SIDE, 64, 128), f32),
            pltpu.VMEM((2, 2, 64, 128), f32),
            pltpu.VMEM((COLS, 128), bf16),
            pltpu.VMEM((CHIPS, 8, 128), f32),
            pltpu.VMEM((2, 8, 128), f32),
            pltpu.VMEM((NF, 8, 128), f32),
            pltpu.VMEM((128, 128), f32),
            pltpu.VMEM((2, PIECE, 128), f32),
            pltpu.VMEM((NF, 8, 128), f32),
            pltpu.VMEM((NF, 8, 128), f32),
        ]
        + [
            dma(n)
            for n in ((NF,), (2, NF), (2, NF), (2, SIDE), (CHIPS,), (NF,), (5,))
            for _ in range(2)
        ]
        + [dma(())],
        compiler_params=pltpu.CompilerParams(
            collective_id=0, has_side_effects=True, vmem_limit_bytes=52 * 1024 * 1024
        ),
    )(
        grow,
        last,
        keep,
        has,
        coefficients,
        digits,
        dict_t,
        place[None, :],
        cols[None, :],
        cols[:, None],
        w_in,
        sig_in,
    )
    weights = jnp.concatenate([w_new[:, :BF], w_new[:, BF:]], axis=0).reshape(-1)
    res = res[:, :, :HALF].reshape(8, 2, 8, 2, PIECE).transpose(0, 2, 3, 1, 4)
    return (weights, res.reshape(ROWS, 4 * DIRS))


def solution(mesh):
    placed = (
        P("vox", "fas"),
        P("fas"),
        P(("vox", "fas"), None),
        P(("vox", "fas")),
        P(("vox", "fas")),
        P(("vox", "fas"), None),
        P(("vox", "fas")),
        P(),
    )
    return jax.shard_map(
        local, mesh=mesh, in_specs=placed, out_specs=(P("fas"), P("vox", "fas")), check_vma=False
    )
```

```python
import jax
import jax.numpy as jnp
from jax import lax
from jax.experimental import pallas as pl
from jax.experimental.pallas import tpu as pltpu
from jax.sharding import PartitionSpec as P

BV = 64
BF = 64
DIRS = 96
ATOMS = 360
ITERS = 5
SLOTS = 256
ROWS = 16
COLS = 512
NV = 8
NF = 16
SIDE = 4
CHIPS = 64
QUAD = 4
GROUPS = (SLOTS + (QUAD - 1) * ROWS) // QUAD
GPAD = 80
SPAD = 384
ATOMPAD = 384
HALF = DIRS // 2
PIECE = HALF // 2


def hops(off):
    return sum(min(d, SIDE - d) for d in off)


CHIP_FAR_FIRST = sorted(
    [(y, z, x) for y in range(SIDE) for z in range(SIDE) for x in range(SIDE) if y + z + x],
    key=lambda off: (-hops(off), off),
)
FAR_FIRST = [off[1:] for off in CHIP_FAR_FIRST if off[0] == 0]

f32 = jnp.float32
bf16 = jnp.bfloat16


def low_lanes(shape):
    return lax.broadcasted_iota(jnp.int32, shape, len(shape) - 1) < 64


def split_pair(x):
    h = x.astype(bf16).astype(f32)
    low = x - h
    mask = low_lanes(x.shape)
    first = jnp.where(mask, h, pltpu.roll(low, 64, 1))
    second = jnp.where(mask, pltpu.roll(h, 64, 1), low)
    return first.astype(bf16), second.astype(bf16)


def fold(x):
    return x + pltpu.roll(x, 64, 1)


def kernel(
    grow,
    last,
    keep,
    has,
    coef_hbm,
    digits,
    dict_t,
    place_lane,
    cols_lane,
    cols_sub,
    w_in,
    sig_in,
    w_out,
    res_out,
    coef,
    wide,
    pick,
    names,
    cg,
    at,
    sel,
    sel_t,
    u_p,
    u_w,
    table,
    buf,
    part,
    rs_in,
    r_all,
    r_two,
    contrib,
    b_two,
    g_part,
    g_pair,
    g_in,
    g_all,
    p_two,
    sc_in,
    sc_pair,
    sg_in,
    turn,
    sig_own,
    fin_out,
    fin_in,
    s_sig,
    r_sig,
    s_rs,
    r_rs,
    s_ag,
    r_ag,
    s_gr,
    r_gr,
    s_sc,
    r_sc,
    s_fin,
    r_fin,
    s_two,
    r_twin,
    s_coef,
):
    me_v = lax.axis_index("vox")
    me_f = lax.axis_index("fas")
    me_c = lax.rem(me_v, 2)
    me_y = me_v // 2
    twin = me_v + 1 - 2 * me_c
    fetch = pltpu.make_async_copy(coef_hbm, coef, s_coef)
    fetch.start()

    def remote(src, dst, send_sem, recv_sem, device):
        return pltpu.make_async_remote_copy(
            src_ref=src,
            dst_ref=dst,
            send_sem=send_sem,
            recv_sem=recv_sem,
            device_id=device,
            device_id_type=pl.DeviceIdType.MESH,
        )

    def pair(out, arrive):
        def start():
            for c in out:
                c.start()

        def wait():
            for c in arrive:
                c.wait_recv()
            for c in out:
                c.wait_send()

        return start, wait

    def copies(src_at, dst, send_sem, recv_sem):
        out, arrive = [], []
        for off in FAR_FIRST:
            peer = other_fas(off)
            where = {"fas": peer}
            out.append(
                remote(src_at(peer), dst.at[me_f], send_sem.at[peer], recv_sem.at[me_f], where)
            )
            arrive.append(
                remote(src_at(peer), dst.at[peer], send_sem.at[peer], recv_sem.at[peer], where)
            )
        return pair(out, arrive)

    def half_copies(src_at, dst, send_sem, recv_sem):
        return [
            copies(lambda p: src_at(h, p), dst.at[h], send_sem.at[h], recv_sem.at[h])
            for h in range(2)
        ]

    def other_fas(off):
        return lax.rem(me_f // SIDE + off[0], SIDE) * SIDE + lax.rem(me_f + off[1], SIDE)

    def with_twin(src, dst, landing, index):
        sems, where = (s_two.at[index], r_twin.at[index]), {"vox": twin}
        return pair([remote(src, dst, *sems, where)], [remote(src, landing, *sems, where)])

    barrier = pltpu.get_barrier_semaphore()
    pl.semaphore_signal(
        barrier, inc=1, device_id={"vox": twin}, device_id_type=pl.DeviceIdType.MESH
    )
    for off in CHIP_FAR_FIRST:
        pl.semaphore_signal(
            barrier,
            inc=1,
            device_id={"vox": lax.rem(me_y + off[0], SIDE) * 2 + me_c, "fas": other_fas(off[1:])},
            device_id_type=pl.DeviceIdType.MESH,
        )

    turn_row = lax.broadcasted_iota(jnp.int32, (GPAD, SLOTS), 0) * QUAD
    for q in range(QUAD):
        hot = (place_lane[...] == turn_row + q).astype(f32).astype(bf16)
        pick[q * GPAD : (q + 1) * GPAD, :] = hot
    pick[QUAD * GPAD :, :] = jnp.zeros((SPAD - QUAD * GPAD, SLOTS), bf16)
    found = jnp.dot(pick[0 : QUAD * GPAD, :], digits[...], preferred_element_type=f32)
    found = jnp.where(low_lanes(found.shape), found, found * 256.0)
    found = fold(found)
    mask = low_lanes((GPAD, 128))
    names[:, 0:128] = jnp.where(mask, found[0:GPAD], found[GPAD : 2 * GPAD])
    names[:, 128:256] = jnp.where(mask, found[2 * GPAD : 3 * GPAD], found[3 * GPAD :])

    def name_atoms(g, carry):
        row = names[pl.ds(g, 1), :].astype(jnp.int32)
        hot = (lax.broadcasted_iota(jnp.int32, (ATOMPAD, 256), 0) == row).astype(f32).astype(bf16)
        made = jnp.dot(dict_t[...], hot, preferred_element_type=f32).astype(bf16)
        at[0, g] = made[:HALF]
        at[1, g] = made[HALF:]
        return carry

    lax.fori_loop(0, GROUPS, name_atoms, 0, unroll=4)
    where_col = (lax.broadcasted_iota(jnp.int32, (COLS, SLOTS), 0) == cols_lane[...]).astype(f32)
    sel[...] = lax.dot_general(
        where_col.astype(bf16), pick[...], (((1,), (1,)), ((), ())), preferred_element_type=f32
    ).astype(bf16)
    where_col = (lax.broadcasted_iota(jnp.int32, (SLOTS, COLS), 1) == cols_sub[...]).astype(f32)
    sel_t[...] = jnp.dot(
        pick[...], where_col.astype(bf16), preferred_element_type=f32
    ).astype(bf16)
    contrib[...] = jnp.zeros_like(contrib)
    b_two[...] = jnp.zeros_like(b_two)

    pl.semaphore_wait(barrier, CHIPS)
    start_sig, wait_sig = copies(lambda p: sig_in.at[p // 2], sg_in, s_sig, r_sig)
    start_sig()

    fetch.wait()

    def spread(t, carry):
        at_lane = pl.multiple_of(t * 128, 128)
        moved = jnp.dot(pick[0 : QUAD * GPAD, :], coef[:, pl.ds(at_lane, 128)], preferred_element_type=f32)
        mask = low_lanes((GPAD, 128))
        for half in range(2):
            x = moved[2 * half * GPAD : (2 * half + 1) * GPAD]
            y = moved[(2 * half + 1) * GPAD : (2 * half + 2) * GPAD]
            lanes = slice(half * 128, half * 128 + 128)
            even = jnp.where(mask, x, pltpu.roll(y, 64, 1))
            odd = jnp.where(mask, pltpu.roll(x, 64, 1), y)
            first = pl.multiple_of(t * (2 * GPAD), 8)
            wide[half, pl.ds(first, GPAD), :] = even
            wide[half, pl.ds(first + GPAD, GPAD), :] = odd
        return carry

    lax.fori_loop(0, BV // 2, spread, 0, unroll=4)

    def bring(g, carry):
        for half in range(2):
            block = wide[half, pl.ds(g, BV, stride=GPAD), :]
            cg[g, :, half * 128 : half * 128 + 128] = block.astype(bf16)
        return carry

    lax.fori_loop(0, GROUPS, bring, 0, unroll=4)


    def gather(values, u_ref):
        first, second = split_pair(values)
        p_two[0:256, :] = first
        p_two[256:512, :] = second
        got = fold(jnp.dot(sel_t[...], p_two[...], preferred_element_type=f32))
        mask = low_lanes((GPAD, 128))
        u_ref[:, 0:128] = jnp.where(mask, got[0:GPAD], got[GPAD : 2 * GPAD])
        u_ref[:, 128:256] = jnp.where(mask, got[2 * GPAD : 3 * GPAD], got[3 * GPAD : 4 * GPAD])

    def forward(u_ref, exact):
        lanes = 128 if exact else 64

        def finish(g, acc, h, block):
            made = lax.dot_general(
                at[h, g], block, (((1,), (1,)), ((), ())), preferred_element_type=f32
            )
            acc = acc * keep[g] + made
            buf[h, g, :, 0:lanes] = acc
            return acc

        def first(g, acc):
            scaled = cg[g].astype(f32) * u_ref[pl.ds(g, 1), :]
            block = scaled.astype(bf16)
            if exact:
                low = (scaled - block.astype(f32)).astype(bf16)
                block = jnp.concatenate([block, low], axis=0)
            table[g, 0:lanes, :] = block
            return finish(g, acc, 0, block)

        def second(g, acc):
            return finish(g, acc, 1, table[g, 0:lanes, :])

        mask = low_lanes((HALF, 128))
        for h, step in ((0, first), (1, second)):
            lax.fori_loop(0, GROUPS, step, jnp.zeros((HALF, lanes), f32), unroll=76)
            for two in range(ROWS // 2):
                even = buf[h, last[2 * two]] * has[2 * two]
                odd = buf[h, last[2 * two + 1]] * has[2 * two + 1]
                if exact:
                    both = jnp.where(mask, fold(even), fold(odd))
                else:
                    both = jnp.where(mask, even, pltpu.roll(odd, 64, 1))
                part[h, 2 * two] = both[:PIECE]
                part[h, 2 * two + 1] = both[PIECE:]
            rs[h][0]()

    def summed(h):
        rs[h][1]()
        total = part[h, me_f]
        for off in range(1, NF):
            total = total + rs_in[h, lax.rem(me_f + off, NF)]
        return total

    def gather_residual(start):
        for h in range(2):
            r_all[h, me_f] = summed(h) - sig_own[h]
            pl.when(start)(ag[h][0])

    rs = half_copies(lambda h, p: part.at[h, p], rs_in, s_rs, r_rs)
    ag = half_copies(lambda h, p: r_all.at[h, me_f], r_all, s_ag, r_ag)
    start_fin, wait_fin = copies(lambda p: fin_out.at[p], fin_in, s_fin, r_fin)

    swap, along_y, back = [], [], []
    for h in range(2):
        landing = g_pair.at[h]
        swap.append(with_twin(g_part.at[1 - me_c, h], landing, landing, h))
        own, other = g_all.at[me_c, h], g_all.at[1 - me_c, h]
        back.append(with_twin(own, own, other, 2 + h))
        out, arrive = [], []
        for off in (2, 1, 3):
            y = lax.rem(me_y + off, SIDE)
            where = {"vox": y * 2 + me_c}
            own, other = g_in.at[h, me_y], g_in.at[h, y]
            out.append(remote(own, own, s_gr.at[h, y], r_gr.at[h, me_y], where))
            arrive.append(remote(own, other, s_gr.at[h, y], r_gr.at[h, y], where))
        along_y.append(pair(out, arrive))

    mine = me_y * NF + me_f
    out, arrive = [], []
    for off in CHIP_FAR_FIRST:
        y, f = lax.rem(me_y + off[0], SIDE), other_fas(off[1:])
        where = {"vox": y * 2 + me_c, "fas": f}
        chip = y * NF + f
        src = sc_in.at[mine, 0:1]
        out.append(remote(src, src, s_sc.at[chip], r_sc.at[mine], where))
        src = sc_in.at[chip, 0:1]
        arrive.append(remote(src, src, s_sc.at[chip], r_sc.at[chip], where))
    start_sc, wait_sc = pair(out, arrive)
    start_two, wait_two = with_twin(sc_pair.at[me_c], sc_pair.at[me_c], sc_pair.at[1 - me_c], 4)

    w_out[...] = w_in[...]
    gather(w_in[...], u_w)
    forward(u_w, True)
    wait_sig()
    sg_in[me_f] = sig_in[me_f // 2]
    for f in range(NF):
        for r in range(2):
            turn[r * 64 + f * 4 : r * 64 + f * 4 + 4, :] = sg_in[f, r * 4 : r * 4 + 4, :]
    turn[...] = jnp.transpose(turn[...])
    for h in range(2):
        first_row = pl.multiple_of(h * HALF + lax.rem(me_f, 2) * PIECE, 8)
        sig_own[h] = turn[pl.ds(first_row, PIECE), :]
    gather_residual(me_f >= 0)

    def backward(h):
        for two in range(ROWS // 2):
            x = jnp.concatenate([r_all[h, 2 * two], r_all[h, 2 * two + 1]], axis=0)
            even, odd = split_pair(x)
            r_two[h, 2 * two] = even
            r_two[h, 2 * two + 1] = odd

        def step(g, c):
            block = cg[g]
            twice = jnp.concatenate([block, block], axis=0)
            inner = jnp.dot(r_two[h, grow[g]], twice, preferred_element_type=f32)
            row = jnp.sum(inner * at[h, g].astype(f32), axis=0, keepdims=True)
            contrib[pl.ds(g, 1), :] = row if h == 0 else contrib[pl.ds(g, 1), :] + row
            return c

        lax.fori_loop(0, GROUPS, step, 0, unroll=76)

    def sweep(turns, carry):
        for h in range(2):
            ag[h][1]()
            backward(h)
        for half in range(2):
            first, second = split_pair(contrib[:, half * 128 : (half + 1) * 128])
            b_two[2 * half * GPAD : (2 * half + 1) * GPAD, :] = first
            b_two[(2 * half + 1) * GPAD : (2 * half + 2) * GPAD, :] = second
        got = fold(jnp.dot(sel[...], b_two[...], preferred_element_type=f32))
        mask = low_lanes((256, 128))
        g_part[...] = jnp.where(mask, got[0:256], got[256:512]).reshape(2, 2, 64, 128)
        for h in range(2):
            swap[h][0]()
        for h in range(2):
            swap[h][1]()
            g_in[h, me_y] = g_part[me_c, h] + g_pair[h]
            along_y[h][0]()
        for h in range(2):
            along_y[h][1]()
            g_all[me_c, h] = (g_in[h, 0] + g_in[h, 1]) + (g_in[h, 2] + g_in[h, 3])
            back[h][0]()
        for h in range(2):
            back[h][1]()
        weights = w_out[...]
        gradient = g_all[...].reshape(256, 128)
        projected = jnp.where((weights > 0) | (gradient < 0), gradient, 0.0)
        gather(projected, u_p)
        forward(u_p, False)
        steep = jnp.sum((projected * projected).reshape(32, 8, 128), axis=0)
        steep = jnp.sum(fold(steep), axis=0, keepdims=True)
        squares = jnp.zeros((8, 128), f32)
        for h in range(2):
            image = summed(h)
            squares = squares + jnp.sum((image * image).reshape(PIECE // 8, 8, 128), axis=0)
        squares = jnp.sum(fold(squares), axis=0, keepdims=True)
        sc_in[mine, 0:1, :] = jnp.where(low_lanes((1, 128)), squares, steep)
        start_sc()
        wait_sc()
        sums = jnp.sum(sc_in[:, 0, :], axis=0, keepdims=True)
        sc_pair[me_c] = jnp.broadcast_to(sums, (8, 128))
        start_two()
        wait_two()
        both = sc_pair[0, 0:1, :] + sc_pair[1, 0:1, :]
        mask = low_lanes((1, 128))
        image_sq = jnp.sum(jnp.where(mask, both, 0.0), axis=(0, 1), keepdims=True)
        grad_sq = jnp.sum(jnp.where(mask, 0.0, both), axis=(0, 1), keepdims=True) * (1.0 / NV)
        size = grad_sq / (image_sq + 1e-06)
        w_out[...] = jnp.maximum(weights - size * projected, 0.0)
        u_w[...] = jnp.maximum(u_w[...] - size * u_p[...], 0.0)
        forward(u_w, True)
        gather_residual(turns < ITERS - 1)
        return carry

    lax.fori_loop(0, ITERS, sweep, 0)

    turn[0:PIECE, :] = r_all[0, me_f]
    turn[PIECE:HALF, :] = r_all[1, me_f]
    turn[HALF:, :] = jnp.zeros((128 - HALF, 128), f32)
    turn[...] = jnp.transpose(turn[...])
    for f in range(NF):
        for r in range(2):
            fin_out[f, r * 4 : r * 4 + 4, :] = turn[r * 64 + f * 4 : r * 64 + f * 4 + 4, :]
    start_fin()
    wait_fin()
    fin_in[me_f] = fin_out[me_f]
    res_out[...] = fin_in[...]


def local(
    signal,
    initial_weights,
    coefficients,
    block_rows,
    block_cols,
    block_atoms,
    block_count,
    dictionary,
):
    i32 = jnp.int32
    rows = block_rows - lax.axis_index("vox") * ROWS
    cols = block_cols - lax.axis_index("fas") * COLS
    slots = jnp.arange(SLOTS, dtype=i32)
    lives = slots < block_count[0]
    hot = (rows[:, None] == jnp.arange(ROWS, dtype=i32)[None, :]) & lives[:, None]
    before = (slots[None, :] < slots[:, None]) & lives[None, :] & (rows[None, :] == rows[:, None])
    rank = jnp.sum(before.astype(i32), axis=1)
    count = jnp.sum(hot.astype(i32), axis=0)
    groups = (count + QUAD - 1) // QUAD
    span = jnp.arange(ROWS, dtype=i32)
    ends = jnp.sum(jnp.where(span[None, :] <= span[:, None], groups[None, :], 0), axis=1)
    firsts = ends - groups
    place = jnp.where(
        lives, jnp.sum(jnp.where(hot, firsts[None, :], 0), axis=1) * QUAD + rank, -1
    )
    turns = jnp.arange(GPAD, dtype=i32)
    grow = jnp.minimum(jnp.sum((ends[None, :] <= turns[:, None]).astype(i32), axis=1), ROWS - 1)
    is_first = jnp.any((firsts[None, :] == turns[:, None]) & (groups[None, :] > 0), axis=1)
    keep = 1.0 - is_first.astype(f32)
    last = jnp.maximum(ends - 1, 0)
    has = (groups > 0).astype(f32)
    upper = (block_atoms >= 256).astype(i32)
    digits = jnp.concatenate([block_atoms - 256 * upper, upper], axis=1).astype(bf16)
    dict_t = jnp.pad(dictionary.T, ((0, 0), (0, ATOMPAD - ATOMS)))
    w_in = initial_weights.reshape(2, 256, BF)
    w_in = jnp.concatenate([w_in[0], w_in[1]], axis=1)
    sig_in = jnp.pad(signal.reshape(8, 8, DIRS), ((0, 0), (0, 0), (0, 128 - DIRS)))

    smem = pl.BlockSpec(memory_space=pltpu.SMEM)
    vmem = pl.BlockSpec(memory_space=pltpu.VMEM)
    dma = pltpu.SemaphoreType.DMA
    w_new, res = pl.pallas_call(
        kernel,
        out_shape=(
            jax.ShapeDtypeStruct((256, 128), f32),
            jax.ShapeDtypeStruct((NF, 8, 128), f32),
        ),
        in_specs=[smem] * 4 + [pl.BlockSpec(memory_space=pl.ANY)] + [vmem] * 7,
        out_specs=(vmem, vmem),
        scratch_shapes=[
            pltpu.VMEM((SLOTS, BV * BF), bf16),
            pltpu.VMEM((2, BV * GPAD, 128), f32),
            pltpu.VMEM((SPAD, SLOTS), bf16),
            pltpu.VMEM((GPAD, 256), f32),
            pltpu.VMEM((GROUPS, BV, 256), bf16),
            pltpu.VMEM((2, GROUPS, HALF, 256), bf16),
            pltpu.VMEM((COLS, SPAD), bf16),
            pltpu.VMEM((SPAD, COLS), bf16),
            pltpu.VMEM((GPAD, 256), f32),
            pltpu.VMEM((GPAD, 256), f32),
            pltpu.VMEM((GROUPS, 128, 256), bf16),
            pltpu.VMEM((2, GROUPS, HALF, 128), f32),
            pltpu.VMEM((2, NF, PIECE, 128), f32),
            pltpu.VMEM((2, NF, PIECE, 128), f32),
            pltpu.VMEM((2, NF, PIECE, 128), f32),
            pltpu.VMEM((2, ROWS, HALF, 128), bf16),
            pltpu.VMEM((GPAD, 256), f32),
            pltpu.VMEM((SPAD, 128), bf16),
            pltpu.VMEM((2, 2, 64, 128), f32),
            pltpu.VMEM((2, 64, 128), f32),
            pltpu.VMEM((2, SIDE, 64, 128), f32),
            pltpu.VMEM((2, 2, 64, 128), f32),
            pltpu.VMEM((COLS, 128), bf16),
            pltpu.VMEM((CHIPS, 8, 128), f32),
            pltpu.VMEM((2, 8, 128), f32),
            pltpu.VMEM((NF, 8, 128), f32),
            pltpu.VMEM((128, 128), f32),
            pltpu.VMEM((2, PIECE, 128), f32),
            pltpu.VMEM((NF, 8, 128), f32),
            pltpu.VMEM((NF, 8, 128), f32),
        ]
        + [
            dma(n)
            for n in ((NF,), (2, NF), (2, NF), (2, SIDE), (CHIPS,), (NF,), (5,))
            for _ in range(2)
        ]
        + [dma(())],
        compiler_params=pltpu.CompilerParams(
            collective_id=0, has_side_effects=True, vmem_limit_bytes=52 * 1024 * 1024
        ),
    )(
        grow,
        last,
        keep,
        has,
        coefficients,
        digits,
        dict_t,
        place[None, :],
        cols[None, :],
        cols[:, None],
        w_in,
        sig_in,
    )
    weights = jnp.concatenate([w_new[:, :BF], w_new[:, BF:]], axis=0).reshape(-1)
    res = res[:, :, :HALF].reshape(8, 2, 8, 2, PIECE).transpose(0, 2, 3, 1, 4)
    return (weights, res.reshape(ROWS, 4 * DIRS))


def solution(mesh):
    placed = (
        P("vox", "fas"),
        P("fas"),
        P(("vox", "fas"), None),
        P(("vox", "fas")),
        P(("vox", "fas")),
        P(("vox", "fas"), None),
        P(("vox", "fas")),
        P(),
    )
    return jax.shard_map(
        local, mesh=mesh, in_specs=placed, out_specs=(P("fas"), P("vox", "fas")), check_vma=False
    )
```

```python
import jax
import jax.numpy as jnp
from jax import lax
from jax.experimental import pallas as pl
from jax.experimental.pallas import tpu as pltpu
from jax.sharding import PartitionSpec as P

BV = 64
BF = 64
DIRS = 96
ATOMS = 360
ITERS = 5
SLOTS = 256
ROWS = 16
COLS = 512
NV = 8
NF = 16
SIDE = 4
CHIPS = 64
QUAD = 4
GROUPS = (SLOTS + (QUAD - 1) * ROWS) // QUAD
GPAD = 80
SPAD = 384
ATOMPAD = 384
HALF = DIRS // 2
PIECE = HALF // 2


def hops(off):
    return sum(min(d, SIDE - d) for d in off)


CHIP_FAR_FIRST = sorted(
    [(y, z, x) for y in range(SIDE) for z in range(SIDE) for x in range(SIDE) if y + z + x],
    key=lambda off: (-hops(off), off),
)
FAR_FIRST = [off[1:] for off in CHIP_FAR_FIRST if off[0] == 0]

f32 = jnp.float32
bf16 = jnp.bfloat16


def low_lanes(shape):
    return lax.broadcasted_iota(jnp.int32, shape, len(shape) - 1) < 64


def split_pair(x):
    h = x.astype(bf16).astype(f32)
    low = x - h
    mask = low_lanes(x.shape)
    first = jnp.where(mask, h, pltpu.roll(low, 64, 1))
    second = jnp.where(mask, pltpu.roll(h, 64, 1), low)
    return first.astype(bf16), second.astype(bf16)


def fold(x):
    return x + pltpu.roll(x, 64, 1)


def kernel(
    grow,
    last,
    keep,
    has,
    coef_hbm,
    digits,
    dict_t,
    place_lane,
    cols_lane,
    cols_sub,
    w_in,
    sig_in,
    w_out,
    res_out,
    coef,
    wide,
    pick,
    names,
    cg,
    at,
    sel,
    sel_t,
    u_p,
    u_w,
    table,
    buf,
    part,
    rs_in,
    r_all,
    r_two,
    contrib,
    b_two,
    g_part,
    g_pair,
    g_in,
    g_all,
    p_two,
    sc_in,
    sc_pair,
    sg_in,
    turn,
    sig_own,
    fin_out,
    fin_in,
    s_sig,
    r_sig,
    s_rs,
    r_rs,
    s_ag,
    r_ag,
    s_gr,
    r_gr,
    s_sc,
    r_sc,
    s_fin,
    r_fin,
    s_two,
    r_twin,
    s_coef,
):
    me_v = lax.axis_index("vox")
    me_f = lax.axis_index("fas")
    me_c = lax.rem(me_v, 2)
    me_y = me_v // 2
    twin = me_v + 1 - 2 * me_c
    fetch = pltpu.make_async_copy(coef_hbm, coef, s_coef)
    fetch.start()

    def remote(src, dst, send_sem, recv_sem, device):
        return pltpu.make_async_remote_copy(
            src_ref=src,
            dst_ref=dst,
            send_sem=send_sem,
            recv_sem=recv_sem,
            device_id=device,
            device_id_type=pl.DeviceIdType.MESH,
        )

    def pair(out, arrive):
        def start():
            for c in out:
                c.start()

        def wait():
            for c in reversed(arrive):
                c.wait_recv()

        def sent():
            for c in reversed(out):
                c.wait_send()

        return start, wait, sent

    def copies(src_at, dst, send_sem, recv_sem):
        out, arrive = [], []
        for off in FAR_FIRST:
            peer = other_fas(off)
            where = {"fas": peer}
            out.append(
                remote(src_at(peer), dst.at[me_f], send_sem.at[peer], recv_sem.at[me_f], where)
            )
            arrive.append(
                remote(src_at(peer), dst.at[peer], send_sem.at[peer], recv_sem.at[peer], where)
            )
        return pair(out, arrive)

    def half_copies(src_at, dst, send_sem, recv_sem):
        return [
            copies(lambda p: src_at(h, p), dst.at[h], send_sem.at[h], recv_sem.at[h])
            for h in range(2)
        ]

    def other_fas(off):
        return lax.rem(me_f // SIDE + off[0], SIDE) * SIDE + lax.rem(me_f + off[1], SIDE)

    def with_twin(src, dst, landing, index):
        sems, where = (s_two.at[index], r_twin.at[index]), {"vox": twin}
        return pair([remote(src, dst, *sems, where)], [remote(src, landing, *sems, where)])

    barrier = pltpu.get_barrier_semaphore()
    pl.semaphore_signal(
        barrier, inc=1, device_id={"vox": twin}, device_id_type=pl.DeviceIdType.MESH
    )
    for off in CHIP_FAR_FIRST:
        pl.semaphore_signal(
            barrier,
            inc=1,
            device_id={"vox": lax.rem(me_y + off[0], SIDE) * 2 + me_c, "fas": other_fas(off[1:])},
            device_id_type=pl.DeviceIdType.MESH,
        )

    turn_row = lax.broadcasted_iota(jnp.int32, (GPAD, SLOTS), 0) * QUAD
    for q in range(QUAD):
        hot = (place_lane[...] == turn_row + q).astype(f32).astype(bf16)
        pick[q * GPAD : (q + 1) * GPAD, :] = hot
    pick[QUAD * GPAD :, :] = jnp.zeros((SPAD - QUAD * GPAD, SLOTS), bf16)
    found = jnp.dot(pick[0 : QUAD * GPAD, :], digits[...], preferred_element_type=f32)
    found = jnp.where(low_lanes(found.shape), found, found * 256.0)
    found = fold(found)
    mask = low_lanes((GPAD, 128))
    names[:, 0:128] = jnp.where(mask, found[0:GPAD], found[GPAD : 2 * GPAD])
    names[:, 128:256] = jnp.where(mask, found[2 * GPAD : 3 * GPAD], found[3 * GPAD :])

    def name_atoms(g, carry):
        row = names[pl.ds(g, 1), :].astype(jnp.int32)
        hot = (lax.broadcasted_iota(jnp.int32, (ATOMPAD, 256), 0) == row).astype(f32).astype(bf16)
        made = jnp.dot(dict_t[...], hot, preferred_element_type=f32).astype(bf16)
        at[0, g] = made[:HALF]
        at[1, g] = made[HALF:]
        return carry

    lax.fori_loop(0, GROUPS, name_atoms, 0, unroll=19)
    where_col = (lax.broadcasted_iota(jnp.int32, (COLS, SLOTS), 0) == cols_lane[...]).astype(f32)
    sel[...] = lax.dot_general(
        where_col.astype(bf16), pick[...], (((1,), (1,)), ((), ())), preferred_element_type=f32
    ).astype(bf16)
    where_col = (lax.broadcasted_iota(jnp.int32, (SLOTS, COLS), 1) == cols_sub[...]).astype(f32)
    sel_t[...] = jnp.dot(
        pick[...], where_col.astype(bf16), preferred_element_type=f32
    ).astype(bf16)
    contrib[...] = jnp.zeros_like(contrib)
    b_two[...] = jnp.zeros_like(b_two)

    pl.semaphore_wait(barrier, CHIPS)
    start_sig, wait_sig, sent_sig = copies(lambda p: sig_in.at[p // 2], sg_in, s_sig, r_sig)
    start_sig()

    fetch.wait()

    def spread(t, carry):
        at_lane = pl.multiple_of(t * 128, 128)
        moved = jnp.dot(pick[0 : QUAD * GPAD, :], coef[:, pl.ds(at_lane, 128)], preferred_element_type=f32)
        mask = low_lanes((GPAD, 128))
        for half in range(2):
            x = moved[2 * half * GPAD : (2 * half + 1) * GPAD]
            y = moved[(2 * half + 1) * GPAD : (2 * half + 2) * GPAD]
            lanes = slice(half * 128, half * 128 + 128)
            even = jnp.where(mask, x, pltpu.roll(y, 64, 1))
            odd = jnp.where(mask, pltpu.roll(x, 64, 1), y)
            first = pl.multiple_of(t * (2 * GPAD), 8)
            wide[half, pl.ds(first, GPAD), :] = even
            wide[half, pl.ds(first + GPAD, GPAD), :] = odd
        return carry

    lax.fori_loop(0, BV // 2, spread, 0, unroll=8)

    def bring(g, carry):
        for half in range(2):
            block = wide[half, pl.ds(g, BV, stride=GPAD), :]
            cg[g, :, half * 128 : half * 128 + 128] = block.astype(bf16)
        return carry

    lax.fori_loop(0, GROUPS, bring, 0, unroll=19)


    def gather(values, u_ref):
        first, second = split_pair(values)
        p_two[0:256, :] = first
        p_two[256:512, :] = second
        got = fold(jnp.dot(sel_t[...], p_two[...], preferred_element_type=f32))
        mask = low_lanes((GPAD, 128))
        u_ref[:, 0:128] = jnp.where(mask, got[0:GPAD], got[GPAD : 2 * GPAD])
        u_ref[:, 128:256] = jnp.where(mask, got[2 * GPAD : 3 * GPAD], got[3 * GPAD : 4 * GPAD])

    def forward(u_ref, exact):
        lanes = 128 if exact else 64

        def finish(g, acc, h, block):
            made = lax.dot_general(
                at[h, g], block, (((1,), (1,)), ((), ())), preferred_element_type=f32
            )
            acc = acc * keep[g] + made
            buf[h, g, :, 0:lanes] = acc
            return acc

        def first(g, acc):
            scaled = cg[g].astype(f32) * u_ref[pl.ds(g, 1), :]
            block = scaled.astype(bf16)
            if exact:
                low = (scaled - block.astype(f32)).astype(bf16)
                block = jnp.concatenate([block, low], axis=0)
            table[g, 0:lanes, :] = block
            return finish(g, acc, 0, block)

        def second(g, acc):
            return finish(g, acc, 1, table[g, 0:lanes, :])

        mask = low_lanes((HALF, 128))
        for h, step in ((0, first), (1, second)):
            lax.fori_loop(0, GROUPS, step, jnp.zeros((HALF, lanes), f32), unroll=76)
            for two in range(ROWS // 2):
                even = buf[h, last[2 * two]] * has[2 * two]
                odd = buf[h, last[2 * two + 1]] * has[2 * two + 1]
                if exact:
                    both = jnp.where(mask, fold(even), fold(odd))
                else:
                    both = jnp.where(mask, even, pltpu.roll(odd, 64, 1))
                part[h, 2 * two] = both[:PIECE]
                part[h, 2 * two + 1] = both[PIECE:]
            rs[h][0]()

    def summed(h):
        rs[h][1]()
        total = part[h, me_f]
        for off in range(1, NF):
            total = total + rs_in[h, lax.rem(me_f + off, NF)]
        return total

    def gather_residual(start):
        for h in range(2):
            r_all[h, me_f] = summed(h) - sig_own[h]
            pl.when(start)(ag[h][0])

    rs = half_copies(lambda h, p: part.at[h, p], rs_in, s_rs, r_rs)
    ag = half_copies(lambda h, p: r_all.at[h, me_f], r_all, s_ag, r_ag)
    start_fin, wait_fin, sent_fin = copies(lambda p: fin_out.at[p], fin_in, s_fin, r_fin)

    swap, along_y, back = [], [], []
    for h in range(2):
        landing = g_pair.at[h]
        swap.append(with_twin(g_part.at[1 - me_c, h], landing, landing, h))
        own, other = g_all.at[me_c, h], g_all.at[1 - me_c, h]
        back.append(with_twin(own, own, other, 2 + h))
        out, arrive = [], []
        for off in (2, 1, 3):
            y = lax.rem(me_y + off, SIDE)
            where = {"vox": y * 2 + me_c}
            own, other = g_in.at[h, me_y], g_in.at[h, y]
            out.append(remote(own, own, s_gr.at[h, y], r_gr.at[h, me_y], where))
            arrive.append(remote(own, other, s_gr.at[h, y], r_gr.at[h, y], where))
        along_y.append(pair(out, arrive))

    mine = me_y * NF + me_f
    out, arrive = [], []
    for off in CHIP_FAR_FIRST:
        y, f = lax.rem(me_y + off[0], SIDE), other_fas(off[1:])
        where = {"vox": y * 2 + me_c, "fas": f}
        chip = y * NF + f
        src = sc_in.at[mine, 0:1]
        out.append(remote(src, src, s_sc.at[chip], r_sc.at[mine], where))
        src = sc_in.at[chip, 0:1]
        arrive.append(remote(src, src, s_sc.at[chip], r_sc.at[chip], where))
    start_sc, wait_sc, sent_sc = pair(out, arrive)
    start_two, wait_two, sent_two = with_twin(sc_pair.at[me_c], sc_pair.at[me_c], sc_pair.at[1 - me_c], 4)

    w_out[...] = w_in[...]
    gather(w_in[...], u_w)
    forward(u_w, True)
    wait_sig()
    sg_in[me_f] = sig_in[me_f // 2]
    for f in range(NF):
        for r in range(2):
            turn[r * 64 + f * 4 : r * 64 + f * 4 + 4, :] = sg_in[f, r * 4 : r * 4 + 4, :]
    turn[...] = jnp.transpose(turn[...])
    for h in range(2):
        first_row = pl.multiple_of(h * HALF + lax.rem(me_f, 2) * PIECE, 8)
        sig_own[h] = turn[pl.ds(first_row, PIECE), :]
    gather_residual(me_f >= 0)

    def backward(h):
        for two in range(ROWS // 2):
            x = jnp.concatenate([r_all[h, 2 * two], r_all[h, 2 * two + 1]], axis=0)
            even, odd = split_pair(x)
            r_two[h, 2 * two] = even
            r_two[h, 2 * two + 1] = odd

        def step(g, c):
            block = cg[g]
            twice = jnp.concatenate([block, block], axis=0)
            inner = jnp.dot(r_two[h, grow[g]], twice, preferred_element_type=f32)
            row = jnp.sum(inner * at[h, g].astype(f32), axis=0, keepdims=True)
            contrib[pl.ds(g, 1), :] = row if h == 0 else contrib[pl.ds(g, 1), :] + row
            return c

        lax.fori_loop(0, GROUPS, step, 0, unroll=76)

    def sweep(turns, carry):
        for h in range(2):
            rs[h][2]()
        for h in range(2):
            ag[h][1]()
            backward(h)
        for half in range(2):
            first, second = split_pair(contrib[:, half * 128 : (half + 1) * 128])
            b_two[2 * half * GPAD : (2 * half + 1) * GPAD, :] = first
            b_two[(2 * half + 1) * GPAD : (2 * half + 2) * GPAD, :] = second

        def produce(core, h):
            at_row = pl.multiple_of(core * 128 + h * 64, 64)
            near = sel[pl.ds(at_row, 64), :]
            far = sel[pl.ds(at_row + 256, 64), :]
            got = jnp.concatenate([near, far], axis=0)
            got = fold(jnp.dot(got, b_two[...], preferred_element_type=f32))
            g_part[core, h] = jnp.where(low_lanes((64, 128)), got[0:64], got[64:128])

        for h in range(2):
            produce(1 - me_c, h)
            swap[h][0]()
        for h in range(2):
            produce(me_c, h)
        for h in range(2):
            ag[h][2]()
        for h in range(2):
            swap[h][1]()
            g_in[h, me_y] = g_part[me_c, h] + g_pair[h]
            along_y[h][0]()
        for h in range(2):
            along_y[h][1]()
            g_all[me_c, h] = (g_in[h, 0] + g_in[h, 1]) + (g_in[h, 2] + g_in[h, 3])
            back[h][0]()
        for h in range(2):
            back[h][1]()
        weights = w_out[...]
        gradient = g_all[...].reshape(256, 128)
        projected = jnp.where((weights > 0) | (gradient < 0), gradient, 0.0)
        gather(projected, u_p)
        forward(u_p, False)
        for stage in (swap, along_y, back):
            for h in range(2):
                stage[h][2]()
        steep = jnp.sum((projected * projected).reshape(32, 8, 128), axis=0)
        steep = jnp.sum(fold(steep), axis=0, keepdims=True)
        squares = jnp.zeros((8, 128), f32)
        for h in range(2):
            image = summed(h)
            squares = squares + jnp.sum((image * image).reshape(PIECE // 8, 8, 128), axis=0)
        squares = jnp.sum(fold(squares), axis=0, keepdims=True)
        sc_in[mine, 0:1, :] = jnp.where(low_lanes((1, 128)), squares, steep)
        start_sc()
        for h in range(2):
            rs[h][2]()
        wait_sc()
        sums = jnp.sum(sc_in[:, 0, :], axis=0, keepdims=True)
        sc_pair[me_c] = jnp.broadcast_to(sums, (8, 128))
        start_two()
        wait_two()
        both = sc_pair[0, 0:1, :] + sc_pair[1, 0:1, :]
        mask = low_lanes((1, 128))
        image_sq = jnp.sum(jnp.where(mask, both, 0.0), axis=(0, 1), keepdims=True)
        grad_sq = jnp.sum(jnp.where(mask, 0.0, both), axis=(0, 1), keepdims=True) * (1.0 / NV)
        size = grad_sq / (image_sq + 1e-06)
        w_out[...] = jnp.maximum(weights - size * projected, 0.0)
        u_w[...] = jnp.maximum(u_w[...] - size * u_p[...], 0.0)
        forward(u_w, True)
        sent_sc()
        sent_two()
        gather_residual(turns < ITERS - 1)
        return carry

    lax.fori_loop(0, ITERS, sweep, 0)
    for h in range(2):
        rs[h][2]()

    turn[0:PIECE, :] = r_all[0, me_f]
    turn[PIECE:HALF, :] = r_all[1, me_f]
    turn[HALF:, :] = jnp.zeros((128 - HALF, 128), f32)
    turn[...] = jnp.transpose(turn[...])
    for f in range(NF):
        for r in range(2):
            fin_out[f, r * 4 : r * 4 + 4, :] = turn[r * 64 + f * 4 : r * 64 + f * 4 + 4, :]
    start_fin()
    wait_fin()
    sent_fin()
    sent_sig()
    fin_in[me_f] = fin_out[me_f]
    res_out[...] = fin_in[...]


def local(
    signal,
    initial_weights,
    coefficients,
    block_rows,
    block_cols,
    block_atoms,
    block_count,
    dictionary,
):
    i32 = jnp.int32
    rows = block_rows - lax.axis_index("vox") * ROWS
    cols = block_cols - lax.axis_index("fas") * COLS
    slots = jnp.arange(SLOTS, dtype=i32)
    lives = slots < block_count[0]
    hot = (rows[:, None] == jnp.arange(ROWS, dtype=i32)[None, :]) & lives[:, None]
    before = (slots[None, :] < slots[:, None]) & lives[None, :] & (rows[None, :] == rows[:, None])
    rank = jnp.sum(before.astype(i32), axis=1)
    count = jnp.sum(hot.astype(i32), axis=0)
    groups = (count + QUAD - 1) // QUAD
    span = jnp.arange(ROWS, dtype=i32)
    ends = jnp.sum(jnp.where(span[None, :] <= span[:, None], groups[None, :], 0), axis=1)
    firsts = ends - groups
    place = jnp.where(
        lives, jnp.sum(jnp.where(hot, firsts[None, :], 0), axis=1) * QUAD + rank, -1
    )
    turns = jnp.arange(GPAD, dtype=i32)
    grow = jnp.minimum(jnp.sum((ends[None, :] <= turns[:, None]).astype(i32), axis=1), ROWS - 1)
    is_first = jnp.any((firsts[None, :] == turns[:, None]) & (groups[None, :] > 0), axis=1)
    keep = 1.0 - is_first.astype(f32)
    last = jnp.maximum(ends - 1, 0)
    has = (groups > 0).astype(f32)
    upper = (block_atoms >= 256).astype(i32)
    digits = jnp.concatenate([block_atoms - 256 * upper, upper], axis=1).astype(bf16)
    dict_t = jnp.pad(dictionary.T, ((0, 0), (0, ATOMPAD - ATOMS)))
    w_in = initial_weights.reshape(2, 256, BF)
    w_in = jnp.concatenate([w_in[0], w_in[1]], axis=1)
    sig_in = jnp.pad(signal.reshape(8, 8, DIRS), ((0, 0), (0, 0), (0, 128 - DIRS)))

    smem = pl.BlockSpec(memory_space=pltpu.SMEM)
    vmem = pl.BlockSpec(memory_space=pltpu.VMEM)
    dma = pltpu.SemaphoreType.DMA
    w_new, res = pl.pallas_call(
        kernel,
        out_shape=(
            jax.ShapeDtypeStruct((256, 128), f32),
            jax.ShapeDtypeStruct((NF, 8, 128), f32),
        ),
        in_specs=[smem] * 4 + [pl.BlockSpec(memory_space=pl.ANY)] + [vmem] * 7,
        out_specs=(vmem, vmem),
        scratch_shapes=[
            pltpu.VMEM((SLOTS, BV * BF), bf16),
            pltpu.VMEM((2, BV * GPAD, 128), f32),
            pltpu.VMEM((SPAD, SLOTS), bf16),
            pltpu.VMEM((GPAD, 256), f32),
            pltpu.VMEM((GROUPS, BV, 256), bf16),
            pltpu.VMEM((2, GROUPS, HALF, 256), bf16),
            pltpu.VMEM((COLS, SPAD), bf16),
            pltpu.VMEM((SPAD, COLS), bf16),
            pltpu.VMEM((GPAD, 256), f32),
            pltpu.VMEM((GPAD, 256), f32),
            pltpu.VMEM((GROUPS, 128, 256), bf16),
            pltpu.VMEM((2, GROUPS, HALF, 128), f32),
            pltpu.VMEM((2, NF, PIECE, 128), f32),
            pltpu.VMEM((2, NF, PIECE, 128), f32),
            pltpu.VMEM((2, NF, PIECE, 128), f32),
            pltpu.VMEM((2, ROWS, HALF, 128), bf16),
            pltpu.VMEM((GPAD, 256), f32),
            pltpu.VMEM((SPAD, 128), bf16),
            pltpu.VMEM((2, 2, 64, 128), f32),
            pltpu.VMEM((2, 64, 128), f32),
            pltpu.VMEM((2, SIDE, 64, 128), f32),
            pltpu.VMEM((2, 2, 64, 128), f32),
            pltpu.VMEM((COLS, 128), bf16),
            pltpu.VMEM((CHIPS, 8, 128), f32),
            pltpu.VMEM((2, 8, 128), f32),
            pltpu.VMEM((NF, 8, 128), f32),
            pltpu.VMEM((128, 128), f32),
            pltpu.VMEM((2, PIECE, 128), f32),
            pltpu.VMEM((NF, 8, 128), f32),
            pltpu.VMEM((NF, 8, 128), f32),
        ]
        + [
            dma(n)
            for n in ((NF,), (2, NF), (2, NF), (2, SIDE), (CHIPS,), (NF,), (5,))
            for _ in range(2)
        ]
        + [dma(())],
        compiler_params=pltpu.CompilerParams(
            collective_id=0, has_side_effects=True, vmem_limit_bytes=52 * 1024 * 1024
        ),
    )(
        grow,
        last,
        keep,
        has,
        coefficients,
        digits,
        dict_t,
        place[None, :],
        cols[None, :],
        cols[:, None],
        w_in,
        sig_in,
    )
    weights = jnp.concatenate([w_new[:, :BF], w_new[:, BF:]], axis=0).reshape(-1)
    res = res[:, :, :HALF].reshape(8, 2, 8, 2, PIECE).transpose(0, 2, 3, 1, 4)
    return (weights, res.reshape(ROWS, 4 * DIRS))


def solution(mesh):
    placed = (
        P("vox", "fas"),
        P("fas"),
        P(("vox", "fas"), None),
        P(("vox", "fas")),
        P(("vox", "fas")),
        P(("vox", "fas"), None),
        P(("vox", "fas")),
        P(),
    )
    return jax.shard_map(
        local, mesh=mesh, in_specs=placed, out_specs=(P("fas"), P("vox", "fas")), check_vma=False
    )
```

```python
import jax
import jax.numpy as jnp
from jax import lax
from jax.experimental import pallas as pl
from jax.experimental.pallas import tpu as pltpu
from jax.sharding import PartitionSpec as P

BV = 64
BF = 64
DIRS = 96
ATOMS = 360
ITERS = 5
SLOTS = 256
ROWS = 16
COLS = 512
NV = 8
NF = 16
SIDE = 4
CHIPS = 64
QUAD = 4
GROUPS = (SLOTS + (QUAD - 1) * ROWS) // QUAD
GPAD = 80
SPAD = 384
ATOMPAD = 384
HALF = DIRS // 2
PIECE = HALF // 2


def hops(off):
    return sum(min(d, SIDE - d) for d in off)


CHIP_FAR_FIRST = sorted(
    [(y, z, x) for y in range(SIDE) for z in range(SIDE) for x in range(SIDE) if y + z + x],
    key=lambda off: (-hops(off), off),
)
FAR_FIRST = [off[1:] for off in CHIP_FAR_FIRST if off[0] == 0]

f32 = jnp.float32
bf16 = jnp.bfloat16


def low_lanes(shape):
    return lax.broadcasted_iota(jnp.int32, shape, len(shape) - 1) < 64


def split_pair(x):
    h = x.astype(bf16).astype(f32)
    low = x - h
    mask = low_lanes(x.shape)
    first = jnp.where(mask, h, pltpu.roll(low, 64, 1))
    second = jnp.where(mask, pltpu.roll(h, 64, 1), low)
    return first.astype(bf16), second.astype(bf16)


def fold(x):
    return x + pltpu.roll(x, 64, 1)


def kernel(
    grow,
    last,
    keep,
    has,
    coef_hbm,
    digits,
    words,
    place_lane,
    cols_lane,
    cols_sub,
    w_in,
    sig_in,
    w_out,
    res_out,
    coef,
    wide,
    pick,
    dict_t,
    names,
    cg,
    at,
    sel,
    sel_t,
    u_p,
    u_w,
    table,
    buf,
    part,
    rs_in,
    r_all,
    r_two,
    contrib,
    b_two,
    g_part,
    g_pair,
    g_in,
    g_all,
    p_two,
    sc_in,
    sc_pair,
    sg_in,
    turn,
    sig_own,
    fin_out,
    fin_in,
    s_sig,
    r_sig,
    s_rs,
    r_rs,
    s_ag,
    r_ag,
    s_gr,
    r_gr,
    s_sc,
    r_sc,
    s_fin,
    r_fin,
    s_two,
    r_twin,
    s_coef,
):
    me_v = lax.axis_index("vox")
    me_f = lax.axis_index("fas")
    me_c = lax.rem(me_v, 2)
    me_y = me_v // 2
    twin = me_v + 1 - 2 * me_c
    fetch = pltpu.make_async_copy(coef_hbm, coef, s_coef)
    fetch.start()

    def remote(src, dst, send_sem, recv_sem, device):
        return pltpu.make_async_remote_copy(
            src_ref=src,
            dst_ref=dst,
            send_sem=send_sem,
            recv_sem=recv_sem,
            device_id=device,
            device_id_type=pl.DeviceIdType.MESH,
        )

    def pair(out, arrive):
        def start():
            for c in out:
                c.start()

        def wait():
            for c in reversed(arrive):
                c.wait_recv()

        def sent():
            for c in reversed(out):
                c.wait_send()

        return start, wait, sent

    def copies(src_at, dst, send_sem, recv_sem):
        out, arrive = [], []
        for off in FAR_FIRST:
            peer = other_fas(off)
            where = {"fas": peer}
            out.append(
                remote(src_at(peer), dst.at[me_f], send_sem.at[peer], recv_sem.at[me_f], where)
            )
            arrive.append(
                remote(src_at(peer), dst.at[peer], send_sem.at[peer], recv_sem.at[peer], where)
            )
        return pair(out, arrive)

    def half_copies(src_at, dst, send_sem, recv_sem):
        return [
            copies(lambda p: src_at(h, p), dst.at[h], send_sem.at[h], recv_sem.at[h])
            for h in range(2)
        ]

    def other_fas(off):
        return lax.rem(me_f // SIDE + off[0], SIDE) * SIDE + lax.rem(me_f + off[1], SIDE)

    def with_twin(src, dst, landing, index):
        sems, where = (s_two.at[index], r_twin.at[index]), {"vox": twin}
        return pair([remote(src, dst, *sems, where)], [remote(src, landing, *sems, where)])

    barrier = pltpu.get_barrier_semaphore()
    pl.semaphore_signal(
        barrier, inc=1, device_id={"vox": twin}, device_id_type=pl.DeviceIdType.MESH
    )
    for off in CHIP_FAR_FIRST:
        pl.semaphore_signal(
            barrier,
            inc=1,
            device_id={"vox": lax.rem(me_y + off[0], SIDE) * 2 + me_c, "fas": other_fas(off[1:])},
            device_id_type=pl.DeviceIdType.MESH,
        )

    turn_row = lax.broadcasted_iota(jnp.int32, (GPAD, SLOTS), 0) * QUAD
    for q in range(QUAD):
        hot = (place_lane[...] == turn_row + q).astype(f32).astype(bf16)
        pick[q * GPAD : (q + 1) * GPAD, :] = hot
    pick[QUAD * GPAD :, :] = jnp.zeros((SPAD - QUAD * GPAD, SLOTS), bf16)
    found = jnp.dot(pick[0 : QUAD * GPAD, :], digits[...], preferred_element_type=f32)
    found = jnp.where(low_lanes(found.shape), found, found * 256.0)
    found = fold(found)
    mask = low_lanes((GPAD, 128))
    names[:, 0:128] = jnp.where(mask, found[0:GPAD], found[GPAD : 2 * GPAD])
    names[:, 128:256] = jnp.where(mask, found[2 * GPAD : 3 * GPAD], found[3 * GPAD :])

    for k in range(ATOMPAD // 128):
        block = jnp.transpose(words[k * 128 : (k + 1) * 128, :].astype(f32))
        dict_t[:, k * 128 : (k + 1) * 128] = block[:DIRS].astype(bf16)

    def name_atoms(g, carry):
        row = names[pl.ds(g, 1), :].astype(jnp.int32)
        hot = (lax.broadcasted_iota(jnp.int32, (ATOMPAD, 256), 0) == row).astype(f32).astype(bf16)
        made = jnp.dot(dict_t[...], hot, preferred_element_type=f32).astype(bf16)
        at[0, g] = made[:HALF]
        at[1, g] = made[HALF:]
        return carry

    lax.fori_loop(0, GROUPS, name_atoms, 0, unroll=19)
    where_col = (lax.broadcasted_iota(jnp.int32, (COLS, SLOTS), 0) == cols_lane[...]).astype(f32)
    sel[...] = lax.dot_general(
        where_col.astype(bf16), pick[...], (((1,), (1,)), ((), ())), preferred_element_type=f32
    ).astype(bf16)
    where_col = (lax.broadcasted_iota(jnp.int32, (SLOTS, COLS), 1) == cols_sub[...]).astype(f32)
    sel_t[...] = jnp.dot(
        pick[...], where_col.astype(bf16), preferred_element_type=f32
    ).astype(bf16)
    contrib[...] = jnp.zeros_like(contrib)
    b_two[...] = jnp.zeros_like(b_two)

    pl.semaphore_wait(barrier, CHIPS)
    start_sig, wait_sig, sent_sig = copies(lambda p: sig_in.at[p // 2], sg_in, s_sig, r_sig)
    start_sig()

    fetch.wait()

    def spread(t, carry):
        at_lane = pl.multiple_of(t * 128, 128)
        moved = jnp.dot(pick[0 : QUAD * GPAD, :], coef[:, pl.ds(at_lane, 128)], preferred_element_type=f32)
        mask = low_lanes((GPAD, 128))
        for half in range(2):
            x = moved[2 * half * GPAD : (2 * half + 1) * GPAD]
            y = moved[(2 * half + 1) * GPAD : (2 * half + 2) * GPAD]
            lanes = slice(half * 128, half * 128 + 128)
            even = jnp.where(mask, x, pltpu.roll(y, 64, 1))
            odd = jnp.where(mask, pltpu.roll(x, 64, 1), y)
            first = pl.multiple_of(t * (2 * GPAD), 8)
            wide[half, pl.ds(first, GPAD), :] = even
            wide[half, pl.ds(first + GPAD, GPAD), :] = odd
        return carry

    lax.fori_loop(0, BV // 2, spread, 0, unroll=8)

    def bring(g, carry):
        for half in range(2):
            block = wide[half, pl.ds(g, BV, stride=GPAD), :]
            cg[g, :, half * 128 : half * 128 + 128] = block.astype(bf16)
        return carry

    lax.fori_loop(0, GROUPS, bring, 0, unroll=19)


    def gather(values, u_ref):
        first, second = split_pair(values)
        p_two[0:256, :] = first
        p_two[256:512, :] = second
        got = fold(jnp.dot(sel_t[...], p_two[...], preferred_element_type=f32))
        mask = low_lanes((GPAD, 128))
        u_ref[:, 0:128] = jnp.where(mask, got[0:GPAD], got[GPAD : 2 * GPAD])
        u_ref[:, 128:256] = jnp.where(mask, got[2 * GPAD : 3 * GPAD], got[3 * GPAD : 4 * GPAD])

    def forward(u_ref, exact):
        lanes = 128 if exact else 64

        def finish(g, acc, h, block):
            made = lax.dot_general(
                at[h, g], block, (((1,), (1,)), ((), ())), preferred_element_type=f32
            )
            acc = acc * keep[g] + made
            buf[h, g, :, 0:lanes] = acc
            return acc

        def first(g, acc):
            scaled = cg[g].astype(f32) * u_ref[pl.ds(g, 1), :]
            block = scaled.astype(bf16)
            if exact:
                low = (scaled - block.astype(f32)).astype(bf16)
                block = jnp.concatenate([block, low], axis=0)
            table[g, 0:lanes, :] = block
            return finish(g, acc, 0, block)

        def second(g, acc):
            return finish(g, acc, 1, table[g, 0:lanes, :])

        mask = low_lanes((HALF, 128))
        for h, step in ((0, first), (1, second)):
            lax.fori_loop(0, GROUPS, step, jnp.zeros((HALF, lanes), f32), unroll=76)
            for two in range(ROWS // 2):
                even = buf[h, last[2 * two]] * has[2 * two]
                odd = buf[h, last[2 * two + 1]] * has[2 * two + 1]
                if exact:
                    both = jnp.where(mask, fold(even), fold(odd))
                else:
                    both = jnp.where(mask, even, pltpu.roll(odd, 64, 1))
                part[h, 2 * two] = both[:PIECE]
                part[h, 2 * two + 1] = both[PIECE:]
            rs[h][0]()

    def summed(h):
        rs[h][1]()
        total = part[h, me_f]
        for off in range(1, NF):
            total = total + rs_in[h, lax.rem(me_f + off, NF)]
        return total

    def gather_residual(start):
        for h in range(2):
            r_all[h, me_f] = summed(h) - sig_own[h]
            pl.when(start)(ag[h][0])

    rs = half_copies(lambda h, p: part.at[h, p], rs_in, s_rs, r_rs)
    ag = half_copies(lambda h, p: r_all.at[h, me_f], r_all, s_ag, r_ag)
    start_fin, wait_fin, sent_fin = copies(lambda p: fin_out.at[p], fin_in, s_fin, r_fin)

    swap, along_y, back = [], [], []
    for h in range(2):
        landing = g_pair.at[h]
        swap.append(with_twin(g_part.at[1 - me_c, h], landing, landing, h))
        own, other = g_all.at[me_c, h], g_all.at[1 - me_c, h]
        back.append(with_twin(own, own, other, 2 + h))
        out, arrive = [], []
        for off in (2, 1, 3):
            y = lax.rem(me_y + off, SIDE)
            where = {"vox": y * 2 + me_c}
            own, other = g_in.at[h, me_y], g_in.at[h, y]
            out.append(remote(own, own, s_gr.at[h, y], r_gr.at[h, me_y], where))
            arrive.append(remote(own, other, s_gr.at[h, y], r_gr.at[h, y], where))
        along_y.append(pair(out, arrive))

    mine = me_y * NF + me_f
    out, arrive = [], []
    for off in CHIP_FAR_FIRST:
        y, f = lax.rem(me_y + off[0], SIDE), other_fas(off[1:])
        where = {"vox": y * 2 + me_c, "fas": f}
        chip = y * NF + f
        src = sc_in.at[mine, 0:1]
        out.append(remote(src, src, s_sc.at[chip], r_sc.at[mine], where))
        src = sc_in.at[chip, 0:1]
        arrive.append(remote(src, src, s_sc.at[chip], r_sc.at[chip], where))
    start_sc, wait_sc, sent_sc = pair(out, arrive)
    start_two, wait_two, sent_two = with_twin(sc_pair.at[me_c], sc_pair.at[me_c], sc_pair.at[1 - me_c], 4)

    w_out[...] = w_in[...]
    gather(w_in[...], u_w)
    forward(u_w, True)
    wait_sig()
    sg_in[me_f] = sig_in[me_f // 2]
    for f in range(NF):
        for r in range(2):
            turn[r * 64 + f * 4 : r * 64 + f * 4 + 4, :] = sg_in[f, r * 4 : r * 4 + 4, :]
    turn[...] = jnp.transpose(turn[...])
    for h in range(2):
        first_row = pl.multiple_of(h * HALF + lax.rem(me_f, 2) * PIECE, 8)
        sig_own[h] = turn[pl.ds(first_row, PIECE), :]
    gather_residual(me_f >= 0)

    def backward(h):
        for two in range(ROWS // 2):
            x = jnp.concatenate([r_all[h, 2 * two], r_all[h, 2 * two + 1]], axis=0)
            even, odd = split_pair(x)
            r_two[h, 2 * two] = even
            r_two[h, 2 * two + 1] = odd

        def step(g, c):
            block = cg[g]
            twice = jnp.concatenate([block, block], axis=0)
            inner = jnp.dot(r_two[h, grow[g]], twice, preferred_element_type=f32)
            row = jnp.sum(inner * at[h, g].astype(f32), axis=0, keepdims=True)
            contrib[pl.ds(g, 1), :] = row if h == 0 else contrib[pl.ds(g, 1), :] + row
            return c

        lax.fori_loop(0, GROUPS, step, 0, unroll=76)

    def sweep(turns, carry):
        for h in range(2):
            rs[h][2]()
        for h in range(2):
            ag[h][1]()
            backward(h)
        for half in range(2):
            first, second = split_pair(contrib[:, half * 128 : (half + 1) * 128])
            b_two[2 * half * GPAD : (2 * half + 1) * GPAD, :] = first
            b_two[(2 * half + 1) * GPAD : (2 * half + 2) * GPAD, :] = second

        def produce(core, h):
            at_row = pl.multiple_of(core * 128 + h * 64, 64)
            near = sel[pl.ds(at_row, 64), :]
            far = sel[pl.ds(at_row + 256, 64), :]
            got = jnp.concatenate([near, far], axis=0)
            got = fold(jnp.dot(got, b_two[...], preferred_element_type=f32))
            g_part[core, h] = jnp.where(low_lanes((64, 128)), got[0:64], got[64:128])

        for h in range(2):
            produce(1 - me_c, h)
            swap[h][0]()
        for h in range(2):
            produce(me_c, h)
        for h in range(2):
            ag[h][2]()
        for h in range(2):
            swap[h][1]()
            g_in[h, me_y] = g_part[me_c, h] + g_pair[h]
            along_y[h][0]()
        for h in range(2):
            along_y[h][1]()
            g_all[me_c, h] = (g_in[h, 0] + g_in[h, 1]) + (g_in[h, 2] + g_in[h, 3])
            back[h][0]()
        for h in range(2):
            back[h][1]()
        weights = w_out[...]
        gradient = g_all[...].reshape(256, 128)
        projected = jnp.where((weights > 0) | (gradient < 0), gradient, 0.0)
        gather(projected, u_p)
        forward(u_p, False)
        for stage in (swap, along_y, back):
            for h in range(2):
                stage[h][2]()
        steep = jnp.sum((projected * projected).reshape(32, 8, 128), axis=0)
        steep = jnp.sum(fold(steep), axis=0, keepdims=True)
        squares = jnp.zeros((8, 128), f32)
        for h in range(2):
            image = summed(h)
            squares = squares + jnp.sum((image * image).reshape(PIECE // 8, 8, 128), axis=0)
        squares = jnp.sum(fold(squares), axis=0, keepdims=True)
        sc_in[mine, 0:1, :] = jnp.where(low_lanes((1, 128)), squares, steep)
        start_sc()
        for h in range(2):
            rs[h][2]()
        wait_sc()
        sums = jnp.sum(sc_in[:, 0, :], axis=0, keepdims=True)
        sc_pair[me_c] = jnp.broadcast_to(sums, (8, 128))
        start_two()
        wait_two()
        both = sc_pair[0, 0:1, :] + sc_pair[1, 0:1, :]
        mask = low_lanes((1, 128))
        image_sq = jnp.sum(jnp.where(mask, both, 0.0), axis=(0, 1), keepdims=True)
        grad_sq = jnp.sum(jnp.where(mask, 0.0, both), axis=(0, 1), keepdims=True) * (1.0 / NV)
        size = grad_sq / (image_sq + 1e-06)
        w_out[...] = jnp.maximum(weights - size * projected, 0.0)
        u_w[...] = jnp.maximum(u_w[...] - size * u_p[...], 0.0)
        forward(u_w, True)
        sent_sc()
        sent_two()
        gather_residual(turns < ITERS - 1)
        return carry

    lax.fori_loop(0, ITERS, sweep, 0)
    for h in range(2):
        rs[h][2]()

    turn[0:PIECE, :] = r_all[0, me_f]
    turn[PIECE:HALF, :] = r_all[1, me_f]
    turn[HALF:, :] = jnp.zeros((128 - HALF, 128), f32)
    turn[...] = jnp.transpose(turn[...])
    for f in range(NF):
        for r in range(2):
            fin_out[f, r * 4 : r * 4 + 4, :] = turn[r * 64 + f * 4 : r * 64 + f * 4 + 4, :]
    start_fin()
    wait_fin()
    sent_fin()
    sent_sig()
    fin_in[me_f] = fin_out[me_f]
    lane = lax.broadcasted_iota(jnp.int32, (8, 128), 1)
    for two in range(ROWS // 2):
        a, b = fin_in[2 * two], fin_in[2 * two + 1]
        out = jnp.where(lane < PIECE, a, pltpu.roll(b, PIECE, 1))
        out = jnp.where(lane < 2 * PIECE, out, pltpu.roll(a, PIECE, 1))
        out = jnp.where(lane < 3 * PIECE, out, pltpu.roll(b, 2 * PIECE, 1))
        res_out[two] = out[:, :DIRS]


def local(
    signal,
    initial_weights,
    coefficients,
    block_rows,
    block_cols,
    block_atoms,
    block_count,
    dictionary,
):
    i32 = jnp.int32
    rows = block_rows & (ROWS - 1)
    cols = block_cols & (COLS - 1)
    cols = (cols & 1) * (COLS // 2) + (cols >> 1)
    slots = jnp.arange(SLOTS, dtype=i32)
    lives = slots < block_count[0]
    hot = (rows[:, None] == jnp.arange(ROWS, dtype=i32)[None, :]) & lives[:, None]
    before = (slots[None, :] < slots[:, None]) & lives[None, :] & (rows[None, :] == rows[:, None])
    rank = jnp.sum(before.astype(i32), axis=1)
    count = jnp.sum(hot.astype(i32), axis=0)
    groups = (count + QUAD - 1) // QUAD
    span = jnp.arange(ROWS, dtype=i32)
    ends = jnp.sum(jnp.where(span[None, :] <= span[:, None], groups[None, :], 0), axis=1)
    firsts = ends - groups
    place = jnp.where(
        lives, jnp.sum(jnp.where(hot, firsts[None, :], 0), axis=1) * QUAD + rank, -1
    )
    turns = jnp.arange(GPAD, dtype=i32)
    grow = jnp.minimum(jnp.sum((ends[None, :] <= turns[:, None]).astype(i32), axis=1), ROWS - 1)
    is_first = jnp.any((firsts[None, :] == turns[:, None]) & (groups[None, :] > 0), axis=1)
    keep = 1.0 - is_first.astype(f32)
    last = jnp.maximum(ends - 1, 0)
    has = (groups > 0).astype(f32)
    upper = (block_atoms >= 256).astype(i32)
    digits = jnp.concatenate([block_atoms - 256 * upper, upper], axis=1).astype(bf16)
    words = jnp.pad(dictionary, ((0, ATOMPAD - ATOMS), (0, 128 - DIRS)))
    w_in = initial_weights.reshape(COLS // 2, 2 * BF)
    sig_in = jnp.pad(signal.reshape(8, 8, DIRS), ((0, 0), (0, 0), (0, 128 - DIRS)))

    smem = pl.BlockSpec(memory_space=pltpu.SMEM)
    vmem = pl.BlockSpec(memory_space=pltpu.VMEM)
    dma = pltpu.SemaphoreType.DMA
    w_new, res = pl.pallas_call(
        kernel,
        out_shape=(
            jax.ShapeDtypeStruct((256, 128), f32),
            jax.ShapeDtypeStruct((ROWS // 2, 8, DIRS), f32),
        ),
        in_specs=[smem] * 4 + [pl.BlockSpec(memory_space=pl.ANY)] + [vmem] * 7,
        out_specs=(vmem, vmem),
        scratch_shapes=[
            pltpu.VMEM((SLOTS, BV * BF), bf16),
            pltpu.VMEM((2, BV * GPAD, 128), f32),
            pltpu.VMEM((SPAD, SLOTS), bf16),
            pltpu.VMEM((DIRS, ATOMPAD), bf16),
            pltpu.VMEM((GPAD, 256), f32),
            pltpu.VMEM((GROUPS, BV, 256), bf16),
            pltpu.VMEM((2, GROUPS, HALF, 256), bf16),
            pltpu.VMEM((COLS, SPAD), bf16),
            pltpu.VMEM((SPAD, COLS), bf16),
            pltpu.VMEM((GPAD, 256), f32),
            pltpu.VMEM((GPAD, 256), f32),
            pltpu.VMEM((GROUPS, 128, 256), bf16),
            pltpu.VMEM((2, GROUPS, HALF, 128), f32),
            pltpu.VMEM((2, NF, PIECE, 128), f32),
            pltpu.VMEM((2, NF, PIECE, 128), f32),
            pltpu.VMEM((2, NF, PIECE, 128), f32),
            pltpu.VMEM((2, ROWS, HALF, 128), bf16),
            pltpu.VMEM((GPAD, 256), f32),
            pltpu.VMEM((SPAD, 128), bf16),
            pltpu.VMEM((2, 2, 64, 128), f32),
            pltpu.VMEM((2, 64, 128), f32),
            pltpu.VMEM((2, SIDE, 64, 128), f32),
            pltpu.VMEM((2, 2, 64, 128), f32),
            pltpu.VMEM((COLS, 128), bf16),
            pltpu.VMEM((CHIPS, 8, 128), f32),
            pltpu.VMEM((2, 8, 128), f32),
            pltpu.VMEM((NF, 8, 128), f32),
            pltpu.VMEM((128, 128), f32),
            pltpu.VMEM((2, PIECE, 128), f32),
            pltpu.VMEM((NF, 8, 128), f32),
            pltpu.VMEM((NF, 8, 128), f32),
        ]
        + [
            dma(n)
            for n in ((NF,), (2, NF), (2, NF), (2, SIDE), (CHIPS,), (NF,), (5,))
            for _ in range(2)
        ]
        + [dma(())],
        compiler_params=pltpu.CompilerParams(
            collective_id=0, has_side_effects=True, vmem_limit_bytes=52 * 1024 * 1024
        ),
    )(
        grow,
        last,
        keep,
        has,
        coefficients,
        digits,
        words,
        place[None, :],
        cols[None, :],
        cols[:, None],
        w_in,
        sig_in,
    )
    return (w_new.reshape(-1), res.reshape(ROWS, 4 * DIRS))


def solution(mesh):
    placed = (
        P("vox", "fas"),
        P("fas"),
        P(("vox", "fas"), None),
        P(("vox", "fas")),
        P(("vox", "fas")),
        P(("vox", "fas"), None),
        P(("vox", "fas")),
        P(),
    )
    return jax.shard_map(
        local, mesh=mesh, in_specs=placed, out_specs=(P("fas"), P("vox", "fas")), check_vma=False
    )
```

```python
import jax
import jax.numpy as jnp
from jax import lax
from jax.experimental import pallas as pl
from jax.experimental.pallas import tpu as pltpu
from jax.sharding import PartitionSpec as P

BV = 64
BF = 64
DIRS = 96
ATOMS = 360
ITERS = 5
SLOTS = 256
ROWS = 16
COLS = 512
NV = 8
NF = 16
SIDE = 4
CHIPS = 64
QUAD = 4
GROUPS = (SLOTS + (QUAD - 1) * ROWS) // QUAD
GPAD = 80
SPAD = 384
ATOMPAD = 384
HALF = DIRS // 2
PIECE = HALF // 2


def hops(off):
    return sum(min(d, SIDE - d) for d in off)


CHIP_FAR_FIRST = sorted(
    [(y, z, x) for y in range(SIDE) for z in range(SIDE) for x in range(SIDE) if y + z + x],
    key=lambda off: (-hops(off), off),
)
FAR_FIRST = [off[1:] for off in CHIP_FAR_FIRST if off[0] == 0]

f32 = jnp.float32
bf16 = jnp.bfloat16


def low_lanes(shape):
    return lax.broadcasted_iota(jnp.int32, shape, len(shape) - 1) < 64


def split_pair(x):
    h = x.astype(bf16).astype(f32)
    low = x - h
    mask = low_lanes(x.shape)
    first = jnp.where(mask, h, pltpu.roll(low, 64, 1))
    second = jnp.where(mask, pltpu.roll(h, 64, 1), low)
    return first.astype(bf16), second.astype(bf16)


def fold(x):
    return x + pltpu.roll(x, 64, 1)


def kernel(
    grow,
    last,
    keep,
    has,
    coef_hbm,
    atoms_hbm,
    words_hbm,
    cols_hbm,
    w_hbm,
    place_lane,
    sig_in,
    w_out,
    res_out,
    coef,
    atoms,
    words,
    cols,
    w_in,
    wordpad,
    wide,
    pick,
    dict_t,
    names,
    cg,
    at,
    sel,
    sel_t,
    u_p,
    u_w,
    table,
    buf,
    part,
    rs_in,
    r_all,
    r_two,
    contrib,
    b_two,
    g_part,
    g_pair,
    g_in,
    g_all,
    p_two,
    sc_in,
    sc_pair,
    sg_in,
    turn,
    sig_own,
    fin_out,
    fin_in,
    s_sig,
    r_sig,
    s_rs,
    r_rs,
    s_ag,
    r_ag,
    s_gr,
    r_gr,
    s_sc,
    r_sc,
    s_fin,
    r_fin,
    s_two,
    r_twin,
    s_get,
):
    me_v = lax.axis_index("vox")
    me_f = lax.axis_index("fas")
    me_c = lax.rem(me_v, 2)
    me_y = me_v // 2
    twin = me_v + 1 - 2 * me_c
    fetches = [
        pltpu.make_async_copy(src, dst, s_get.at[k])
        for k, (src, dst) in enumerate(
            ((atoms_hbm, atoms), (words_hbm, words), (cols_hbm, cols), (w_hbm, w_in), (coef_hbm, coef))
        )
    ]
    for fetch in fetches:
        fetch.start()

    def remote(src, dst, send_sem, recv_sem, device):
        return pltpu.make_async_remote_copy(
            src_ref=src,
            dst_ref=dst,
            send_sem=send_sem,
            recv_sem=recv_sem,
            device_id=device,
            device_id_type=pl.DeviceIdType.MESH,
        )

    def pair(out, arrive):
        def start():
            for c in out:
                c.start()

        def wait():
            for c in reversed(arrive):
                c.wait_recv()

        def sent():
            for c in reversed(out):
                c.wait_send()

        return start, wait, sent

    def copies(src_at, dst, send_sem, recv_sem):
        out, arrive = [], []
        for off in FAR_FIRST:
            peer = other_fas(off)
            where = {"fas": peer}
            out.append(
                remote(src_at(peer), dst.at[me_f], send_sem.at[peer], recv_sem.at[me_f], where)
            )
            arrive.append(
                remote(src_at(peer), dst.at[peer], send_sem.at[peer], recv_sem.at[peer], where)
            )
        return pair(out, arrive)

    def half_copies(src_at, dst, send_sem, recv_sem):
        return [
            copies(lambda p: src_at(h, p), dst.at[h], send_sem.at[h], recv_sem.at[h])
            for h in range(2)
        ]

    def other_fas(off):
        return lax.rem(me_f // SIDE + off[0], SIDE) * SIDE + lax.rem(me_f + off[1], SIDE)

    def with_twin(src, dst, landing, index):
        sems, where = (s_two.at[index], r_twin.at[index]), {"vox": twin}
        return pair([remote(src, dst, *sems, where)], [remote(src, landing, *sems, where)])

    barrier = pltpu.get_barrier_semaphore()
    pl.semaphore_signal(
        barrier, inc=1, device_id={"vox": twin}, device_id_type=pl.DeviceIdType.MESH
    )
    for off in CHIP_FAR_FIRST:
        pl.semaphore_signal(
            barrier,
            inc=1,
            device_id={"vox": lax.rem(me_y + off[0], SIDE) * 2 + me_c, "fas": other_fas(off[1:])},
            device_id_type=pl.DeviceIdType.MESH,
        )

    turn_row = lax.broadcasted_iota(jnp.int32, (GPAD, SLOTS), 0) * QUAD
    for q in range(QUAD):
        hot = (place_lane[...] == turn_row + q).astype(f32).astype(bf16)
        pick[q * GPAD : (q + 1) * GPAD, :] = hot
    pick[QUAD * GPAD :, :] = jnp.zeros((SPAD - QUAD * GPAD, SLOTS), bf16)
    wordpad[...] = jnp.zeros_like(wordpad)
    for fetch in fetches[:4]:
        fetch.wait()
    upper = jnp.where(atoms[...] >= 256, 1, 0)
    digits = jnp.concatenate(
        [(atoms[...] - 256 * upper).astype(f32), upper.astype(f32)], axis=1
    ).astype(bf16)
    found = jnp.dot(pick[0 : QUAD * GPAD, :], digits, preferred_element_type=f32)
    wordpad[0:ATOMS, 0:DIRS] = words[...].astype(f32)
    found = jnp.where(low_lanes(found.shape), found, found * 256.0)
    found = fold(found)
    mask = low_lanes((GPAD, 128))
    names[:, 0:128] = jnp.where(mask, found[0:GPAD], found[GPAD : 2 * GPAD])
    names[:, 128:256] = jnp.where(mask, found[2 * GPAD : 3 * GPAD], found[3 * GPAD :])

    for k in range(ATOMPAD // 128):
        block = jnp.transpose(wordpad[k * 128 : (k + 1) * 128, :])
        dict_t[:, k * 128 : (k + 1) * 128] = block[:DIRS].astype(bf16)

    def name_atoms(g, carry):
        row = names[pl.ds(g, 1), :].astype(jnp.int32)
        hot = (lax.broadcasted_iota(jnp.int32, (ATOMPAD, 256), 0) == row).astype(f32).astype(bf16)
        made = jnp.dot(dict_t[...], hot, preferred_element_type=f32).astype(bf16)
        at[0, g] = made[:HALF]
        at[1, g] = made[HALF:]
        return carry

    lax.fori_loop(0, GROUPS, name_atoms, 0, unroll=19)
    col = cols[...] & (COLS - 1)
    col = (col & 1) * (COLS // 2) + lax.shift_right_logical(col, 1)
    where_col = (lax.broadcasted_iota(jnp.int32, (COLS, SLOTS), 0) == col).astype(f32).astype(bf16)
    both_lanes = (((1,), (1,)), ((), ()))
    sel[...] = lax.dot_general(
        where_col, pick[...], both_lanes, preferred_element_type=f32
    ).astype(bf16)
    sel_t[...] = lax.dot_general(
        pick[...], where_col, both_lanes, preferred_element_type=f32
    ).astype(bf16)
    contrib[...] = jnp.zeros_like(contrib)
    b_two[...] = jnp.zeros_like(b_two)

    pl.semaphore_wait(barrier, CHIPS)
    start_sig, wait_sig, sent_sig = copies(lambda p: sig_in.at[p // 2], sg_in, s_sig, r_sig)
    start_sig()

    fetches[4].wait()

    def spread(t, carry):
        at_lane = pl.multiple_of(t * 128, 128)
        moved = jnp.dot(pick[0 : QUAD * GPAD, :], coef[:, pl.ds(at_lane, 128)], preferred_element_type=f32)
        mask = low_lanes((GPAD, 128))
        for half in range(2):
            x = moved[2 * half * GPAD : (2 * half + 1) * GPAD]
            y = moved[(2 * half + 1) * GPAD : (2 * half + 2) * GPAD]
            lanes = slice(half * 128, half * 128 + 128)
            even = jnp.where(mask, x, pltpu.roll(y, 64, 1))
            odd = jnp.where(mask, pltpu.roll(x, 64, 1), y)
            first = pl.multiple_of(t * (2 * GPAD), 8)
            wide[half, pl.ds(first, GPAD), :] = even
            wide[half, pl.ds(first + GPAD, GPAD), :] = odd
        return carry

    lax.fori_loop(0, BV // 2, spread, 0, unroll=8)

    def bring(g, carry):
        for half in range(2):
            block = wide[half, pl.ds(g, BV, stride=GPAD), :]
            cg[g, :, half * 128 : half * 128 + 128] = block.astype(bf16)
        return carry

    lax.fori_loop(0, GROUPS, bring, 0, unroll=19)


    def gather(values, u_ref):
        first, second = split_pair(values)
        p_two[0:256, :] = first
        p_two[256:512, :] = second
        got = fold(jnp.dot(sel_t[...], p_two[...], preferred_element_type=f32))
        mask = low_lanes((GPAD, 128))
        u_ref[:, 0:128] = jnp.where(mask, got[0:GPAD], got[GPAD : 2 * GPAD])
        u_ref[:, 128:256] = jnp.where(mask, got[2 * GPAD : 3 * GPAD], got[3 * GPAD : 4 * GPAD])

    def forward(u_ref, exact):
        lanes = 128 if exact else 64

        def finish(g, acc, h, block):
            made = lax.dot_general(
                at[h, g], block, (((1,), (1,)), ((), ())), preferred_element_type=f32
            )
            acc = acc * keep[g] + made
            buf[h, g, :, 0:lanes] = acc
            return acc

        def first(g, acc):
            scaled = cg[g].astype(f32) * u_ref[pl.ds(g, 1), :]
            block = scaled.astype(bf16)
            if exact:
                low = (scaled - block.astype(f32)).astype(bf16)
                block = jnp.concatenate([block, low], axis=0)
            table[g, 0:lanes, :] = block
            return finish(g, acc, 0, block)

        def second(g, acc):
            return finish(g, acc, 1, table[g, 0:lanes, :])

        mask = low_lanes((HALF, 128))
        for h, step in ((0, first), (1, second)):
            lax.fori_loop(0, GROUPS, step, jnp.zeros((HALF, lanes), f32), unroll=76)
            for two in range(ROWS // 2):
                even = buf[h, last[2 * two]] * has[2 * two]
                odd = buf[h, last[2 * two + 1]] * has[2 * two + 1]
                if exact:
                    both = jnp.where(mask, fold(even), fold(odd))
                else:
                    both = jnp.where(mask, even, pltpu.roll(odd, 64, 1))
                part[h, 2 * two] = both[:PIECE]
                part[h, 2 * two + 1] = both[PIECE:]
            rs[h][0]()

    def summed(h):
        rs[h][1]()
        total = part[h, me_f]
        for off in range(1, NF):
            total = total + rs_in[h, lax.rem(me_f + off, NF)]
        return total

    def gather_residual(start):
        for h in range(2):
            r_all[h, me_f] = summed(h) - sig_own[h]
            pl.when(start)(ag[h][0])

    rs = half_copies(lambda h, p: part.at[h, p], rs_in, s_rs, r_rs)
    ag = half_copies(lambda h, p: r_all.at[h, me_f], r_all, s_ag, r_ag)
    start_fin, wait_fin, sent_fin = copies(lambda p: fin_out.at[p], fin_in, s_fin, r_fin)

    swap, along_y, back = [], [], []
    for h in range(2):
        landing = g_pair.at[h]
        swap.append(with_twin(g_part.at[1 - me_c, h], landing, landing, h))
        own, other = g_all.at[me_c, h], g_all.at[1 - me_c, h]
        back.append(with_twin(own, own, other, 2 + h))
        out, arrive = [], []
        for off in (2, 1, 3):
            y = lax.rem(me_y + off, SIDE)
            where = {"vox": y * 2 + me_c}
            own, other = g_in.at[h, me_y], g_in.at[h, y]
            out.append(remote(own, own, s_gr.at[h, y], r_gr.at[h, me_y], where))
            arrive.append(remote(own, other, s_gr.at[h, y], r_gr.at[h, y], where))
        along_y.append(pair(out, arrive))

    mine = me_y * NF + me_f
    out, arrive = [], []
    for off in CHIP_FAR_FIRST:
        y, f = lax.rem(me_y + off[0], SIDE), other_fas(off[1:])
        where = {"vox": y * 2 + me_c, "fas": f}
        chip = y * NF + f
        src = sc_in.at[mine, 0:1]
        out.append(remote(src, src, s_sc.at[chip], r_sc.at[mine], where))
        src = sc_in.at[chip, 0:1]
        arrive.append(remote(src, src, s_sc.at[chip], r_sc.at[chip], where))
    start_sc, wait_sc, sent_sc = pair(out, arrive)
    start_two, wait_two, sent_two = with_twin(sc_pair.at[me_c], sc_pair.at[me_c], sc_pair.at[1 - me_c], 4)

    w_out[...] = w_in[...]
    gather(w_in[...], u_w)
    forward(u_w, True)
    wait_sig()
    sg_in[me_f] = sig_in[me_f // 2]
    for f in range(NF):
        for r in range(2):
            turn[r * 64 + f * 4 : r * 64 + f * 4 + 4, :] = sg_in[f, r * 4 : r * 4 + 4, :]
    turn[...] = jnp.transpose(turn[...])
    for h in range(2):
        first_row = pl.multiple_of(h * HALF + lax.rem(me_f, 2) * PIECE, 8)
        sig_own[h] = turn[pl.ds(first_row, PIECE), :]
    gather_residual(me_f >= 0)

    def backward(h):
        for two in range(ROWS // 2):
            x = jnp.concatenate([r_all[h, 2 * two], r_all[h, 2 * two + 1]], axis=0)
            even, odd = split_pair(x)
            r_two[h, 2 * two] = even
            r_two[h, 2 * two + 1] = odd

        def step(g, c):
            block = cg[g]
            twice = jnp.concatenate([block, block], axis=0)
            inner = jnp.dot(r_two[h, grow[g]], twice, preferred_element_type=f32)
            row = jnp.sum(inner * at[h, g].astype(f32), axis=0, keepdims=True)
            contrib[pl.ds(g, 1), :] = row if h == 0 else contrib[pl.ds(g, 1), :] + row
            return c

        lax.fori_loop(0, GROUPS, step, 0, unroll=76)

    def sweep(turns, carry):
        for h in range(2):
            rs[h][2]()
        for h in range(2):
            ag[h][1]()
            backward(h)
        for half in range(2):
            first, second = split_pair(contrib[:, half * 128 : (half + 1) * 128])
            b_two[2 * half * GPAD : (2 * half + 1) * GPAD, :] = first
            b_two[(2 * half + 1) * GPAD : (2 * half + 2) * GPAD, :] = second

        def produce(core, h):
            at_row = pl.multiple_of(core * 128 + h * 64, 64)
            near = sel[pl.ds(at_row, 64), :]
            far = sel[pl.ds(at_row + 256, 64), :]
            got = jnp.concatenate([near, far], axis=0)
            got = fold(jnp.dot(got, b_two[...], preferred_element_type=f32))
            g_part[core, h] = jnp.where(low_lanes((64, 128)), got[0:64], got[64:128])

        for h in range(2):
            produce(1 - me_c, h)
            swap[h][0]()
        for h in range(2):
            produce(me_c, h)
        for h in range(2):
            ag[h][2]()
        for h in range(2):
            swap[h][1]()
            g_in[h, me_y] = g_part[me_c, h] + g_pair[h]
            along_y[h][0]()
        for h in range(2):
            along_y[h][1]()
            g_all[me_c, h] = (g_in[h, 0] + g_in[h, 1]) + (g_in[h, 2] + g_in[h, 3])
            back[h][0]()
        for h in range(2):
            back[h][1]()
        weights = w_out[...]
        gradient = g_all[...].reshape(256, 128)
        projected = jnp.where((weights > 0) | (gradient < 0), gradient, 0.0)
        gather(projected, u_p)
        forward(u_p, False)
        for stage in (swap, along_y, back):
            for h in range(2):
                stage[h][2]()
        steep = jnp.sum((projected * projected).reshape(32, 8, 128), axis=0)
        steep = jnp.sum(fold(steep), axis=0, keepdims=True)
        squares = jnp.zeros((8, 128), f32)
        for h in range(2):
            image = summed(h)
            squares = squares + jnp.sum((image * image).reshape(PIECE // 8, 8, 128), axis=0)
        squares = jnp.sum(fold(squares), axis=0, keepdims=True)
        sc_in[mine, 0:1, :] = jnp.where(low_lanes((1, 128)), squares, steep)
        start_sc()
        for h in range(2):
            rs[h][2]()
        wait_sc()
        sums = jnp.sum(sc_in[:, 0, :], axis=0, keepdims=True)
        sc_pair[me_c] = jnp.broadcast_to(sums, (8, 128))
        start_two()
        wait_two()
        both = sc_pair[0, 0:1, :] + sc_pair[1, 0:1, :]
        mask = low_lanes((1, 128))
        image_sq = jnp.sum(jnp.where(mask, both, 0.0), axis=(0, 1), keepdims=True)
        grad_sq = jnp.sum(jnp.where(mask, 0.0, both), axis=(0, 1), keepdims=True) * (1.0 / NV)
        size = grad_sq / (image_sq + 1e-06)
        w_out[...] = jnp.maximum(weights - size * projected, 0.0)
        u_w[...] = jnp.maximum(u_w[...] - size * u_p[...], 0.0)
        forward(u_w, True)
        sent_sc()
        sent_two()
        gather_residual(turns < ITERS - 1)
        return carry

    lax.fori_loop(0, ITERS, sweep, 0)
    for h in range(2):
        rs[h][2]()

    turn[0:PIECE, :] = r_all[0, me_f]
    turn[PIECE:HALF, :] = r_all[1, me_f]
    turn[HALF:, :] = jnp.zeros((128 - HALF, 128), f32)
    turn[...] = jnp.transpose(turn[...])
    for f in range(NF):
        for r in range(2):
            fin_out[f, r * 4 : r * 4 + 4, :] = turn[r * 64 + f * 4 : r * 64 + f * 4 + 4, :]
    start_fin()
    wait_fin()
    sent_fin()
    sent_sig()
    fin_in[me_f] = fin_out[me_f]
    lane = lax.broadcasted_iota(jnp.int32, (8, 128), 1)
    for two in range(ROWS // 2):
        a, b = fin_in[2 * two], fin_in[2 * two + 1]
        out = jnp.where(lane < PIECE, a, pltpu.roll(b, PIECE, 1))
        out = jnp.where(lane < 2 * PIECE, out, pltpu.roll(a, PIECE, 1))
        out = jnp.where(lane < 3 * PIECE, out, pltpu.roll(b, 2 * PIECE, 1))
        res_out[two] = out[:, :DIRS]


def local(
    signal,
    initial_weights,
    coefficients,
    block_rows,
    block_cols,
    block_atoms,
    block_count,
    dictionary,
):
    i32 = jnp.int32
    rows = block_rows & (ROWS - 1)
    slots = jnp.arange(SLOTS, dtype=i32)
    lives = slots < block_count[0]
    hot = (rows[:, None] == jnp.arange(ROWS, dtype=i32)[None, :]) & lives[:, None]
    before = (slots[None, :] < slots[:, None]) & lives[None, :] & (rows[None, :] == rows[:, None])
    rank = jnp.sum(before.astype(i32), axis=1)
    count = jnp.sum(hot.astype(i32), axis=0)
    groups = (count + QUAD - 1) // QUAD
    span = jnp.arange(ROWS, dtype=i32)
    ends = jnp.sum(jnp.where(span[None, :] <= span[:, None], groups[None, :], 0), axis=1)
    firsts = ends - groups
    place = jnp.where(
        lives, jnp.sum(jnp.where(hot, firsts[None, :], 0), axis=1) * QUAD + rank, -1
    )
    turns = jnp.arange(GPAD, dtype=i32)
    grow = jnp.minimum(jnp.sum((ends[None, :] <= turns[:, None]).astype(i32), axis=1), ROWS - 1)
    is_first = jnp.any((firsts[None, :] == turns[:, None]) & (groups[None, :] > 0), axis=1)
    keep = 1.0 - is_first.astype(f32)
    last = jnp.maximum(ends - 1, 0)
    has = (groups > 0).astype(f32)
    sig_in = jnp.pad(signal.reshape(8, 8, DIRS), ((0, 0), (0, 0), (0, 128 - DIRS)))

    smem = pl.BlockSpec(memory_space=pltpu.SMEM)
    vmem = pl.BlockSpec(memory_space=pltpu.VMEM)
    dma = pltpu.SemaphoreType.DMA
    w_new, res = pl.pallas_call(
        kernel,
        out_shape=(
            jax.ShapeDtypeStruct((256, 128), f32),
            jax.ShapeDtypeStruct((ROWS // 2, 8, DIRS), f32),
        ),
        in_specs=[smem] * 4 + [pl.BlockSpec(memory_space=pl.ANY)] * 5 + [vmem] * 2,
        out_specs=(vmem, vmem),
        scratch_shapes=[
            pltpu.VMEM((SLOTS, BV * BF), bf16),
            pltpu.VMEM((SLOTS, BF), jnp.int32),
            pltpu.VMEM((ATOMS, DIRS), bf16),
            pltpu.VMEM((1, SLOTS), jnp.int32),
            pltpu.VMEM((COLS // 2, 2 * BF), f32),
            pltpu.VMEM((ATOMPAD, 128), f32),
            pltpu.VMEM((2, BV * GPAD, 128), f32),
            pltpu.VMEM((SPAD, SLOTS), bf16),
            pltpu.VMEM((DIRS, ATOMPAD), bf16),
            pltpu.VMEM((GPAD, 256), f32),
            pltpu.VMEM((GROUPS, BV, 256), bf16),
            pltpu.VMEM((2, GROUPS, HALF, 256), bf16),
            pltpu.VMEM((COLS, SPAD), bf16),
            pltpu.VMEM((SPAD, COLS), bf16),
            pltpu.VMEM((GPAD, 256), f32),
            pltpu.VMEM((GPAD, 256), f32),
            pltpu.VMEM((GROUPS, 128, 256), bf16),
            pltpu.VMEM((2, GROUPS, HALF, 128), f32),
            pltpu.VMEM((2, NF, PIECE, 128), f32),
            pltpu.VMEM((2, NF, PIECE, 128), f32),
            pltpu.VMEM((2, NF, PIECE, 128), f32),
            pltpu.VMEM((2, ROWS, HALF, 128), bf16),
            pltpu.VMEM((GPAD, 256), f32),
            pltpu.VMEM((SPAD, 128), bf16),
            pltpu.VMEM((2, 2, 64, 128), f32),
            pltpu.VMEM((2, 64, 128), f32),
            pltpu.VMEM((2, SIDE, 64, 128), f32),
            pltpu.VMEM((2, 2, 64, 128), f32),
            pltpu.VMEM((COLS, 128), bf16),
            pltpu.VMEM((CHIPS, 8, 128), f32),
            pltpu.VMEM((2, 8, 128), f32),
            pltpu.VMEM((NF, 8, 128), f32),
            pltpu.VMEM((128, 128), f32),
            pltpu.VMEM((2, PIECE, 128), f32),
            pltpu.VMEM((NF, 8, 128), f32),
            pltpu.VMEM((NF, 8, 128), f32),
        ]
        + [
            dma(n)
            for n in ((NF,), (2, NF), (2, NF), (2, SIDE), (CHIPS,), (NF,), (5,))
            for _ in range(2)
        ]
        + [dma((5,))],
        compiler_params=pltpu.CompilerParams(
            collective_id=0, has_side_effects=True, vmem_limit_bytes=52 * 1024 * 1024
        ),
    )(
        grow,
        last,
        keep,
        has,
        coefficients,
        block_atoms,
        dictionary,
        block_cols[None, :],
        initial_weights.reshape(COLS // 2, 2 * BF),
        place[None, :],
        sig_in,
    )
    return (w_new.reshape(-1), res.reshape(ROWS, 4 * DIRS))


def solution(mesh):
    placed = (
        P("vox", "fas"),
        P("fas"),
        P(("vox", "fas"), None),
        P(("vox", "fas")),
        P(("vox", "fas")),
        P(("vox", "fas"), None),
        P(("vox", "fas")),
        P(),
    )
    return jax.shard_map(
        local, mesh=mesh, in_specs=placed, out_specs=(P("fas"), P("vox", "fas")), check_vma=False
    )
```

```python
import jax
import jax.numpy as jnp
from jax import lax
from jax.experimental import pallas as pl
from jax.experimental.pallas import tpu as pltpu
from jax.sharding import PartitionSpec as P

BV = 64
BF = 64
DIRS = 96
ATOMS = 360
ITERS = 5
SLOTS = 256
ROWS = 16
COLS = 512
NV = 8
NF = 16
SIDE = 4
CHIPS = 64
QUAD = 4
GROUPS = (SLOTS + (QUAD - 1) * ROWS) // QUAD
GPAD = 80
SPAD = 384
ATOMPAD = 384
HALF = DIRS // 2
PIECE = HALF // 2


def hops(off):
    return sum(min(d, SIDE - d) for d in off)


CHIP_FAR_FIRST = sorted(
    [(y, z, x) for y in range(SIDE) for z in range(SIDE) for x in range(SIDE) if y + z + x],
    key=lambda off: (-hops(off), off),
)
FAR_FIRST = [off[1:] for off in CHIP_FAR_FIRST if off[0] == 0]

f32 = jnp.float32
bf16 = jnp.bfloat16


def low_lanes(shape):
    return lax.broadcasted_iota(jnp.int32, shape, len(shape) - 1) < 64


def split_pair(x):
    h = x.astype(bf16).astype(f32)
    low = x - h
    mask = low_lanes(x.shape)
    first = jnp.where(mask, h, pltpu.roll(low, 64, 1))
    second = jnp.where(mask, pltpu.roll(h, 64, 1), low)
    return first.astype(bf16), second.astype(bf16)


def fold(x):
    return x + pltpu.roll(x, 64, 1)


def kernel(
    grow,
    last,
    keep,
    has,
    coef_hbm,
    atoms_hbm,
    words_hbm,
    cols_hbm,
    w_hbm,
    place_hbm,
    sig_hbm,
    w_out,
    res_out,
    coef,
    atoms,
    words,
    cols,
    w_in,
    place_lane,
    sig_in,
    wide,
    pick,
    dict_t,
    names,
    cg,
    at,
    sel,
    sel_t,
    u_p,
    u_w,
    table,
    buf,
    part,
    rs_in,
    r_all,
    r_two,
    contrib,
    b_two,
    g_part,
    g_pair,
    g_in,
    g_all,
    p_two,
    sc_in,
    sc_pair,
    sg_in,
    turn,
    sig_own,
    fin_out,
    fin_in,
    s_sig,
    r_sig,
    s_rs,
    r_rs,
    s_ag,
    r_ag,
    s_gr,
    r_gr,
    s_sc,
    r_sc,
    s_fin,
    r_fin,
    s_two,
    r_twin,
    s_get,
):
    me_v = lax.axis_index("vox")
    me_f = lax.axis_index("fas")
    me_c = lax.rem(me_v, 2)
    me_y = me_v // 2
    twin = me_v + 1 - 2 * me_c
    fetches = [
        pltpu.make_async_copy(src, dst, s_get.at[k])
        for k, (src, dst) in enumerate(
            (
                (place_hbm, place_lane),
                (atoms_hbm, atoms),
                (words_hbm, words),
                (cols_hbm, cols),
                (w_hbm, w_in),
                (sig_hbm, sig_in),
                (coef_hbm, coef),
            )
        )
    ]
    for fetch in fetches:
        fetch.start()

    def remote(src, dst, send_sem, recv_sem, device):
        return pltpu.make_async_remote_copy(
            src_ref=src,
            dst_ref=dst,
            send_sem=send_sem,
            recv_sem=recv_sem,
            device_id=device,
            device_id_type=pl.DeviceIdType.MESH,
        )

    def pair(out, arrive):
        def start():
            for c in out:
                c.start()

        def wait():
            for c in reversed(arrive):
                c.wait_recv()

        def sent():
            for c in reversed(out):
                c.wait_send()

        return start, wait, sent

    def copies(src_at, dst, send_sem, recv_sem):
        out, arrive = [], []
        for off in FAR_FIRST:
            peer = other_fas(off)
            where = {"fas": peer}
            out.append(
                remote(src_at(peer), dst.at[me_f], send_sem.at[peer], recv_sem.at[me_f], where)
            )
            arrive.append(
                remote(src_at(peer), dst.at[peer], send_sem.at[peer], recv_sem.at[peer], where)
            )
        return pair(out, arrive)

    def half_copies(src_at, dst, send_sem, recv_sem):
        return [
            copies(lambda p: src_at(h, p), dst.at[h], send_sem.at[h], recv_sem.at[h])
            for h in range(2)
        ]

    def other_fas(off):
        return lax.rem(me_f // SIDE + off[0], SIDE) * SIDE + lax.rem(me_f + off[1], SIDE)

    def with_twin(src, dst, landing, index):
        sems, where = (s_two.at[index], r_twin.at[index]), {"vox": twin}
        return pair([remote(src, dst, *sems, where)], [remote(src, landing, *sems, where)])

    barrier = pltpu.get_barrier_semaphore()
    pl.semaphore_signal(
        barrier, inc=1, device_id={"vox": twin}, device_id_type=pl.DeviceIdType.MESH
    )
    for off in CHIP_FAR_FIRST:
        pl.semaphore_signal(
            barrier,
            inc=1,
            device_id={"vox": lax.rem(me_y + off[0], SIDE) * 2 + me_c, "fas": other_fas(off[1:])},
            device_id_type=pl.DeviceIdType.MESH,
        )

    for fetch in fetches[:6]:
        fetch.wait()
    turn_row = lax.broadcasted_iota(jnp.int32, (GPAD, SLOTS), 0) * QUAD
    for q in range(QUAD):
        hot = (place_lane[...] == turn_row + q).astype(f32).astype(bf16)
        pick[q * GPAD : (q + 1) * GPAD, :] = hot
    pick[QUAD * GPAD :, :] = jnp.zeros((SPAD - QUAD * GPAD, SLOTS), bf16)
    upper = jnp.where(atoms[...] >= 256, 1, 0)
    digits = jnp.concatenate(
        [(atoms[...] - 256 * upper).astype(f32), upper.astype(f32)], axis=0
    ).astype(bf16)
    both_lanes = (((1,), (1,)), ((), ()))
    found = lax.dot_general(
        pick[0 : QUAD * GPAD, :], digits, both_lanes, preferred_element_type=f32
    )
    found = jnp.where(low_lanes(found.shape), found, found * 256.0)
    found = fold(found)
    mask = low_lanes((GPAD, 128))
    names[:, 0:128] = jnp.where(mask, found[0:GPAD], found[GPAD : 2 * GPAD])
    names[:, 128:256] = jnp.where(mask, found[2 * GPAD : 3 * GPAD], found[3 * GPAD :])

    dict_t[...] = jnp.zeros_like(dict_t)
    dict_t[:, 0:ATOMS] = words[...]

    def name_atoms(g, carry):
        row = names[pl.ds(g, 1), :].astype(jnp.int32)
        hot = (lax.broadcasted_iota(jnp.int32, (ATOMPAD, 256), 0) == row).astype(f32).astype(bf16)
        made = jnp.dot(dict_t[...], hot, preferred_element_type=f32).astype(bf16)
        at[0, g] = made[:HALF]
        at[1, g] = made[HALF:]
        return carry

    lax.fori_loop(0, GROUPS, name_atoms, 0, unroll=19)
    col = cols[...] & (COLS - 1)
    col = (col & 1) * (COLS // 2) + lax.shift_right_logical(col, 1)
    where_col = (lax.broadcasted_iota(jnp.int32, (COLS, SLOTS), 0) == col).astype(f32).astype(bf16)
    sel[...] = lax.dot_general(
        where_col, pick[...], both_lanes, preferred_element_type=f32
    ).astype(bf16)
    sel_t[...] = lax.dot_general(
        pick[...], where_col, both_lanes, preferred_element_type=f32
    ).astype(bf16)
    contrib[...] = jnp.zeros_like(contrib)
    b_two[...] = jnp.zeros_like(b_two)

    pl.semaphore_wait(barrier, CHIPS)
    start_sig, wait_sig, sent_sig = copies(lambda p: sig_in.at[p // 2], sg_in, s_sig, r_sig)
    start_sig()

    fetches[6].wait()

    def spread(t, carry):
        at_lane = pl.multiple_of(t * 128, 128)
        moved = jnp.dot(pick[0 : QUAD * GPAD, :], coef[:, pl.ds(at_lane, 128)], preferred_element_type=f32)
        mask = low_lanes((GPAD, 128))
        for half in range(2):
            x = moved[2 * half * GPAD : (2 * half + 1) * GPAD]
            y = moved[(2 * half + 1) * GPAD : (2 * half + 2) * GPAD]
            lanes = slice(half * 128, half * 128 + 128)
            even = jnp.where(mask, x, pltpu.roll(y, 64, 1))
            odd = jnp.where(mask, pltpu.roll(x, 64, 1), y)
            first = pl.multiple_of(t * (2 * GPAD), 8)
            wide[half, pl.ds(first, GPAD), :] = even
            wide[half, pl.ds(first + GPAD, GPAD), :] = odd
        return carry

    lax.fori_loop(0, BV // 2, spread, 0, unroll=8)

    def bring(g, carry):
        for half in range(2):
            block = wide[half, pl.ds(g, BV, stride=GPAD), :]
            cg[g, :, half * 128 : half * 128 + 128] = block.astype(bf16)
        return carry

    lax.fori_loop(0, GROUPS, bring, 0, unroll=19)


    def gather(values, u_ref):
        first, second = split_pair(values)
        p_two[0:256, :] = first
        p_two[256:512, :] = second
        got = fold(jnp.dot(sel_t[...], p_two[...], preferred_element_type=f32))
        mask = low_lanes((GPAD, 128))
        u_ref[:, 0:128] = jnp.where(mask, got[0:GPAD], got[GPAD : 2 * GPAD])
        u_ref[:, 128:256] = jnp.where(mask, got[2 * GPAD : 3 * GPAD], got[3 * GPAD : 4 * GPAD])

    def forward(u_ref, exact):
        lanes = 128 if exact else 64

        def finish(g, acc, h, block):
            made = lax.dot_general(
                at[h, g], block, (((1,), (1,)), ((), ())), preferred_element_type=f32
            )
            acc = acc * keep[g] + made
            buf[h, g, :, 0:lanes] = acc
            return acc

        def first(g, acc):
            scaled = cg[g].astype(f32) * u_ref[pl.ds(g, 1), :]
            block = scaled.astype(bf16)
            if exact:
                low = (scaled - block.astype(f32)).astype(bf16)
                block = jnp.concatenate([block, low], axis=0)
            table[g, 0:lanes, :] = block
            return finish(g, acc, 0, block)

        def second(g, acc):
            return finish(g, acc, 1, table[g, 0:lanes, :])

        mask = low_lanes((HALF, 128))
        for h, step in ((0, first), (1, second)):
            lax.fori_loop(0, GROUPS, step, jnp.zeros((HALF, lanes), f32), unroll=76)
            for two in range(ROWS // 2):
                even = buf[h, last[2 * two]] * has[2 * two]
                odd = buf[h, last[2 * two + 1]] * has[2 * two + 1]
                if exact:
                    both = jnp.where(mask, fold(even), fold(odd))
                else:
                    both = jnp.where(mask, even, pltpu.roll(odd, 64, 1))
                part[h, 2 * two] = both[:PIECE]
                part[h, 2 * two + 1] = both[PIECE:]
            rs[h][0]()

    def summed(h):
        rs[h][1]()
        total = part[h, me_f]
        for off in range(1, NF):
            total = total + rs_in[h, lax.rem(me_f + off, NF)]
        return total

    def gather_residual(start):
        for h in range(2):
            r_all[h, me_f] = summed(h) - sig_own[h]
            pl.when(start)(ag[h][0])

    rs = half_copies(lambda h, p: part.at[h, p], rs_in, s_rs, r_rs)
    ag = half_copies(lambda h, p: r_all.at[h, me_f], r_all, s_ag, r_ag)
    start_fin, wait_fin, sent_fin = copies(lambda p: fin_out.at[p], fin_in, s_fin, r_fin)

    swap, along_y, back = [], [], []
    for h in range(2):
        landing = g_pair.at[h]
        swap.append(with_twin(g_part.at[1 - me_c, h], landing, landing, h))
        own, other = g_all.at[me_c, h], g_all.at[1 - me_c, h]
        back.append(with_twin(own, own, other, 2 + h))
        out, arrive = [], []
        for off in (2, 1, 3):
            y = lax.rem(me_y + off, SIDE)
            where = {"vox": y * 2 + me_c}
            own, other = g_in.at[h, me_y], g_in.at[h, y]
            out.append(remote(own, own, s_gr.at[h, y], r_gr.at[h, me_y], where))
            arrive.append(remote(own, other, s_gr.at[h, y], r_gr.at[h, y], where))
        along_y.append(pair(out, arrive))

    mine = me_y * NF + me_f
    out, arrive = [], []
    for off in CHIP_FAR_FIRST:
        y, f = lax.rem(me_y + off[0], SIDE), other_fas(off[1:])
        where = {"vox": y * 2 + me_c, "fas": f}
        chip = y * NF + f
        src = sc_in.at[mine, 0:1]
        out.append(remote(src, src, s_sc.at[chip], r_sc.at[mine], where))
        src = sc_in.at[chip, 0:1]
        arrive.append(remote(src, src, s_sc.at[chip], r_sc.at[chip], where))
    start_sc, wait_sc, sent_sc = pair(out, arrive)
    start_two, wait_two, sent_two = with_twin(sc_pair.at[me_c], sc_pair.at[me_c], sc_pair.at[1 - me_c], 4)

    w_out[...] = w_in[...]
    gather(w_in[...], u_w)
    forward(u_w, True)
    wait_sig()
    sg_in[me_f] = sig_in[me_f // 2]
    for f in range(NF):
        for r in range(2):
            turn[r * 64 + f * 4 : r * 64 + f * 4 + 4, :] = sg_in[f, r * 4 : r * 4 + 4, :]
    turn[...] = jnp.transpose(turn[...])
    for h in range(2):
        first_row = pl.multiple_of(h * HALF + lax.rem(me_f, 2) * PIECE, 8)
        sig_own[h] = turn[pl.ds(first_row, PIECE), :]
    gather_residual(me_f >= 0)

    def backward(h):
        for two in range(ROWS // 2):
            x = jnp.concatenate([r_all[h, 2 * two], r_all[h, 2 * two + 1]], axis=0)
            even, odd = split_pair(x)
            r_two[h, 2 * two] = even
            r_two[h, 2 * two + 1] = odd

        def step(g, c):
            block = cg[g]
            twice = jnp.concatenate([block, block], axis=0)
            inner = jnp.dot(r_two[h, grow[g]], twice, preferred_element_type=f32)
            row = jnp.sum(inner * at[h, g].astype(f32), axis=0, keepdims=True)
            contrib[pl.ds(g, 1), :] = row if h == 0 else contrib[pl.ds(g, 1), :] + row
            return c

        lax.fori_loop(0, GROUPS, step, 0, unroll=76)

    def sweep(turns, carry):
        for h in range(2):
            rs[h][2]()
        for h in range(2):
            ag[h][1]()
            backward(h)
        for half in range(2):
            first, second = split_pair(contrib[:, half * 128 : (half + 1) * 128])
            b_two[2 * half * GPAD : (2 * half + 1) * GPAD, :] = first
            b_two[(2 * half + 1) * GPAD : (2 * half + 2) * GPAD, :] = second

        def produce(core, h):
            at_row = pl.multiple_of(core * 128 + h * 64, 64)
            near = sel[pl.ds(at_row, 64), :]
            far = sel[pl.ds(at_row + 256, 64), :]
            got = jnp.concatenate([near, far], axis=0)
            got = fold(jnp.dot(got, b_two[...], preferred_element_type=f32))
            g_part[core, h] = jnp.where(low_lanes((64, 128)), got[0:64], got[64:128])

        for h in range(2):
            produce(1 - me_c, h)
            swap[h][0]()
        for h in range(2):
            produce(me_c, h)
        for h in range(2):
            ag[h][2]()
        for h in range(2):
            swap[h][1]()
            g_in[h, me_y] = g_part[me_c, h] + g_pair[h]
            along_y[h][0]()
        for h in range(2):
            along_y[h][1]()
            g_all[me_c, h] = (g_in[h, 0] + g_in[h, 1]) + (g_in[h, 2] + g_in[h, 3])
            back[h][0]()
        for h in range(2):
            back[h][1]()
        weights = w_out[...]
        gradient = g_all[...].reshape(256, 128)
        projected = jnp.where((weights > 0) | (gradient < 0), gradient, 0.0)
        gather(projected, u_p)
        forward(u_p, False)
        for stage in (swap, along_y, back):
            for h in range(2):
                stage[h][2]()
        steep = jnp.sum((projected * projected).reshape(32, 8, 128), axis=0)
        steep = jnp.sum(fold(steep), axis=0, keepdims=True)
        squares = jnp.zeros((8, 128), f32)
        for h in range(2):
            image = summed(h)
            squares = squares + jnp.sum((image * image).reshape(PIECE // 8, 8, 128), axis=0)
        squares = jnp.sum(fold(squares), axis=0, keepdims=True)
        sc_in[mine, 0:1, :] = jnp.where(low_lanes((1, 128)), squares, steep)
        start_sc()
        for h in range(2):
            rs[h][2]()
        wait_sc()
        sums = jnp.sum(sc_in[:, 0, :], axis=0, keepdims=True)
        sc_pair[me_c] = jnp.broadcast_to(sums, (8, 128))
        start_two()
        wait_two()
        both = sc_pair[0, 0:1, :] + sc_pair[1, 0:1, :]
        mask = low_lanes((1, 128))
        image_sq = jnp.sum(jnp.where(mask, both, 0.0), axis=(0, 1), keepdims=True)
        grad_sq = jnp.sum(jnp.where(mask, 0.0, both), axis=(0, 1), keepdims=True) * (1.0 / NV)
        size = grad_sq / (image_sq + 1e-06)
        w_out[...] = jnp.maximum(weights - size * projected, 0.0)
        u_w[...] = jnp.maximum(u_w[...] - size * u_p[...], 0.0)
        forward(u_w, True)
        sent_sc()
        sent_two()
        gather_residual(turns < ITERS - 1)
        return carry

    lax.fori_loop(0, ITERS, sweep, 0)
    for h in range(2):
        rs[h][2]()

    turn[0:PIECE, :] = r_all[0, me_f]
    turn[PIECE:HALF, :] = r_all[1, me_f]
    turn[HALF:, :] = jnp.zeros((128 - HALF, 128), f32)
    turn[...] = jnp.transpose(turn[...])
    for f in range(NF):
        for r in range(2):
            fin_out[f, r * 4 : r * 4 + 4, :] = turn[r * 64 + f * 4 : r * 64 + f * 4 + 4, :]
    start_fin()
    wait_fin()
    sent_fin()
    sent_sig()
    fin_in[me_f] = fin_out[me_f]
    lane = lax.broadcasted_iota(jnp.int32, (8, 128), 1)
    for two in range(ROWS // 2):
        a, b = fin_in[2 * two], fin_in[2 * two + 1]
        out = jnp.where(lane < PIECE, a, pltpu.roll(b, PIECE, 1))
        out = jnp.where(lane < 2 * PIECE, out, pltpu.roll(a, PIECE, 1))
        out = jnp.where(lane < 3 * PIECE, out, pltpu.roll(b, 2 * PIECE, 1))
        res_out[two] = out[:, :DIRS]


def local(
    signal,
    initial_weights,
    coefficients,
    block_rows,
    block_cols,
    block_atoms,
    block_count,
    dictionary,
):
    i32 = jnp.int32
    rows = block_rows & (ROWS - 1)
    slots = jnp.arange(SLOTS, dtype=i32)
    lives = slots < block_count[0]
    hot = (rows[:, None] == jnp.arange(ROWS, dtype=i32)[None, :]) & lives[:, None]
    before = (slots[None, :] < slots[:, None]) & lives[None, :] & (rows[None, :] == rows[:, None])
    rank = jnp.sum(before.astype(i32), axis=1)
    count = jnp.sum(hot.astype(i32), axis=0)
    groups = (count + QUAD - 1) // QUAD
    span = jnp.arange(ROWS, dtype=i32)
    ends = jnp.sum(jnp.where(span[None, :] <= span[:, None], groups[None, :], 0), axis=1)
    firsts = ends - groups
    place = jnp.where(
        lives, jnp.sum(jnp.where(hot, firsts[None, :], 0), axis=1) * QUAD + rank, -1
    )
    turns = jnp.arange(GPAD, dtype=i32)
    grow = jnp.minimum(jnp.sum((ends[None, :] <= turns[:, None]).astype(i32), axis=1), ROWS - 1)
    is_first = jnp.any((firsts[None, :] == turns[:, None]) & (groups[None, :] > 0), axis=1)
    keep = 1.0 - is_first.astype(f32)
    last = jnp.maximum(ends - 1, 0)
    has = (groups > 0).astype(f32)
    sig_in = jnp.pad(signal.reshape(8, 8, DIRS), ((0, 0), (0, 0), (0, 128 - DIRS)))

    smem = pl.BlockSpec(memory_space=pltpu.SMEM)
    vmem = pl.BlockSpec(memory_space=pltpu.VMEM)
    dma = pltpu.SemaphoreType.DMA
    w_new, res = pl.pallas_call(
        kernel,
        out_shape=(
            jax.ShapeDtypeStruct((256, 128), f32),
            jax.ShapeDtypeStruct((ROWS // 2, 8, DIRS), f32),
        ),
        in_specs=[smem] * 4 + [pl.BlockSpec(memory_space=pl.ANY)] * 7,
        out_specs=(vmem, vmem),
        scratch_shapes=[
            pltpu.VMEM((SLOTS, BV * BF), bf16),
            pltpu.VMEM((BF, SLOTS), jnp.int32),
            pltpu.VMEM((DIRS, ATOMS), bf16),
            pltpu.VMEM((1, SLOTS), jnp.int32),
            pltpu.VMEM((COLS // 2, 2 * BF), f32),
            pltpu.VMEM((1, SLOTS), jnp.int32),
            pltpu.VMEM((NF // 2, 8, 128), f32),
            pltpu.VMEM((2, BV * GPAD, 128), f32),
            pltpu.VMEM((SPAD, SLOTS), bf16),
            pltpu.VMEM((DIRS, ATOMPAD), bf16),
            pltpu.VMEM((GPAD, 256), f32),
            pltpu.VMEM((GROUPS, BV, 256), bf16),
            pltpu.VMEM((2, GROUPS, HALF, 256), bf16),
            pltpu.VMEM((COLS, SPAD), bf16),
            pltpu.VMEM((SPAD, COLS), bf16),
            pltpu.VMEM((GPAD, 256), f32),
            pltpu.VMEM((GPAD, 256), f32),
            pltpu.VMEM((GROUPS, 128, 256), bf16),
            pltpu.VMEM((2, GROUPS, HALF, 128), f32),
            pltpu.VMEM((2, NF, PIECE, 128), f32),
            pltpu.VMEM((2, NF, PIECE, 128), f32),
            pltpu.VMEM((2, NF, PIECE, 128), f32),
            pltpu.VMEM((2, ROWS, HALF, 128), bf16),
            pltpu.VMEM((GPAD, 256), f32),
            pltpu.VMEM((SPAD, 128), bf16),
            pltpu.VMEM((2, 2, 64, 128), f32),
            pltpu.VMEM((2, 64, 128), f32),
            pltpu.VMEM((2, SIDE, 64, 128), f32),
            pltpu.VMEM((2, 2, 64, 128), f32),
            pltpu.VMEM((COLS, 128), bf16),
            pltpu.VMEM((CHIPS, 8, 128), f32),
            pltpu.VMEM((2, 8, 128), f32),
            pltpu.VMEM((NF, 8, 128), f32),
            pltpu.VMEM((128, 128), f32),
            pltpu.VMEM((2, PIECE, 128), f32),
            pltpu.VMEM((NF, 8, 128), f32),
            pltpu.VMEM((NF, 8, 128), f32),
        ]
        + [
            dma(n)
            for n in ((NF,), (2, NF), (2, NF), (2, SIDE), (CHIPS,), (NF,), (5,))
            for _ in range(2)
        ]
        + [dma((7,))],
        compiler_params=pltpu.CompilerParams(
            collective_id=0, has_side_effects=True, vmem_limit_bytes=64 * 1024 * 1024
        ),
    )(
        grow,
        last,
        keep,
        has,
        coefficients,
        block_atoms.T,
        dictionary.T,
        block_cols[None, :],
        initial_weights.reshape(COLS // 2, 2 * BF),
        place[None, :],
        sig_in,
    )
    return (w_new.reshape(-1), res.reshape(ROWS, 4 * DIRS))


def solution(mesh):
    placed = (
        P("vox", "fas"),
        P("fas"),
        P(("vox", "fas"), None),
        P(("vox", "fas")),
        P(("vox", "fas")),
        P(("vox", "fas"), None),
        P(("vox", "fas")),
        P(),
    )
    return jax.shard_map(
        local, mesh=mesh, in_specs=placed, out_specs=(P("fas"), P("vox", "fas")), check_vma=False
    )
```

```python
import jax
import jax.numpy as jnp
from jax import lax
from jax.experimental import pallas as pl
from jax.experimental.pallas import tpu as pltpu
from jax.sharding import PartitionSpec as P

BV = 64
BF = 64
DIRS = 96
ATOMS = 360
ITERS = 5
SLOTS = 256
ROWS = 16
COLS = 512
NV = 8
NF = 16
SIDE = 4
CHIPS = 64
QUAD = 4
GROUPS = (SLOTS + (QUAD - 1) * ROWS) // QUAD
GPAD = 80
SPAD = 384
ATOMPAD = 384
HALF = DIRS // 2
PIECE = HALF // 2


def hops(off):
    return sum(min(d, SIDE - d) for d in off)


CHIP_FAR_FIRST = sorted(
    [(y, z, x) for y in range(SIDE) for z in range(SIDE) for x in range(SIDE) if y + z + x],
    key=lambda off: (-hops(off), off),
)
FAR_FIRST = [off[1:] for off in CHIP_FAR_FIRST if off[0] == 0]

f32 = jnp.float32
bf16 = jnp.bfloat16


def low_lanes(shape):
    return lax.broadcasted_iota(jnp.int32, shape, len(shape) - 1) < 64


def split_pair(x):
    h = x.astype(bf16).astype(f32)
    low = x - h
    mask = low_lanes(x.shape)
    first = jnp.where(mask, h, pltpu.roll(low, 64, 1))
    second = jnp.where(mask, pltpu.roll(h, 64, 1), low)
    return first.astype(bf16), second.astype(bf16)


def fold(x):
    return x + pltpu.roll(x, 64, 1)


def kernel(
    grow,
    last,
    keep,
    has,
    coef_hbm,
    atoms_hbm,
    words_hbm,
    cols_hbm,
    w_hbm,
    place_hbm,
    sig_hbm,
    w_out,
    res_out,
    coef,
    atoms,
    words,
    cols,
    w_in,
    place_lane,
    sig_in,
    wide,
    pick,
    dict_t,
    names,
    cg,
    at,
    sel,
    sel_t,
    u_p,
    u_w,
    table,
    buf,
    part,
    rs_in,
    r_all,
    r_two,
    contrib,
    b_two,
    g_part,
    g_pair,
    g_in,
    g_all,
    p_two,
    sc_in,
    sc_pair,
    sg_in,
    turn,
    sig_own,
    fin_out,
    fin_in,
    s_sig,
    r_sig,
    s_rs,
    r_rs,
    s_ag,
    r_ag,
    s_gr,
    r_gr,
    s_sc,
    r_sc,
    s_fin,
    r_fin,
    s_two,
    r_twin,
    s_get,
):
    me_v = lax.axis_index("vox")
    me_f = lax.axis_index("fas")
    me_c = lax.rem(me_v, 2)
    me_y = me_v // 2
    twin = me_v + 1 - 2 * me_c
    fetches = [
        pltpu.make_async_copy(src, dst, s_get.at[k])
        for k, (src, dst) in enumerate(
            (
                (place_hbm, place_lane),
                (atoms_hbm, atoms),
                (words_hbm, words),
                (cols_hbm, cols),
                (w_hbm, w_in),
                (sig_hbm, sig_in),
                (coef_hbm, coef),
            )
        )
    ]
    for fetch in fetches:
        fetch.start()

    def remote(src, dst, send_sem, recv_sem, device):
        return pltpu.make_async_remote_copy(
            src_ref=src,
            dst_ref=dst,
            send_sem=send_sem,
            recv_sem=recv_sem,
            device_id=device,
            device_id_type=pl.DeviceIdType.MESH,
        )

    def pair(out, arrive):
        def start():
            for c in out:
                c.start()

        def wait():
            for c in reversed(arrive):
                c.wait_recv()

        def sent():
            for c in reversed(out):
                c.wait_send()

        return start, wait, sent

    def copies(src_at, dst, send_sem, recv_sem):
        out, arrive = [], []
        for off in FAR_FIRST:
            peer = other_fas(off)
            where = {"fas": peer}
            out.append(
                remote(src_at(peer), dst.at[me_f], send_sem.at[peer], recv_sem.at[me_f], where)
            )
            arrive.append(
                remote(src_at(peer), dst.at[peer], send_sem.at[peer], recv_sem.at[peer], where)
            )
        return pair(out, arrive)

    def half_copies(src_at, dst, send_sem, recv_sem):
        return [
            copies(lambda p: src_at(h, p), dst.at[h], send_sem.at[h], recv_sem.at[h])
            for h in range(2)
        ]

    def other_fas(off):
        return lax.rem(me_f // SIDE + off[0], SIDE) * SIDE + lax.rem(me_f + off[1], SIDE)

    def with_twin(src, dst, landing, index):
        sems, where = (s_two.at[index], r_twin.at[index]), {"vox": twin}
        return pair([remote(src, dst, *sems, where)], [remote(src, landing, *sems, where)])

    barrier = pltpu.get_barrier_semaphore()
    pl.semaphore_signal(
        barrier, inc=1, device_id={"vox": twin}, device_id_type=pl.DeviceIdType.MESH
    )
    for off in CHIP_FAR_FIRST:
        pl.semaphore_signal(
            barrier,
            inc=1,
            device_id={"vox": lax.rem(me_y + off[0], SIDE) * 2 + me_c, "fas": other_fas(off[1:])},
            device_id_type=pl.DeviceIdType.MESH,
        )

    for fetch in fetches[:6]:
        fetch.wait()
    turn_row = lax.broadcasted_iota(jnp.int32, (GPAD, SLOTS), 0) * QUAD
    for q in range(QUAD):
        hot = (place_lane[...] == turn_row + q).astype(f32).astype(bf16)
        pick[q * GPAD : (q + 1) * GPAD, :] = hot
    pick[QUAD * GPAD :, :] = jnp.zeros((SPAD - QUAD * GPAD, SLOTS), bf16)
    upper = jnp.where(atoms[...] >= 256, 1, 0)
    digits = jnp.concatenate(
        [(atoms[...] - 256 * upper).astype(f32), upper.astype(f32)], axis=0
    ).astype(bf16)
    both_lanes = (((1,), (1,)), ((), ()))
    found = lax.dot_general(
        pick[0 : QUAD * GPAD, :], digits, both_lanes, preferred_element_type=f32
    )
    found = jnp.where(low_lanes(found.shape), found, found * 256.0)
    found = fold(found)
    mask = low_lanes((GPAD, 128))
    names[:, 0:128] = jnp.where(mask, found[0:GPAD], found[GPAD : 2 * GPAD])
    names[:, 128:256] = jnp.where(mask, found[2 * GPAD : 3 * GPAD], found[3 * GPAD :])

    dict_t[...] = jnp.zeros_like(dict_t)
    dict_t[:, 0:ATOMS] = words[...]

    def name_atoms(g, carry):
        row = names[pl.ds(g, 1), :].astype(jnp.int32)
        hot = (lax.broadcasted_iota(jnp.int32, (ATOMPAD, 256), 0) == row).astype(f32).astype(bf16)
        made = jnp.dot(dict_t[...], hot, preferred_element_type=f32).astype(bf16)
        at[0, g] = made[:HALF]
        at[1, g] = made[HALF:]
        return carry

    lax.fori_loop(0, GROUPS, name_atoms, 0, unroll=19)
    col = cols[...] & (COLS - 1)
    col = (col & 1) * (COLS // 2) + lax.shift_right_logical(col, 1)
    where_col = (lax.broadcasted_iota(jnp.int32, (COLS, SLOTS), 0) == col).astype(f32).astype(bf16)
    sel[...] = lax.dot_general(
        where_col, pick[...], both_lanes, preferred_element_type=f32
    ).astype(bf16)
    sel_t[...] = lax.dot_general(
        pick[...], where_col, both_lanes, preferred_element_type=f32
    ).astype(bf16)
    contrib[...] = jnp.zeros_like(contrib)
    b_two[...] = jnp.zeros_like(b_two)

    pl.semaphore_wait(barrier, CHIPS)
    start_sig, wait_sig, sent_sig = copies(lambda p: sig_in.at[p // 2], sg_in, s_sig, r_sig)
    start_sig()

    fetches[6].wait()

    def spread(t, carry):
        at_lane = pl.multiple_of(t * 128, 128)
        moved = jnp.dot(pick[0 : QUAD * GPAD, :], coef[:, pl.ds(at_lane, 128)], preferred_element_type=f32)
        mask = low_lanes((GPAD, 128))
        for half in range(2):
            x = moved[2 * half * GPAD : (2 * half + 1) * GPAD]
            y = moved[(2 * half + 1) * GPAD : (2 * half + 2) * GPAD]
            lanes = slice(half * 128, half * 128 + 128)
            even = jnp.where(mask, x, pltpu.roll(y, 64, 1))
            odd = jnp.where(mask, pltpu.roll(x, 64, 1), y)
            first = pl.multiple_of(t * (2 * GPAD), 8)
            wide[half, pl.ds(first, GPAD), :] = even
            wide[half, pl.ds(first + GPAD, GPAD), :] = odd
        return carry

    lax.fori_loop(0, BV // 2, spread, 0, unroll=8)

    def bring(g, carry):
        for half in range(2):
            block = wide[half, pl.ds(g, BV, stride=GPAD), :]
            cg[g, :, half * 128 : half * 128 + 128] = block.astype(bf16)
        return carry

    lax.fori_loop(0, GROUPS, bring, 0, unroll=19)


    def gather(values, u_ref):
        first, second = split_pair(values)
        p_two[0:256, :] = first
        p_two[256:512, :] = second
        got = fold(jnp.dot(sel_t[...], p_two[...], preferred_element_type=f32))
        mask = low_lanes((GPAD, 128))
        u_ref[:, 0:128] = jnp.where(mask, got[0:GPAD], got[GPAD : 2 * GPAD])
        u_ref[:, 128:256] = jnp.where(mask, got[2 * GPAD : 3 * GPAD], got[3 * GPAD : 4 * GPAD])

    def forward(u_ref, exact):
        lanes = 128 if exact else 64

        def finish(g, acc, h, block):
            made = lax.dot_general(
                at[h, g], block, (((1,), (1,)), ((), ())), preferred_element_type=f32
            )
            acc = acc * keep[g] + made
            buf[h, g, :, 0:lanes] = acc
            return acc

        def first(g, acc):
            scaled = cg[g].astype(f32) * u_ref[pl.ds(g, 1), :]
            block = scaled.astype(bf16)
            if exact:
                low = (scaled - block.astype(f32)).astype(bf16)
                block = jnp.concatenate([block, low], axis=0)
            table[g, 0:lanes, :] = block
            return finish(g, acc, 0, block)

        def second(g, acc):
            return finish(g, acc, 1, table[g, 0:lanes, :])

        mask = low_lanes((HALF, 128))
        for h, step in ((0, first), (1, second)):
            lax.fori_loop(0, GROUPS, step, jnp.zeros((HALF, lanes), f32), unroll=76)
            for two in range(ROWS // 2):
                even = buf[h, last[2 * two]] * has[2 * two]
                odd = buf[h, last[2 * two + 1]] * has[2 * two + 1]
                if exact:
                    both = jnp.where(mask, fold(even), fold(odd))
                else:
                    both = jnp.where(mask, even, pltpu.roll(odd, 64, 1))
                part[h, 2 * two] = both[:PIECE]
                part[h, 2 * two + 1] = both[PIECE:]
            rs[h][0]()

    def summed(h):
        rs[h][1]()
        total = part[h, me_f]
        for off in range(1, NF):
            total = total + rs_in[h, lax.rem(me_f + off, NF)]
        return total

    def gather_residual(start):
        for h in range(2):
            r_all[h, me_f] = summed(h) - sig_own[h]
            pl.when(start)(ag[h][0])

    rs = half_copies(lambda h, p: part.at[h, p], rs_in, s_rs, r_rs)
    ag = half_copies(lambda h, p: r_all.at[h, me_f], r_all, s_ag, r_ag)
    start_fin, wait_fin, sent_fin = copies(lambda p: fin_out.at[p], fin_in, s_fin, r_fin)

    swap, along_y, back = [], [], []
    for h in range(2):
        landing = g_pair.at[h]
        swap.append(with_twin(g_part.at[1 - me_c, h], landing, landing, h))
        own, other = g_all.at[me_c, h], g_all.at[1 - me_c, h]
        back.append(with_twin(own, own, other, 2 + h))
        out, arrive = [], []
        for off in (2, 1, 3):
            y = lax.rem(me_y + off, SIDE)
            where = {"vox": y * 2 + me_c}
            own, other = g_in.at[h, me_y], g_in.at[h, y]
            out.append(remote(own, own, s_gr.at[h, y], r_gr.at[h, me_y], where))
            arrive.append(remote(own, other, s_gr.at[h, y], r_gr.at[h, y], where))
        along_y.append(pair(out, arrive))

    mine = me_y * NF + me_f
    out, arrive = [], []
    for off in CHIP_FAR_FIRST:
        y, f = lax.rem(me_y + off[0], SIDE), other_fas(off[1:])
        where = {"vox": y * 2 + me_c, "fas": f}
        chip = y * NF + f
        src = sc_in.at[mine, 0:1]
        out.append(remote(src, src, s_sc.at[chip], r_sc.at[mine], where))
        src = sc_in.at[chip, 0:1]
        arrive.append(remote(src, src, s_sc.at[chip], r_sc.at[chip], where))
    start_sc, wait_sc, sent_sc = pair(out, arrive)
    start_two, wait_two, sent_two = with_twin(sc_pair.at[me_c], sc_pair.at[me_c], sc_pair.at[1 - me_c], 4)

    w_out[...] = w_in[...]
    gather(w_in[...], u_w)
    forward(u_w, True)
    wait_sig()
    sg_in[me_f] = sig_in[me_f // 2]
    for f in range(NF):
        for r in range(2):
            turn[r * 64 + f * 4 : r * 64 + f * 4 + 4, :] = sg_in[f, r * 4 : r * 4 + 4, :]
    turn[...] = jnp.transpose(turn[...])
    for h in range(2):
        first_row = pl.multiple_of(h * HALF + lax.rem(me_f, 2) * PIECE, 8)
        sig_own[h] = turn[pl.ds(first_row, PIECE), :]
    gather_residual(me_f >= 0)

    def backward(h):
        for two in range(ROWS // 2):
            x = jnp.concatenate([r_all[h, 2 * two], r_all[h, 2 * two + 1]], axis=0)
            even, odd = split_pair(x)
            r_two[h, 2 * two] = even
            r_two[h, 2 * two + 1] = odd

        def step(g, c):
            block = cg[g]
            twice = jnp.concatenate([block, block], axis=0)
            inner = jnp.dot(r_two[h, grow[g]], twice, preferred_element_type=f32)
            row = jnp.sum(inner * at[h, g].astype(f32), axis=0, keepdims=True)
            contrib[pl.ds(g, 1), :] = row if h == 0 else contrib[pl.ds(g, 1), :] + row
            return c

        lax.fori_loop(0, GROUPS, step, 0, unroll=76)

    def sweep(turns, carry):
        for h in range(2):
            rs[h][2]()
        for h in range(2):
            ag[h][1]()
            backward(h)
        for half in range(2):
            first, second = split_pair(contrib[:, half * 128 : (half + 1) * 128])
            b_two[2 * half * GPAD : (2 * half + 1) * GPAD, :] = first
            b_two[(2 * half + 1) * GPAD : (2 * half + 2) * GPAD, :] = second

        def produce(core, h):
            at_row = pl.multiple_of(core * 128 + h * 64, 64)
            near = sel[pl.ds(at_row, 64), :]
            far = sel[pl.ds(at_row + 256, 64), :]
            got = jnp.concatenate([near, far], axis=0)
            got = fold(jnp.dot(got, b_two[...], preferred_element_type=f32))
            g_part[core, h] = jnp.where(low_lanes((64, 128)), got[0:64], got[64:128])

        for h in range(2):
            produce(1 - me_c, h)
            swap[h][0]()
        for h in range(2):
            produce(me_c, h)
        for h in range(2):
            ag[h][2]()
        for h in range(2):
            swap[h][1]()
            g_in[h, me_y] = g_part[me_c, h] + g_pair[h]
            along_y[h][0]()
        for h in range(2):
            along_y[h][1]()
            g_all[me_c, h] = (g_in[h, 0] + g_in[h, 1]) + (g_in[h, 2] + g_in[h, 3])
            back[h][0]()
        for h in range(2):
            back[h][1]()
        weights = w_out[...]
        gradient = g_all[...].reshape(256, 128)
        projected = jnp.where((weights > 0) | (gradient < 0), gradient, 0.0)
        gather(projected, u_p)
        forward(u_p, False)
        for stage in (swap, along_y, back):
            for h in range(2):
                stage[h][2]()
        steep = jnp.sum((projected * projected).reshape(32, 8, 128), axis=0)
        steep = jnp.sum(fold(steep), axis=0, keepdims=True)
        squares = jnp.zeros((8, 128), f32)
        for h in range(2):
            image = summed(h)
            squares = squares + jnp.sum((image * image).reshape(PIECE // 8, 8, 128), axis=0)
        squares = jnp.sum(fold(squares), axis=0, keepdims=True)
        sc_in[mine, 0:1, :] = jnp.where(low_lanes((1, 128)), squares, steep)
        start_sc()
        for h in range(2):
            rs[h][2]()
        wait_sc()
        sums = jnp.sum(sc_in[:, 0, :], axis=0, keepdims=True)
        sc_pair[me_c] = jnp.broadcast_to(sums, (8, 128))
        start_two()
        wait_two()
        both = sc_pair[0, 0:1, :] + sc_pair[1, 0:1, :]
        mask = low_lanes((1, 128))
        image_sq = jnp.sum(jnp.where(mask, both, 0.0), axis=(0, 1), keepdims=True)
        grad_sq = jnp.sum(jnp.where(mask, 0.0, both), axis=(0, 1), keepdims=True) * (1.0 / NV)
        size = grad_sq / (image_sq + 1e-06)
        w_out[...] = jnp.maximum(weights - size * projected, 0.0)
        u_w[...] = jnp.maximum(u_w[...] - size * u_p[...], 0.0)
        forward(u_w, True)
        sent_sc()
        sent_two()
        gather_residual(turns < ITERS - 1)
        return carry

    lax.fori_loop(0, ITERS, sweep, 0)
    for h in range(2):
        rs[h][2]()

    turn[0:PIECE, :] = r_all[0, me_f]
    turn[PIECE:HALF, :] = r_all[1, me_f]
    turn[HALF:, :] = jnp.zeros((128 - HALF, 128), f32)
    turn[...] = jnp.transpose(turn[...])
    for f in range(NF):
        for r in range(2):
            fin_out[f, r * 4 : r * 4 + 4, :] = turn[r * 64 + f * 4 : r * 64 + f * 4 + 4, :]
    start_fin()
    wait_fin()
    sent_fin()
    sent_sig()
    fin_in[me_f] = fin_out[me_f]
    lane = lax.broadcasted_iota(jnp.int32, (8, 128), 1)
    for two in range(ROWS // 2):
        a, b = fin_in[2 * two], fin_in[2 * two + 1]
        out = jnp.where(lane < PIECE, a, pltpu.roll(b, PIECE, 1))
        out = jnp.where(lane < 2 * PIECE, out, pltpu.roll(a, PIECE, 1))
        out = jnp.where(lane < 3 * PIECE, out, pltpu.roll(b, 2 * PIECE, 1))
        res_out[two] = out[:, :DIRS]


def local(
    signal,
    initial_weights,
    coefficients,
    block_rows,
    block_cols,
    block_atoms,
    block_count,
    dictionary,
):
    i32 = jnp.int32
    rows = block_rows & (ROWS - 1)
    slots = jnp.arange(SLOTS, dtype=i32)
    lives = slots < block_count[0]
    hot = (rows[:, None] == jnp.arange(ROWS, dtype=i32)[None, :]) & lives[:, None]
    before = (slots[None, :] < slots[:, None]) & lives[None, :] & (rows[None, :] == rows[:, None])
    rank = jnp.sum(before.astype(i32), axis=1)
    count = jnp.sum(hot.astype(i32), axis=0)
    groups = (count + QUAD - 1) // QUAD
    span = jnp.arange(ROWS, dtype=i32)
    ends = jnp.sum(jnp.where(span[None, :] <= span[:, None], groups[None, :], 0), axis=1)
    firsts = ends - groups
    place = jnp.where(
        lives, jnp.sum(jnp.where(hot, firsts[None, :], 0), axis=1) * QUAD + rank, -1
    )
    turns = jnp.arange(GPAD, dtype=i32)
    grow = jnp.minimum(jnp.sum((ends[None, :] <= turns[:, None]).astype(i32), axis=1), ROWS - 1)
    is_first = jnp.any((firsts[None, :] == turns[:, None]) & (groups[None, :] > 0), axis=1)
    keep = 1.0 - is_first.astype(f32)
    last = jnp.maximum(ends - 1, 0)
    has = (groups > 0).astype(f32)
    sig_in = jnp.pad(signal.reshape(8, 8, DIRS), ((0, 0), (0, 0), (0, 128 - DIRS)))

    smem = pl.BlockSpec(memory_space=pltpu.SMEM)
    vmem = pl.BlockSpec(memory_space=pltpu.VMEM)
    dma = pltpu.SemaphoreType.DMA
    w_new, res = pl.pallas_call(
        kernel,
        out_shape=(
            jax.ShapeDtypeStruct((256, 128), f32),
            jax.ShapeDtypeStruct((ROWS // 2, 8, DIRS), f32),
        ),
        in_specs=[smem] * 4 + [pl.BlockSpec(memory_space=pl.ANY)] * 7,
        out_specs=(vmem, vmem),
        scratch_shapes=[
            pltpu.VMEM((SLOTS, BV * BF), bf16),
            pltpu.VMEM((BF, SLOTS), jnp.int32),
            pltpu.VMEM((DIRS, ATOMS), bf16),
            pltpu.VMEM((1, SLOTS), jnp.int32),
            pltpu.VMEM((COLS // 2, 2 * BF), f32),
            pltpu.VMEM((1, SLOTS), jnp.int32),
            pltpu.VMEM((NF // 2, 8, 128), f32),
            pltpu.VMEM((2, BV * GPAD, 128), f32),
            pltpu.VMEM((SPAD, SLOTS), bf16),
            pltpu.VMEM((DIRS, ATOMPAD), bf16),
            pltpu.VMEM((GPAD, 256), f32),
            pltpu.VMEM((GROUPS, BV, 256), bf16),
            pltpu.VMEM((2, GROUPS, HALF, 256), bf16),
            pltpu.VMEM((COLS, SPAD), bf16),
            pltpu.VMEM((SPAD, COLS), bf16),
            pltpu.VMEM((GPAD, 256), f32),
            pltpu.VMEM((GPAD, 256), f32),
            pltpu.VMEM((GROUPS, 128, 256), bf16),
            pltpu.VMEM((2, GROUPS, HALF, 128), f32),
            pltpu.VMEM((2, NF, PIECE, 128), f32),
            pltpu.VMEM((2, NF, PIECE, 128), f32),
            pltpu.VMEM((2, NF, PIECE, 128), f32),
            pltpu.VMEM((2, ROWS, HALF, 128), bf16),
            pltpu.VMEM((GPAD, 256), f32),
            pltpu.VMEM((SPAD, 128), bf16),
            pltpu.VMEM((2, 2, 64, 128), f32),
            pltpu.VMEM((2, 64, 128), f32),
            pltpu.VMEM((2, SIDE, 64, 128), f32),
            pltpu.VMEM((2, 2, 64, 128), f32),
            pltpu.VMEM((COLS, 128), bf16),
            pltpu.VMEM((CHIPS, 8, 128), f32),
            pltpu.VMEM((2, 8, 128), f32),
            pltpu.VMEM((NF, 8, 128), f32),
            pltpu.VMEM((128, 128), f32),
            pltpu.VMEM((2, PIECE, 128), f32),
            pltpu.VMEM((NF, 8, 128), f32),
            pltpu.VMEM((NF, 8, 128), f32),
        ]
        + [
            dma(n)
            for n in ((NF,), (2, NF), (2, NF), (2, SIDE), (CHIPS,), (NF,), (5,))
            for _ in range(2)
        ]
        + [dma((7,))],
        compiler_params=pltpu.CompilerParams(
            collective_id=0, has_side_effects=True, vmem_limit_bytes=52 * 1024 * 1024
        ),
    )(
        grow,
        last,
        keep,
        has,
        coefficients,
        block_atoms.T,
        dictionary.T,
        block_cols[None, :],
        initial_weights.reshape(COLS // 2, 2 * BF),
        place[None, :],
        sig_in,
    )
    return (w_new.reshape(-1), res.reshape(ROWS, 4 * DIRS))


def solution(mesh):
    placed = (
        P("vox", "fas"),
        P("fas"),
        P(("vox", "fas"), None),
        P(("vox", "fas")),
        P(("vox", "fas")),
        P(("vox", "fas"), None),
        P(("vox", "fas")),
        P(),
    )
    return jax.shard_map(
        local, mesh=mesh, in_specs=placed, out_specs=(P("fas"), P("vox", "fas")), check_vma=False
    )
```
